128 devices in a mesh: query: 4 (over x_hi, core), corpus: 32 (over y, x_lo, z).
Axes of the slice: x: 4 (x_hi: 2, x_lo: 2; x = x_hi * 2 + x_lo), y: 4, z: 4, core: 2. Of those that a mesh axis runs over, the one named last changes fastest.
Arguments:
- passages: bfloat16 [4096, 768], P('corpus'), may hold values from -64 to 64
- queries: bfloat16 [8192, 768], P(('query', 'corpus')), may hold values from -64 to 64
- codebook: float32 [96, 8, 256], replicated, may hold values from -6 to 6
Outputs:
- divergence: float32 [8192], P('query')
- codebook_grad: float32 [96, 8, 256], replicated
The draws below stay inside these ranges and needn't reach their ends.
All inputs are finite; a program needn't handle non-finite values.
Results may differ from the reference program's by a relative error of at most 0.0053.
Values may be sent and summed in bfloat16 or wider, within the bound.
A program may use at most 64 MiB of HBM per device.

```python
import math
import jax
import jax.numpy as jnp
from jax import lax

D = 768
SUBSPACES = 96
CODEWORDS = 256
SUB_WIDTH = 8
QB_DEV = 64
PASSAGES = 4096
QUERIES = 8192
N_QUERY = 4
N_CORPUS = 32


def passage_rows(key):
    normal_rows = jax.random.normal(jax.random.fold_in(key, 11), (PASSAGES, D), jnp.float32)
    return normal_rows


def draw_passages(key, part):
    return passage_rows(key).astype(jnp.bfloat16)


def draw_queries(key, part):
    query_rows = jax.random.normal(jax.random.fold_in(key, 21), (QUERIES, D), jnp.float32)
    return query_rows.astype(jnp.bfloat16)


def bell_draw(own_key, shape, deviation, most, held_as=jnp.bfloat16):
    return jnp.clip(deviation * jax.random.normal(own_key, shape, jnp.float32), -most, most).astype(held_as)


def setup_inputs(seed: int = 0) -> dict:
    splits = jax.random.split(jax.random.key(seed), 4)
    return {
        "passages": draw_passages(jax.random.fold_in(splits[3], 71), 0),
        "queries": draw_queries(jax.random.fold_in(splits[3], 71), 0),
        "codebook": bell_draw(splits[2], (SUBSPACES, SUB_WIDTH, CODEWORDS), 1.0, 6.0, jnp.float32),
    }


ASSIGN_TEMP = 2.0
HIGHEST = lax.Precision.HIGHEST

def soft_assign(row_block, codebook):
    row_count = row_block.shape[0]
    subspaces, sub_width, codewords = codebook.shape
    pieces = row_block.astype(jnp.float32).reshape(row_count, subspaces, sub_width)
    cross_term = jnp.einsum('rms,msk->rmk', pieces, codebook, precision=HIGHEST)
    distance = lax.optimization_barrier(jnp.sum(pieces * pieces, axis=-1))[:, :, None] - 2.0 * cross_term + lax.optimization_barrier(jnp.sum(codebook * codebook, axis=1))[None]
    weights = jax.nn.softmax(-distance / ASSIGN_TEMP, axis=-1)
    rebuilt = jnp.einsum('rmk,msk->rms', weights, codebook, precision=HIGHEST)
    return rebuilt.reshape(row_count, subspaces * sub_width)

def assign_grad(row_block, codebook, cotangent):
    _, pullback = jax.vjp(lambda book_value: soft_assign(row_block, book_value), codebook)
    return pullback(cotangent)[0]

def reference(passages, queries, codebook):
    total_rows = passages.shape[0]
    block_rows = math.gcd(total_rows, 256)
    blocked = passages.reshape(total_rows // block_rows, block_rows, D)
    rebuilt = lax.map(lambda row_block: soft_assign(row_block, codebook), blocked)
    rebuilt = rebuilt.reshape(total_rows, D).astype(jnp.bfloat16)
    score_scale = float(D) ** (-0.5)
    kl_weight = PASSAGES / 64.0
    grouped = queries.reshape(N_QUERY, QB_DEV * N_CORPUS, D)
    dims_rows = (((1,), (1,)), ((), ()))
    dims_first = (((0,), (0,)), ((), ()))

    def per_group(running, gathered):
        teacher = lax.dot_general(gathered, passages, dims_rows, preferred_element_type=jnp.float32) * score_scale
        student = lax.dot_general(gathered, rebuilt, dims_rows, preferred_element_type=jnp.float32) * score_scale
        log_teacher = jax.nn.log_softmax(teacher, axis=-1)
        log_student = jax.nn.log_softmax(student, axis=-1)
        prob_teacher = jnp.exp(log_teacher)
        prob_student = jnp.exp(log_student)
        divergence = lax.optimization_barrier(jnp.sum(prob_teacher * (log_teacher - log_student), axis=-1))
        grad_scores = ((prob_student - prob_teacher) * (kl_weight * score_scale)).astype(jnp.bfloat16)
        grad_rebuilt = lax.dot_general(grad_scores, gathered, dims_first, preferred_element_type=jnp.float32)
        return (running + grad_rebuilt, divergence)
    grad_rebuilt, divergence = lax.scan(per_group, jnp.zeros((total_rows, D), jnp.float32), grouped)
    grad_blocks = grad_rebuilt.reshape(total_rows // block_rows, block_rows, D)

    def add_block(running, block_pair):
        return (running + assign_grad(block_pair[0], codebook, block_pair[1]), None)
    codebook_grad, _ = lax.scan(add_block, jnp.zeros_like(codebook), (blocked, grad_blocks))
    return (divergence.reshape(QUERIES), codebook_grad)
```

```python
import functools

import jax
import jax.numpy as jnp
from jax import lax
from jax.experimental import pallas as pl
from jax.experimental.pallas import tpu as pltpu
from jax.sharding import PartitionSpec as P

MESH = pl.DeviceIdType.MESH
F32 = jnp.float32
BF16 = jnp.bfloat16
NT = (((1,), (1,)), ((), ()))
NN = (((1,), (0,)), ((), ()))

D = 768
SUB = 8
CODES = 256
QB = 64
PB = 128
PLANE = 16
TILE = 128
GROUPS = 16
ROWS = 256
QN = 1024
N_SEM = 136


def split3(value):
    high = value.astype(BF16)
    rest = value - high.astype(F32)
    mid = rest.astype(BF16)
    low = (rest - mid.astype(F32)).astype(BF16)
    return high, mid, low


def split2(value):
    high = value.astype(BF16)
    low = (value - high.astype(F32)).astype(BF16)
    return high, low


def dot(a, b, dims):
    return lax.dot_general(a, b, dims, preferred_element_type=F32)


def kernel(
    p_ref, q_ref, cb_ref,
    out_ref, div_ref,
    qbuf, pbuf, rbuf,
    lhs_f, lhs_b, cp3, ct, rt, a1b, a2b,
    tbuf, ebt, ebs, mloc, stat,
    gown, gsib, gsrc, rs1, rs1s, rs2, rs2s,
    acc, dcs, dcr, piece, dbuf, divb,
    send_sem, recv_sem,
):
    qi = lax.axis_index("query")
    ci = lax.axis_index("corpus")
    xh, core = qi // 2, qi % 2
    y, xl, z = ci // 8, (ci // 4) % 2, ci % 4
    x = xh * 2 + xl
    u = (x + 4 - 2 * core) % 4

    def dev(x_, y_, z_, core_):
        return ((x_ // 2) * 2 + core_, y_ * 8 + (x_ % 2) * 4 + z_)

    def dev_x(step, core_=None):
        return dev((x + step) % 4, y, z, core if core_ is None else core_)

    def dev_yz(dy, dz):
        return dev(x, (y + dy) % 4, (z + dz) % 4, core)

    sibling = dev(x, y, z, 1 - core)
    left, right = dev_x(3), dev_x(1)

    sends = []
    count = [0]

    def push(src, dst, index, device):
        copy = pltpu.make_async_remote_copy(
            src_ref=src, dst_ref=dst, send_sem=send_sem.at[len(sends)],
            recv_sem=recv_sem.at[index], device_id=device, device_id_type=MESH,
        )
        copy.start()
        sends.append(copy)

    def arrive(dst, index):
        pltpu.make_async_remote_copy(
            src_ref=dst, dst_ref=dst, send_sem=send_sem.at[0],
            recv_sem=recv_sem.at[index], device_id=sibling, device_id_type=MESH,
        ).wait_recv()

    def block(n):
        first = count[0]
        count[0] += n
        return first

    barrier = pltpu.get_barrier_semaphore()
    peers = [dev_x(s, c) for s in range(4) for c in (core, 1 - core)][1:]
    peers += [dev_yz(a, b) for a in range(4) for b in range(4)][1:]
    for peer in peers:
        pl.semaphore_signal(barrier, inc=1, device_id=peer, device_id_type=MESH)

    me = y * 4 + z
    qbuf[me] = q_ref[...]
    pbuf[xl] = p_ref[...]

    pl.semaphore_wait(barrier, len(peers))

    def gather_plane(own, piece_of, base):
        def rel(h, a, b):
            return (a, b) if h == 0 else (b, a)

        def slot(dy, dz):
            return ((y + dy) % 4) * 4 + (z + dz) % 4

        def sem(dy, dz, h, part):
            return base + (((dy % 4) * 4 + dz % 4) * 2 + h) * 2 + (part or 0)

        def send(h, a, b, part, first_axis, step):
            dy, dz = rel(h, a, b)
            sy, sz = rel(h, step, 0) if first_axis else rel(h, 0, step)
            dst = piece_of(slot(dy, dz), h, part)
            src = own(h) if (a, b) == (0, 0) else dst
            push(src, dst, sem(dy - sy, dz - sz, h, part), dev_yz(sy % 4, sz % 4))

        def wait(h, a, b, part):
            dy, dz = rel(h, a, b)
            arrive(piece_of(slot(dy, dz), h, part), sem(dy, dz, h, part))

        def wave0():
            for first in (True, False):
                for h in range(2):
                    for step in (1, 3):
                        send(h, 0, 0, None, first, step)

        def wave1():
            for h in range(2):
                for a, part, step in ((3, 0, 1), (1, 1, 3)):
                    wait(h, a, 0, None)
                    send(h, a, 0, part, True, step)
                    send(h, a, 0, None, False, 1)
                    send(h, a, 0, None, False, 3)
            for h in range(2):
                for b, part, step in ((3, 0, 1), (1, 1, 3)):
                    wait(h, 0, b, None)
                    send(h, 0, b, part, False, step)

        def wave2():
            for h in range(2):
                wait(h, 2, 0, 0)
                wait(h, 2, 0, 1)
                send(h, 2, 0, None, False, 1)
                send(h, 2, 0, None, False, 3)
            for h in range(2):
                for a in (3, 1):
                    for b, part, step in ((3, 0, 1), (1, 1, 3)):
                        wait(h, a, b, None)
                        send(h, a, b, part, False, step)

        def wave3():
            for h in range(2):
                for b, part, step in ((3, 0, 1), (1, 1, 3)):
                    wait(h, 2, b, None)
                    send(h, 2, b, part, False, step)

        def wave4():
            for h in range(2):
                for a in (0, 1, 3, 2):
                    wait(h, a, 2, 0)
                    wait(h, a, 2, 1)

        return wave0, wave1, wave2, wave3, wave4

    def q_piece(s, h, part):
        if part is None:
            return qbuf.at[s, pl.ds(32 * h, 32), :]
        return qbuf.at[s, pl.ds(32 * h + 16 * part, 16), :]

    qw = gather_plane(lambda h: q_ref.at[pl.ds(32 * h, 32), :], q_piece, block(64))
    s_p = block(1)
    x_to = (x + 3 + 2 * core) % 4
    push(p_ref, pbuf.at[xl], s_p, dev(x_to, y, z, core))
    qw[0]()

    tile = 3 * core + jnp.minimum(u, 2)
    col = pl.multiple_of(tile * TILE, TILE)
    cb = cb_ref[pl.ds(col, TILE), :]
    grouped = cb.reshape(GROUPS, SUB, CODES)
    bias = -0.5 * jnp.sum(grouped * grouped, axis=1)
    c_parts = split3(cb)
    c32 = [c.astype(F32).reshape(GROUPS, SUB, CODES) for c in c_parts]
    cp3[...] = jnp.concatenate(c32 + [jnp.zeros((GROUPS, SUB, CODES), F32)], axis=1).astype(BF16)
    cbt = cb.T
    ct[...] = cbt
    t1, t2, t3 = split3(cbt)

    def stack_rows(parts, width):
        rows = [p.astype(F32) for p in parts]
        rows.append(jnp.zeros((TILE - len(parts) * GROUPS, width), F32))
        return jnp.concatenate(rows, axis=0).T.astype(BF16)

    lane = lax.broadcasted_iota(jnp.int32, (1, 4 * TILE), 1)
    in_tile = lane % TILE
    group_id = jnp.where(
        lane < 3 * TILE, in_tile // SUB, jnp.where(in_tile < 3 * GROUPS, in_tile % GROUPS, -1)
    )
    ones48 = jnp.where(
        lax.broadcasted_iota(jnp.int32, (CODES, TILE), 1) < 3 * GROUPS, 1.0, 0.0
    ).astype(BF16)
    lhs_f[...] = jnp.concatenate([t1, t2, t3, stack_rows(split3(bias), CODES)], axis=1)
    lhs_b[...] = jnp.concatenate([t1, t1, t2, ones48], axis=1)

    qw[1]()
    arrive(pbuf.at[1 - xl], s_p)

    xt = jnp.concatenate([pbuf[0, :, pl.ds(col, TILE)], pbuf[1, :, pl.ds(col, TILE)]], axis=0)
    rhs_f = jnp.concatenate([xt, xt, xt, ones48], axis=1)

    def group_mask(i):
        return jnp.where(group_id == i, 1.0, 0.0).astype(BF16)

    def assign_step(i, carry):
        logits = dot(lhs_f[...] * group_mask(i), rhs_f, NT)
        top = jnp.max(logits, axis=0, keepdims=True)
        e = jnp.exp(logits - top)
        w = e * (1.0 / jnp.sum(e, axis=0, keepdims=True))
        w1, w2 = split2(w)
        a1b[i] = w1
        a2b[i] = w2
        got = dot(cp3[i], w1, NN) + dot(cp3[i], w2, NN)
        rt[i] = got[0:8] + got[8:16] + got[16:24]
        return carry

    lax.fori_loop(0, 8, assign_step, 0)
    qw[2]()
    lax.fori_loop(8, 16, assign_step, 0)

    mine = core * 4 + u
    rbuf[mine] = rt[...].reshape(TILE, ROWS).T.astype(BF16)

    def r_slot(step):
        return core * 4 + (u + step) % 4

    def r_sib(step):
        return (1 - core) * 4 + (u + 2 + step) % 4

    def r_half(s, part):
        return rbuf.at[s, pl.ds(128 * part, 128), :]

    s_r = block(4)
    s_rs = block(5)
    push(rbuf.at[mine], rbuf.at[mine], s_r + 0, right)
    push(rbuf.at[mine], rbuf.at[mine], s_r + 1, left)
    push(rbuf.at[mine], rbuf.at[mine], s_rs + 0, sibling)
    qw[3]()
    for step, sem_i, part, far in ((3, 0, 0, right), (1, 1, 1, left)):
        s = r_slot(step)
        arrive(rbuf.at[s], s_r + sem_i)
        push(r_half(s, part), r_half(s, part), s_r + 2 + part, far)
        push(rbuf.at[s], rbuf.at[s], s_rs + 1 + sem_i, sibling)
    qw[4]()

    p_all = pbuf[...].reshape(ROWS, D)
    scale = float(D) ** (-0.5)
    for n in range(4):
        qc = qbuf[4 * n:4 * n + 4].reshape(256, D)
        t = dot(p_all, qc, NT) * scale
        m_t = jnp.max(t, axis=0, keepdims=True)
        tbuf[n] = t
        e_t = jnp.exp(t - m_t)
        ebt[n] = e_t
        lt = m_t + jnp.log(jnp.sum(e_t, axis=0, keepdims=True))
        for k in range(2):
            mloc[2 * n + k:2 * n + k + 1, :] = m_t[:, 128 * k:128 * k + 128]
            stat[me, 2 * n + k:2 * n + k + 1, :] = lt[:, 128 * k:128 * k + 128]
        if n == 0:
            far_slot = r_slot(2)
            for part in range(2):
                arrive(r_half(far_slot, part), s_r + 2 + part)
                push(r_half(far_slot, part), r_half(far_slot, part), s_rs + 3 + part, sibling)

    arrive(rbuf.at[r_sib(0)], s_rs + 0)
    arrive(rbuf.at[r_sib(3)], s_rs + 1)
    arrive(rbuf.at[r_sib(1)], s_rs + 2)
    for part in range(2):
        arrive(r_half(r_sib(2), part), s_rs + 3 + part)

    r_all = jnp.concatenate([rbuf[k] for k in (0, 1, 2, 4, 5, 6)], axis=1)
    for n in range(4):
        qc = qbuf[4 * n:4 * n + 4].reshape(256, D)
        s = dot(r_all, qc, NT) * scale
        m_s = jnp.max(s, axis=0, keepdims=True)
        e_s = jnp.exp(s - m_s)
        ebs[n] = e_s
        ls = m_s + jnp.log(jnp.sum(e_s, axis=0, keepdims=True))
        e_t = ebt[n]
        cross = jnp.sum(e_t * (tbuf[n] - s), axis=0, keepdims=True)
        cross = cross / jnp.sum(e_t, axis=0, keepdims=True)
        for k in range(2):
            r = 2 * n + k
            mloc[8 + r:9 + r, :] = m_s[:, 128 * k:128 * k + 128]
            stat[me, 8 + r:9 + r, :] = ls[:, 128 * k:128 * k + 128]
            stat[me, 16 + r:17 + r, :] = cross[:, 128 * k:128 * k + 128]

    s_st = block(16)
    for a in range(4):
        for b in range(4):
            if (a, b) != (0, 0):
                push(stat.at[me], stat.at[me], s_st + ((4 - a) % 4) * 4 + (4 - b) % 4, dev_yz(a, b))
    for a in range(4):
        for b in range(4):
            if (a, b) != (0, 0):
                arrive(stat.at[((y + a) % 4) * 4 + (z + b) % 4], s_st + a * 4 + b)

    st = stat[...]
    lt, ls, cx = st[:, 0:8], st[:, 8:16], st[:, 16:24]
    top_t = jnp.max(lt, axis=0)
    top_s = jnp.max(ls, axis=0)
    big_t = top_t + jnp.log(jnp.sum(jnp.exp(lt - top_t[None]), axis=0))
    big_s = top_s + jnp.log(jnp.sum(jnp.exp(ls - top_s[None]), axis=0))
    cross = jnp.sum(jnp.exp(lt - big_t[None]) * cx, axis=0)
    divb[xl] = cross - big_t + big_s
    s_d = block(1)
    push(divb.at[xl], divb.at[xl], s_d, dev(x + 1 - 2 * xl, y, z, core))
    f_t = jnp.exp(mloc[0:8, :] - big_t)
    f_s = jnp.exp(mloc[8:16, :] - big_s)
    weight = (PB * 32 / 64.0) * scale

    grads = []
    for n in range(4):
        for k in range(2):
            r = 2 * n + k
            cols = slice(128 * k, 128 * k + 128)
            diff = ebs[n, :, cols] * f_s[r:r + 1] - ebt[n, :, cols] * f_t[r:r + 1]
            grads.append((diff * weight).astype(BF16))
    grad_scores = jnp.concatenate(grads, axis=1)

    def partial(group, dest):
        for k in range(3):
            at = pl.multiple_of(group * 384 + 128 * k, 128)
            qcol = qbuf[:, :, pl.ds(at, 128)].reshape(QN, 128)
            dest[k] = dot(grad_scores, qcol, NN)

    partial(1 - core, gsrc)
    s_g = block(1)
    push(gsrc, gsib, s_g, sibling)
    partial(core, gown)
    gown[3] = jnp.zeros((ROWS, TILE), F32)
    arrive(gsib, s_g)
    gown[0:3] = gown[0:3] + gsib[...]

    s_1 = block(2)
    s_2 = block(2)
    far = (u + 2) % 4
    for part, to in ((0, right), (1, left)):
        push(gown.at[far, pl.ds(128 * part, 128), :], rs1.at[part], s_1 + part, to)
    for part, to, step in ((0, right, 1), (1, left, 3)):
        d = (u + step) % 4
        arrive(rs1.at[part], s_1 + part)
        keep, add = (128, 0) if part == 0 else (0, 128)
        rs2s[part, pl.ds(keep, 128), :] = gown[d, pl.ds(keep, 128), :]
        rs2s[part, pl.ds(add, 128), :] = gown[d, pl.ds(add, 128), :] + rs1[part]
        push(rs2s.at[part], rs2.at[part], s_2 + part, to)
    arrive(rs2.at[0], s_2)
    arrive(rs2.at[1], s_2 + 1)
    g = gown[u] + rs2[0] + rs2[1]

    g1, g2 = split2(g)
    gt = g.T
    inner = jnp.sum((gt * rt[...].reshape(TILE, ROWS)).reshape(GROUPS, SUB, ROWS), axis=1)
    rhs_b = jnp.concatenate([g1, g2, g1, stack_rows(split3(-inner), ROWS)], axis=1)
    g12 = jnp.concatenate([g1, g2], axis=1)
    xo = jnp.concatenate([xt, jnp.full((ROWS, TILE), 1.0, BF16)], axis=1)
    lane_group = lax.broadcasted_iota(jnp.int32, (1, TILE), 1) // SUB

    def grad_step(i, carry):
        diff = dot(lhs_b[...] * group_mask(i), rhs_b, NT)
        w1 = a1b[i]
        w2 = a2b[i]
        d1, d2 = split2((w1.astype(F32) + w2.astype(F32)) * diff)
        o1 = dot(w1, g12, NN)
        o2 = dot(w2, g1, NN)
        o3 = dot(d1, xo, NN) + dot(d2, xo, NN)
        val = o1[:, :TILE] + o1[:, TILE:] + o2 + o3[:, :TILE] - ct[...] * o3[:, TILE:]
        acc[...] = jnp.where(lane_group == i, val, acc[...])
        return carry

    acc[...] = jnp.zeros_like(acc)
    lax.fori_loop(0, GROUPS, grad_step, 0)
    dcs[...] = acc[...].T.reshape(GROUPS, SUB, CODES)

    s_c = block(16)
    for a in range(4):
        for b in range(4):
            if (a, b) != (0, 0):
                other = ((y + a) % 4) * 4 + (z + b) % 4
                push(dcs.at[other], dcr.at[me], s_c + ((4 - a) % 4) * 4 + (4 - b) % 4, dev_yz(a, b))
    dcr[me] = dcs[me]
    for a in range(4):
        for b in range(4):
            if (a, b) != (0, 0):
                arrive(dcr.at[((y + a) % 4) * 4 + (z + b) % 4], s_c + a * 4 + b)
    piece[...] = jnp.sum(dcr[...], axis=0)

    s_x = block(8)
    dbuf[me, mine] = piece[...]
    for step in range(4):
        for other in range(2):
            if (step, other) != (0, 0):
                who = core if other == 0 else 1 - core
                push(piece, dbuf.at[me, mine], s_x + ((4 - step) % 4) * 2 + other, dev_x(step, who))
    for step in range(4):
        for other in range(2):
            if (step, other) != (0, 0):
                s = r_slot(step) if other == 0 else r_sib(step)
                arrive(dbuf.at[me, s], s_x + step * 2 + other)

    def d_piece(s, h, part):
        if part is None:
            return dbuf.at[s, pl.ds(4 * h, 3), :, :]
        return dbuf.at[s, pl.ds(4 * h, 3), :, pl.ds(128 * part, 128)]

    dw = gather_plane(lambda h: d_piece(me, h, None), d_piece, block(64))
    for wave in dw:
        wave()
    for t in range(6):
        for p in range(PLANE):
            out_ref[t * TILE + p * SUB:t * TILE + (p + 1) * SUB, :] = dbuf[p, t + (t // 3)]

    arrive(divb.at[1 - xl], s_d)
    for k in range(4):
        for h in range(2):
            div_ref[4 * k + 2 * h:4 * k + 2 * h + 2, :] = divb[h, 2 * k:2 * k + 2, :]

    for copy in sends:
        copy.wait_send()


def local(passages, queries, codebook):
    vmem = pl.BlockSpec(memory_space=pltpu.VMEM)
    grad, divergence = pl.pallas_call(
        kernel,
        out_shape=(
            jax.ShapeDtypeStruct((D, CODES), F32),
            jax.ShapeDtypeStruct((16, 128), F32),
        ),
        in_specs=[vmem] * 3,
        out_specs=(vmem, vmem),
        scratch_shapes=[
            pltpu.VMEM((PLANE, QB, D), BF16),
            pltpu.VMEM((2, PB, D), BF16),
            pltpu.VMEM((8, ROWS, TILE), BF16),
            pltpu.VMEM((CODES, 4 * TILE), BF16),
            pltpu.VMEM((CODES, 4 * TILE), BF16),
            pltpu.VMEM((GROUPS, 32, CODES), BF16),
            pltpu.VMEM((CODES, TILE), F32),
            pltpu.VMEM((GROUPS, SUB, ROWS), F32),
            pltpu.VMEM((GROUPS, CODES, ROWS), BF16),
            pltpu.VMEM((GROUPS, CODES, ROWS), BF16),
            pltpu.VMEM((4, ROWS, 256), F32),
            pltpu.VMEM((4, ROWS, 256), F32),
            pltpu.VMEM((4, ROWS, 256), F32),
            pltpu.VMEM((16, 128), F32),
            pltpu.VMEM((PLANE, 24, 128), F32),
            pltpu.VMEM((4, ROWS, TILE), F32),
            pltpu.VMEM((3, ROWS, TILE), F32),
            pltpu.VMEM((3, ROWS, TILE), F32),
            pltpu.VMEM((2, 128, TILE), F32),
            pltpu.VMEM((2, 128, TILE), F32),
            pltpu.VMEM((2, ROWS, TILE), F32),
            pltpu.VMEM((2, ROWS, TILE), F32),
            pltpu.VMEM((CODES, TILE), F32),
            pltpu.VMEM((PLANE, SUB, CODES), F32),
            pltpu.VMEM((PLANE, SUB, CODES), F32),
            pltpu.VMEM((SUB, CODES), F32),
            pltpu.VMEM((PLANE, 8, SUB, CODES), F32),
            pltpu.VMEM((2, 8, 128), F32),
            pltpu.SemaphoreType.DMA((N_SEM,)),
            pltpu.SemaphoreType.DMA((192,)),
        ],
        compiler_params=pltpu.CompilerParams(
            collective_id=0, has_side_effects=True, vmem_limit_bytes=60 * 1024 * 1024
        ),
    )(passages, queries, codebook.reshape(D, CODES))
    return divergence.reshape(2048), grad.reshape(96, SUB, CODES)


def solution(mesh):
    placed = (P("corpus", None), P(("query", "corpus"), None), P())
    return jax.shard_map(
        local, mesh=mesh, in_specs=placed, out_specs=(P("query"), P()), check_vma=False
    )
```

```python
import functools

import jax
import jax.numpy as jnp
from jax import lax
from jax.experimental import pallas as pl
from jax.experimental.pallas import tpu as pltpu
from jax.sharding import PartitionSpec as P

MESH = pl.DeviceIdType.MESH
F32 = jnp.float32
BF16 = jnp.bfloat16
NT = (((1,), (1,)), ((), ()))
NN = (((1,), (0,)), ((), ()))

D = 768
SUB = 8
CODES = 256
QB = 64
PB = 128
PLANE = 16
TILE = 128
GROUPS = 16
ROWS = 256
QN = 1024
N_SEM = 160
FAR_FIRST = [(2, 2), (2, 1), (2, 3), (1, 2), (3, 2), (1, 1), (1, 3), (3, 1), (3, 3), (2, 0), (0, 2), (1, 0), (3, 0), (0, 1), (0, 3)]


def split3(value):
    high = value.astype(BF16)
    rest = value - high.astype(F32)
    mid = rest.astype(BF16)
    low = (rest - mid.astype(F32)).astype(BF16)
    return high, mid, low


def split2(value):
    high = value.astype(BF16)
    low = (value - high.astype(F32)).astype(BF16)
    return high, low


def dot(a, b, dims):
    return lax.dot_general(a, b, dims, preferred_element_type=F32)


def kernel(
    p_ref, q_ref, cb_ref,
    out_ref, div_ref,
    qbuf, pbuf, rbuf,
    lhs_f, lhs_b, cp3, ct, rt, a1b, a2b,
    tbuf, ebt, ebs, mloc, stat_t, stat,
    gown, gsib, gsrc, rs1, rs2, rs2s,
    acc, dcs, dcr, piece, dbuf, divb,
    send_sem, recv_sem,
):
    qi = lax.axis_index("query")
    ci = lax.axis_index("corpus")
    xh, core = qi // 2, qi % 2
    y, xl, z = ci // 8, (ci // 4) % 2, ci % 4
    x = xh * 2 + xl
    u = (x + 4 - 2 * core) % 4

    def dev(x_, y_, z_, core_):
        return ((x_ // 2) * 2 + core_, y_ * 8 + (x_ % 2) * 4 + z_)

    def dev_x(step, core_=None):
        return dev((x + step) % 4, y, z, core if core_ is None else core_)

    def dev_yz(dy, dz):
        return dev(x, (y + dy) % 4, (z + dz) % 4, core)

    sibling = dev(x, y, z, 1 - core)
    left, right = dev_x(3), dev_x(1)

    sends = []
    count = [0]

    def guarded(cond, action):
        if cond is None:
            action()
        else:
            pl.when(cond)(action)

    def push(src, dst, index, device, cond=None):
        copy = pltpu.make_async_remote_copy(
            src_ref=src, dst_ref=dst, send_sem=send_sem.at[len(sends)],
            recv_sem=recv_sem.at[index], device_id=device, device_id_type=MESH,
        )
        guarded(cond, copy.start)
        sends.append((copy, cond))

    def arrive(dst, index, cond=None):
        guarded(cond, pltpu.make_async_remote_copy(
            src_ref=dst, dst_ref=dst, send_sem=send_sem.at[0],
            recv_sem=recv_sem.at[index], device_id=sibling, device_id_type=MESH,
        ).wait_recv)

    def block(n):
        first = count[0]
        count[0] += n
        return first

    barrier = pltpu.get_barrier_semaphore()
    peers = [dev_x(s, c) for s in range(4) for c in (core, 1 - core)][1:]
    peers += [dev_yz(a, b) for a in range(4) for b in range(4)][1:]
    for peer in peers:
        pl.semaphore_signal(barrier, inc=1, device_id=peer, device_id_type=MESH)

    me = y * 4 + z
    qbuf[me] = q_ref[...]
    pbuf[xl] = p_ref[...]

    pl.semaphore_wait(barrier, len(peers))

    def gather_plane(own, piece_of, base):
        def rel(h, a, b):
            return (a, b) if h == 0 else (b, a)

        def slot(dy, dz):
            return ((y + dy) % 4) * 4 + (z + dz) % 4

        def sem(dy, dz, h, part):
            return base + (((dy % 4) * 4 + dz % 4) * 2 + h) * 2 + (part or 0)

        def send(h, a, b, part, first_axis, step):
            dy, dz = rel(h, a, b)
            sy, sz = rel(h, step, 0) if first_axis else rel(h, 0, step)
            dst = piece_of(slot(dy, dz), h, part)
            src = own(h) if (a, b) == (0, 0) else dst
            push(src, dst, sem(dy - sy, dz - sz, h, part), dev_yz(sy % 4, sz % 4))

        def wait(h, a, b, part):
            dy, dz = rel(h, a, b)
            arrive(piece_of(slot(dy, dz), h, part), sem(dy, dz, h, part))

        def wave0():
            for h in range(2):
                for step in (1, 3, 2):
                    send(h, 0, 0, None, True, step)
            for h in range(2):
                for step in (1, 3):
                    send(h, 0, 0, None, False, step)

        def wave1():
            for h in range(2):
                for a in (3, 1):
                    wait(h, a, 0, None)
                    send(h, a, 0, None, False, 1)
                    send(h, a, 0, None, False, 3)
            for h in range(2):
                for b, part, step in ((3, 0, 1), (1, 1, 3)):
                    wait(h, 0, b, None)
                    send(h, 0, b, part, False, step)

        def wave2():
            for h in range(2):
                wait(h, 2, 0, None)
                for step in (2, 1, 3):
                    send(h, 2, 0, None, False, step)
            for h in range(2):
                for a in (3, 1):
                    for b, part, step in ((3, 0, 1), (1, 1, 3)):
                        wait(h, a, b, None)
                        send(h, a, b, part, False, step)

        def wave3():
            for h in range(2):
                for a in (0, 1, 3):
                    wait(h, a, 2, 0)
                    wait(h, a, 2, 1)
                for b in (1, 3, 2):
                    wait(h, 2, b, None)

        return wave0, wave1, wave2, wave3

    def q_piece(s, h, part):
        if part is None:
            return qbuf.at[s, pl.ds(32 * h, 32), :]
        return qbuf.at[s, pl.ds(32 * h + 16 * part, 16), :]

    qw = gather_plane(lambda h: q_ref.at[pl.ds(32 * h, 32), :], q_piece, block(64))
    s_p = block(1)
    x_to = (x + 3 + 2 * core) % 4
    push(p_ref, pbuf.at[xl], s_p, dev(x_to, y, z, core))
    qw[0]()

    tile = 3 * core + jnp.minimum(u, 2)
    col = pl.multiple_of(tile * TILE, TILE)
    cb = cb_ref[pl.ds(col, TILE), :]
    grouped = cb.reshape(GROUPS, SUB, CODES)
    bias = -0.5 * jnp.sum(grouped * grouped, axis=1)
    c_parts = split3(cb)
    c32 = [c.astype(F32).reshape(GROUPS, SUB, CODES) for c in c_parts]
    cp3[...] = jnp.concatenate(c32 + [jnp.zeros((GROUPS, SUB, CODES), F32)], axis=1).astype(BF16)
    cbt = cb.T
    ct[...] = cbt
    t1, t2, t3 = split3(cbt)

    def stack_rows(parts, width):
        rows = [p.astype(F32) for p in parts]
        rows.append(jnp.zeros((TILE - len(parts) * GROUPS, width), F32))
        return jnp.concatenate(rows, axis=0).T.astype(BF16)

    lane = lax.broadcasted_iota(jnp.int32, (1, 4 * TILE), 1)
    in_tile = lane % TILE
    group_id = jnp.where(
        lane < 3 * TILE, in_tile // SUB, jnp.where(in_tile < 3 * GROUPS, in_tile % GROUPS, -1)
    )
    ones48 = jnp.where(
        lax.broadcasted_iota(jnp.int32, (CODES, TILE), 1) < 3 * GROUPS, 1.0, 0.0
    ).astype(BF16)
    lhs_f[...] = jnp.concatenate([t1, t2, t3, stack_rows(split3(bias), CODES)], axis=1)
    lhs_b[...] = jnp.concatenate([t1, t1, t2, ones48], axis=1)

    qw[1]()
    arrive(pbuf.at[1 - xl], s_p)

    xt = jnp.concatenate([pbuf[0, :, pl.ds(col, TILE)], pbuf[1, :, pl.ds(col, TILE)]], axis=0)
    rhs_f = jnp.concatenate([xt, xt, xt, ones48], axis=1)

    def group_mask(i):
        return jnp.where(group_id == i, 1.0, 0.0).astype(BF16)

    def assign_step(i, carry):
        logits = dot(lhs_f[...] * group_mask(i), rhs_f, NT)
        top = jnp.max(logits, axis=0, keepdims=True)
        e = jnp.exp(logits - top)
        w = e * (1.0 / jnp.sum(e, axis=0, keepdims=True))
        w1, w2 = split2(w)
        a1b[i] = w1
        a2b[i] = w2
        got = dot(cp3[i], w1, NN) + dot(cp3[i], w2, NN)
        rt[i] = got[0:8] + got[8:16] + got[16:24]
        return carry

    lax.fori_loop(0, 8, assign_step, 0)
    qw[2]()
    lax.fori_loop(8, 16, assign_step, 0)

    mine = core * 4 + u
    rbuf[mine] = rt[...].reshape(TILE, ROWS).T.astype(BF16)

    def r_slot(step):
        return core * 4 + (u + step) % 4

    def r_sib(step):
        return (1 - core) * 4 + (u + 2 + step) % 4

    s_r = block(4)
    s_rs = block(4)
    owner = u != 3
    for step in (2, 1, 3):
        push(rbuf.at[mine], rbuf.at[mine], s_r + 4 - step, dev_x(step), owner)
    push(rbuf.at[mine], rbuf.at[mine], s_rs, sibling, owner)
    for step in (1, 3, 2):
        s = r_slot(step)
        real = (u + step) % 4 != 3
        arrive(rbuf.at[s], s_r + step, real)
        push(rbuf.at[s], rbuf.at[s], s_rs + step, sibling, real)
    qw[3]()

    p_all = pbuf[...].reshape(ROWS, D)
    scale = float(D) ** (-0.5)
    for n in range(4):
        qc = qbuf[4 * n:4 * n + 4].reshape(256, D)
        t = dot(p_all, qc, NT) * scale
        m_t = jnp.max(t, axis=0, keepdims=True)
        tbuf[n] = t
        e_t = jnp.exp(t - m_t)
        ebt[n] = e_t
        lt = m_t + jnp.log(jnp.sum(e_t, axis=0, keepdims=True))
        for k in range(2):
            mloc[2 * n + k:2 * n + k + 1, :] = m_t[:, 128 * k:128 * k + 128]
            stat_t[me, 2 * n + k:2 * n + k + 1, :] = lt[:, 128 * k:128 * k + 128]

    def plane_send(buf, base):
        for a, b in FAR_FIRST:
            push(buf.at[me], buf.at[me], base + ((4 - a) % 4) * 4 + (4 - b) % 4, dev_yz(a, b))

    def plane_wait(buf, base):
        for a, b in FAR_FIRST:
            arrive(buf.at[((y + a) % 4) * 4 + (z + b) % 4], base + a * 4 + b)

    s_ta = block(16)
    plane_send(stat_t, s_ta)
    for step in (0, 1, 3, 2):
        arrive(rbuf.at[r_sib(step)], s_rs + step, (u + 2 + step) % 4 != 3)

    r_all = jnp.concatenate([rbuf[k] for k in (0, 1, 2, 4, 5, 6)], axis=1)
    for n in range(4):
        qc = qbuf[4 * n:4 * n + 4].reshape(256, D)
        s = dot(r_all, qc, NT) * scale
        m_s = jnp.max(s, axis=0, keepdims=True)
        e_s = jnp.exp(s - m_s)
        ebs[n] = e_s
        ls = m_s + jnp.log(jnp.sum(e_s, axis=0, keepdims=True))
        e_t = ebt[n]
        cross = jnp.sum(e_t * (tbuf[n] - s), axis=0, keepdims=True)
        cross = cross / jnp.sum(e_t, axis=0, keepdims=True)
        for k in range(2):
            r = 2 * n + k
            mloc[8 + r:9 + r, :] = m_s[:, 128 * k:128 * k + 128]
            stat[me, r:r + 1, :] = ls[:, 128 * k:128 * k + 128]
            stat[me, 8 + r:9 + r, :] = cross[:, 128 * k:128 * k + 128]

    s_st = block(16)
    plane_send(stat, s_st)
    plane_wait(stat_t, s_ta)
    lt = stat_t[...]
    plane_wait(stat, s_st)
    ls, cx = stat[:, 0:8], stat[:, 8:16]
    top_t = jnp.max(lt, axis=0)
    top_s = jnp.max(ls, axis=0)
    big_t = top_t + jnp.log(jnp.sum(jnp.exp(lt - top_t[None]), axis=0))
    big_s = top_s + jnp.log(jnp.sum(jnp.exp(ls - top_s[None]), axis=0))
    cross = jnp.sum(jnp.exp(lt - big_t[None]) * cx, axis=0)
    divb[xl] = cross - big_t + big_s
    s_d = block(1)
    push(divb.at[xl], divb.at[xl], s_d, dev(x + 1 - 2 * xl, y, z, core))
    f_t = jnp.exp(mloc[0:8, :] - big_t)
    f_s = jnp.exp(mloc[8:16, :] - big_s)
    weight = (PB * 32 / 64.0) * scale

    grads = []
    for n in range(4):
        for k in range(2):
            r = 2 * n + k
            cols = slice(128 * k, 128 * k + 128)
            diff = ebs[n, :, cols] * f_s[r:r + 1] - ebt[n, :, cols] * f_t[r:r + 1]
            grads.append((diff * weight).astype(BF16))
    grad_scores = jnp.concatenate(grads, axis=1)

    def partial(group, d):
        at = pl.multiple_of(group * 384 + jnp.minimum(d, 2) * TILE, TILE)
        return dot(grad_scores, qbuf[:, :, pl.ds(at, TILE)].reshape(QN, TILE), NN)

    s_g = block(4)
    order = (2, 1, 3, 0)
    for k, step in enumerate(order):
        gsrc[k] = partial(1 - core, (u + 2 + step) % 4)
        push(gsrc.at[k], gsib.at[k], s_g + k, sibling)
    for k, step in enumerate(order):
        gown[k] = partial(core, (u + step) % 4)

    s_1 = block(2)
    s_2 = block(4)

    def half(n):
        return pl.ds(128 * n, 128)

    far_ok = (u + 2) % 4 != 3
    arrive(gsib.at[0], s_g)
    gown[0] = gown[0] + gsib[0]
    for part, to in ((0, right), (1, left)):
        push(gown.at[0, half(part), :], rs1.at[part], s_1 + part, to, far_ok)
    for part, to, step in ((0, right, 1), (1, left, 3)):
        k = 1 + part
        arrive(gsib.at[k], s_g + k)
        gown[k] = gown[k] + gsib[k]
        push(
            gown.at[k, half(1 - part), :], rs2.at[part, half(1 - part), :],
            s_2 + 2 * part, to, (u + step) % 4 != 3,
        )
    arrive(gsib.at[3], s_g + 3)
    gown[3] = gown[3] + gsib[3]
    for part, to, step in ((0, right, 1), (1, left, 3)):
        k = 1 + part
        ok = (u + step) % 4 != 3
        arrive(rs1.at[part], s_1 + part, ok)
        rs2s[part] = gown[k, half(part), :] + rs1[part]
        push(rs2s.at[part], rs2.at[part, half(part), :], s_2 + 2 * part + 1, to, ok)
    for part in range(2):
        arrive(rs2.at[part, half(1 - part), :], s_2 + 2 * part, owner)
        arrive(rs2.at[part, half(part), :], s_2 + 2 * part + 1, owner)
    g = gown[3] + rs2[0] + rs2[1]

    g1, g2 = split2(g)
    gt = g.T
    inner = jnp.sum((gt * rt[...].reshape(TILE, ROWS)).reshape(GROUPS, SUB, ROWS), axis=1)
    rhs_b = jnp.concatenate([g1, g2, g1, stack_rows(split3(-inner), ROWS)], axis=1)
    g12 = jnp.concatenate([g1, g2], axis=1)
    xo = jnp.concatenate([xt, jnp.full((ROWS, TILE), 1.0, BF16)], axis=1)
    lane_group = lax.broadcasted_iota(jnp.int32, (1, TILE), 1) // SUB

    def grad_step(i, carry):
        diff = dot(lhs_b[...] * group_mask(i), rhs_b, NT)
        w1 = a1b[i]
        w2 = a2b[i]
        d1, d2 = split2((w1.astype(F32) + w2.astype(F32)) * diff)
        o1 = dot(w1, g12, NN)
        o2 = dot(w2, g1, NN)
        o3 = dot(d1, xo, NN) + dot(d2, xo, NN)
        val = o1[:, :TILE] + o1[:, TILE:] + o2 + o3[:, :TILE] - ct[...] * o3[:, TILE:]
        acc[...] = jnp.where(lane_group == i, val, acc[...])
        return carry

    acc[...] = jnp.zeros_like(acc)
    lax.fori_loop(0, GROUPS, grad_step, 0)
    dcs[...] = acc[...].T.reshape(GROUPS, SUB, CODES)

    s_c = block(16)
    for a, b in FAR_FIRST:
        other = ((y + a) % 4) * 4 + (z + b) % 4
        push(dcs.at[other], dcr.at[me], s_c + ((4 - a) % 4) * 4 + (4 - b) % 4, dev_yz(a, b))
    dcr[me] = dcs[me]
    plane_wait(dcr, s_c)
    piece[...] = jnp.sum(dcr[...], axis=0)

    s_x = block(4)
    dbuf[me, mine] = piece[...]
    for step in (2, 1, 3):
        push(piece, dbuf.at[me, mine], s_x + 4 - step, dev_x(step), owner)
    for step in (1, 3, 2):
        arrive(dbuf.at[me, r_slot(step)], s_x + step, (u + step) % 4 != 3)

    def trio(s, c):
        return dbuf.at[s, pl.ds(4 * c, 3), :, :]

    s_f = block(16)
    s_fs = block(16)
    for a, b in FAR_FIRST:
        push(trio(me, core), trio(me, core), s_f + ((4 - a) % 4) * 4 + (4 - b) % 4, dev_yz(a, b))
    push(trio(me, core), trio(me, core), s_fs, sibling)
    for a, b in FAR_FIRST[::-1]:
        s = ((y + a) % 4) * 4 + (z + b) % 4
        arrive(trio(s, core), s_f + a * 4 + b)
        push(trio(s, core), trio(s, core), s_fs + a * 4 + b, sibling)
    for a, b in [(0, 0)] + FAR_FIRST[::-1]:
        arrive(trio(((y + a) % 4) * 4 + (z + b) % 4, 1 - core), s_fs + a * 4 + b)
    for t in range(6):
        for p in range(PLANE):
            out_ref[t * TILE + p * SUB:t * TILE + (p + 1) * SUB, :] = dbuf[p, t + (t // 3)]

    arrive(divb.at[1 - xl], s_d)
    for k in range(4):
        for h in range(2):
            div_ref[4 * k + 2 * h:4 * k + 2 * h + 2, :] = divb[h, 2 * k:2 * k + 2, :]

    for copy, cond in sends:
        guarded(cond, copy.wait_send)


def local(passages, queries, codebook):
    vmem = pl.BlockSpec(memory_space=pltpu.VMEM)
    grad, divergence = pl.pallas_call(
        kernel,
        out_shape=(
            jax.ShapeDtypeStruct((D, CODES), F32),
            jax.ShapeDtypeStruct((16, 128), F32),
        ),
        in_specs=[vmem] * 3,
        out_specs=(vmem, vmem),
        scratch_shapes=[
            pltpu.VMEM((PLANE, QB, D), BF16),
            pltpu.VMEM((2, PB, D), BF16),
            pltpu.VMEM((8, ROWS, TILE), BF16),
            pltpu.VMEM((CODES, 4 * TILE), BF16),
            pltpu.VMEM((CODES, 4 * TILE), BF16),
            pltpu.VMEM((GROUPS, 32, CODES), BF16),
            pltpu.VMEM((CODES, TILE), F32),
            pltpu.VMEM((GROUPS, SUB, ROWS), F32),
            pltpu.VMEM((GROUPS, CODES, ROWS), BF16),
            pltpu.VMEM((GROUPS, CODES, ROWS), BF16),
            pltpu.VMEM((4, ROWS, 256), F32),
            pltpu.VMEM((4, ROWS, 256), F32),
            pltpu.VMEM((4, ROWS, 256), F32),
            pltpu.VMEM((16, 128), F32),
            pltpu.VMEM((PLANE, 8, 128), F32),
            pltpu.VMEM((PLANE, 16, 128), F32),
            pltpu.VMEM((4, ROWS, TILE), F32),
            pltpu.VMEM((4, ROWS, TILE), F32),
            pltpu.VMEM((4, ROWS, TILE), F32),
            pltpu.VMEM((2, 128, TILE), F32),
            pltpu.VMEM((2, ROWS, TILE), F32),
            pltpu.VMEM((2, 128, TILE), F32),
            pltpu.VMEM((CODES, TILE), F32),
            pltpu.VMEM((PLANE, SUB, CODES), F32),
            pltpu.VMEM((PLANE, SUB, CODES), F32),
            pltpu.VMEM((SUB, CODES), F32),
            pltpu.VMEM((PLANE, 8, SUB, CODES), F32),
            pltpu.VMEM((2, 8, 128), F32),
            pltpu.SemaphoreType.DMA((N_SEM,)),
            pltpu.SemaphoreType.DMA((200,)),
        ],
        compiler_params=pltpu.CompilerParams(
            collective_id=0, has_side_effects=True, vmem_limit_bytes=60 * 1024 * 1024
        ),
    )(passages, queries, codebook.reshape(D, CODES))
    return divergence.reshape(2048), grad.reshape(96, SUB, CODES)


def solution(mesh):
    placed = (P("corpus", None), P(("query", "corpus"), None), P())
    return jax.shard_map(
        local, mesh=mesh, in_specs=placed, out_specs=(P("query"), P()), check_vma=False
    )
```

```python
import functools

import jax
import jax.numpy as jnp
from jax import lax
from jax.experimental import pallas as pl
from jax.experimental.pallas import tpu as pltpu
from jax.sharding import PartitionSpec as P

MESH = pl.DeviceIdType.MESH
F32 = jnp.float32
BF16 = jnp.bfloat16
NT = (((1,), (1,)), ((), ()))
NN = (((1,), (0,)), ((), ()))

D = 768
SUB = 8
CODES = 256
QB = 64
PB = 128
PLANE = 16
TILE = 128
GROUPS = 16
ROWS = 256
QN = 1024
BEFORE = 3
N_SEM = 160
FAR_FIRST = [(2, 2), (2, 1), (2, 3), (1, 2), (3, 2), (1, 1), (1, 3), (3, 1), (3, 3), (2, 0), (0, 2), (1, 0), (3, 0), (0, 1), (0, 3)]


def split3(value):
    high = value.astype(BF16)
    rest = value - high.astype(F32)
    mid = rest.astype(BF16)
    low = (rest - mid.astype(F32)).astype(BF16)
    return high, mid, low


def split2(value):
    high = value.astype(BF16)
    low = (value - high.astype(F32)).astype(BF16)
    return high, low


def dot(a, b, dims):
    return lax.dot_general(a, b, dims, preferred_element_type=F32)


def kernel(
    p_ref, q_ref, cb_ref,
    out_ref, div_ref,
    qbuf, pbuf, rbuf,
    xtb, xpack, lhs_f, cp3, rt, inv, a1b, a2b,
    tbuf, ebt, ebs, mloc, stat_t, stat,
    gown, gsib, gsrc, rs1, rs2, rs2s,
    gl, ts, xlt, gpack, dcs, dcr, piece, dbuf, divb,
    send_sem, recv_sem,
):
    qi = lax.axis_index("query")
    ci = lax.axis_index("corpus")
    xh, core = qi // 2, qi % 2
    y, xl, z = ci // 8, (ci // 4) % 2, ci % 4
    x = xh * 2 + xl
    u = (x + 4 - 2 * core) % 4

    def dev(x_, y_, z_, core_):
        return ((x_ // 2) * 2 + core_, y_ * 8 + (x_ % 2) * 4 + z_)

    def dev_x(step, core_=None):
        return dev((x + step) % 4, y, z, core if core_ is None else core_)

    def dev_yz(dy, dz):
        return dev(x, (y + dy) % 4, (z + dz) % 4, core)

    sibling = dev(x, y, z, 1 - core)
    left, right = dev_x(3), dev_x(1)

    sends = []
    count = [0]

    def guarded(cond, action):
        if cond is None:
            action()
        else:
            pl.when(cond)(action)

    def push(src, dst, index, device, cond=None):
        copy = pltpu.make_async_remote_copy(
            src_ref=src, dst_ref=dst, send_sem=send_sem.at[len(sends)],
            recv_sem=recv_sem.at[index], device_id=device, device_id_type=MESH,
        )
        guarded(cond, copy.start)
        sends.append((copy, cond))

    def arrive(dst, index, cond=None):
        guarded(cond, pltpu.make_async_remote_copy(
            src_ref=dst, dst_ref=dst, send_sem=send_sem.at[0],
            recv_sem=recv_sem.at[index], device_id=sibling, device_id_type=MESH,
        ).wait_recv)

    def block(n):
        first = count[0]
        count[0] += n
        return first

    barrier = pltpu.get_barrier_semaphore()
    peers = [dev_x(s, c) for s in range(4) for c in (core, 1 - core)][1:]
    peers += [dev_yz(a, b) for a in range(4) for b in range(4)][1:]
    for peer in peers:
        pl.semaphore_signal(barrier, inc=1, device_id=peer, device_id_type=MESH)

    me = y * 4 + z
    qbuf[me] = q_ref[...]
    pbuf[xl] = p_ref[...]

    def tile_col(u_):
        return pl.multiple_of((3 * core + jnp.minimum(u_, 2)) * TILE, TILE)

    col = tile_col(u)
    cb = cb_ref[pl.ds(col, TILE), :]
    grouped = cb.reshape(GROUPS, SUB, CODES)
    bias = -0.5 * jnp.sum(grouped * grouped, axis=1, keepdims=True)
    b_parts = [jnp.broadcast_to(b.astype(F32), grouped.shape) for b in split3(bias)]
    row = lax.broadcasted_iota(jnp.int32, grouped.shape, 1)
    extra = jnp.where(row == 3, 1.0, 0.0)
    for k in range(3):
        extra = jnp.where(row == k, b_parts[k], extra)
    c_parts = [c.astype(F32).reshape(GROUPS, SUB, CODES) for c in split3(cb)]
    packed = jnp.concatenate(c_parts + [extra], axis=1)
    cp3[...] = packed.reshape(8, 64, CODES).astype(BF16)
    for g in range(4):
        lhs_f[g] = packed[4 * g:4 * g + 4].reshape(TILE, CODES).T.astype(BF16)

    lane = lax.broadcasted_iota(jnp.int32, (TILE, 4 * TILE), 1)
    source = lax.broadcasted_iota(jnp.int32, (TILE, 4 * TILE), 0)
    inner_lane = lane % 32
    select = jnp.where(
        (source == (lane // 32) * SUB + lane % SUB) & (inner_lane < 24), 1.0, 0.0
    ).astype(BF16)
    tail_ones = jnp.where(
        (inner_lane[0:1] >= 24) & (inner_lane[0:1] < 27), 1.0, 0.0
    )
    pack_lane = lax.broadcasted_iota(jnp.int32, (1, TILE), 1) // 32

    def pack_mask(j):
        return jnp.where(pack_lane == j, 1.0, 0.0).astype(BF16)

    def pack_rows(h):
        packs = (dot(xtb[h], select, NN) + tail_ones).astype(BF16)
        for g in range(4):
            xpack[g] = packs[:, TILE * g:TILE * g + TILE]

    def assign_step(h):
        lanes = pl.ds(pl.multiple_of(h * 128, 128), 128)

        def step(v, carry):
            g, j = v // 2, 2 * (v % 2)
            xp = xpack[g]
            rhs = jnp.concatenate([xp * pack_mask(j), xp * pack_mask(j + 1)], axis=0)
            logits = dot(lhs_f[g], rhs, NT)
            e1, e2 = split2(jnp.exp(logits - jnp.max(logits, axis=0, keepdims=True)))
            got = dot(cp3[v], e1, NN) + dot(cp3[v], e2, NN)
            for k in range(2):
                i = 2 * v + k
                half_lanes = slice(128 * k, 128 * k + 128)
                a1b[i, :, lanes] = e1[:, half_lanes]
                a2b[i, :, lanes] = e2[:, half_lanes]
                part = got[32 * k:32 * k + 32, half_lanes]
                scale_i = 1.0 / part[27:28]
                inv[i, :, lanes] = scale_i
                rt[i, :, lanes] = (part[0:8] + part[8:16] + part[16:24]) * scale_i
            return carry

        return step

    xtb[xl] = p_ref[:, pl.ds(col, TILE)]
    pack_rows(xl)
    lax.fori_loop(0, BEFORE, assign_step(xl), 0)
    pl.semaphore_wait(barrier, len(peers))

    def gather_plane(own, piece_of, base):
        def rel(h, a, b):
            return (a, b) if h == 0 else (b, a)

        def slot(dy, dz):
            return ((y + dy) % 4) * 4 + (z + dz) % 4

        def sem(dy, dz, h, part):
            return base + (((dy % 4) * 4 + dz % 4) * 2 + h) * 2 + (part or 0)

        def send(h, a, b, part, first_axis, step):
            dy, dz = rel(h, a, b)
            sy, sz = rel(h, step, 0) if first_axis else rel(h, 0, step)
            dst = piece_of(slot(dy, dz), h, part)
            src = own(h) if (a, b) == (0, 0) else dst
            push(src, dst, sem(dy - sy, dz - sz, h, part), dev_yz(sy % 4, sz % 4))

        def wait(h, a, b, part):
            dy, dz = rel(h, a, b)
            arrive(piece_of(slot(dy, dz), h, part), sem(dy, dz, h, part))

        def wave0():
            for h in range(2):
                for step in (1, 3, 2):
                    send(h, 0, 0, None, True, step)
            for h in range(2):
                for step in (1, 3):
                    send(h, 0, 0, None, False, step)

        def wave1():
            for h in range(2):
                for a in (3, 1):
                    wait(h, a, 0, None)
                    send(h, a, 0, None, False, 1)
                    send(h, a, 0, None, False, 3)
            for h in range(2):
                for b, part, step in ((3, 0, 1), (1, 1, 3)):
                    wait(h, 0, b, None)
                    send(h, 0, b, part, False, step)

        def wave2():
            for h in range(2):
                wait(h, 2, 0, None)
                for step in (2, 1, 3):
                    send(h, 2, 0, None, False, step)
            for h in range(2):
                for a in (3, 1):
                    for b, part, step in ((3, 0, 1), (1, 1, 3)):
                        wait(h, a, b, None)
                        send(h, a, b, part, False, step)

        def wave3():
            for h in range(2):
                for a in (0, 1, 3):
                    wait(h, a, 2, 0)
                    wait(h, a, 2, 1)
                for b in (1, 3, 2):
                    wait(h, 2, b, None)

        return wave0, wave1, wave2, wave3

    def q_piece(s, h, part):
        if part is None:
            return qbuf.at[s, pl.ds(32 * h, 32), :]
        return qbuf.at[s, pl.ds(32 * h + 16 * part, 16), :]

    qw = gather_plane(lambda h: q_ref.at[pl.ds(32 * h, 32), :], q_piece, block(64))
    s_p = block(2)
    x_to = (x + 3 + 2 * core) % 4
    p_to = dev(x_to, y, z, core)
    col_to = tile_col((x_to + 4 - 2 * core) % 4)
    push(p_ref.at[:, pl.ds(col_to, TILE)], xtb.at[xl], s_p, p_to)
    qw[0]()
    push(p_ref, pbuf.at[xl], s_p + 1, p_to)

    lax.fori_loop(BEFORE, 8, assign_step(xl), 0)
    qw[1]()
    arrive(xtb.at[1 - xl], s_p)
    pack_rows(1 - xl)
    lax.fori_loop(0, 4, assign_step(1 - xl), 0)
    qw[2]()
    lax.fori_loop(4, 8, assign_step(1 - xl), 0)

    mine = core * 4 + u
    rbuf[mine] = rt[...].reshape(TILE, ROWS).T.astype(BF16)

    def r_slot(step):
        return core * 4 + (u + step) % 4

    def r_sib(step):
        return (1 - core) * 4 + (u + 2 + step) % 4

    s_r = block(4)
    s_rs = block(4)
    owner = u != 3
    for step in (2, 1, 3):
        push(rbuf.at[mine], rbuf.at[mine], s_r + 4 - step, dev_x(step), owner)
    push(rbuf.at[mine], rbuf.at[mine], s_rs, sibling, owner)
    for step in (1, 3, 2):
        s = r_slot(step)
        real = (u + step) % 4 != 3
        arrive(rbuf.at[s], s_r + step, real)
        push(rbuf.at[s], rbuf.at[s], s_rs + step, sibling, real)
    qw[3]()
    arrive(pbuf.at[1 - xl], s_p + 1)

    p_all = pbuf[...].reshape(ROWS, D)
    scale = float(D) ** (-0.5)
    for n in range(4):
        qc = qbuf[4 * n:4 * n + 4].reshape(256, D)
        t = dot(p_all, qc, NT) * scale
        m_t = jnp.max(t, axis=0, keepdims=True)
        tbuf[n] = t
        e_t = jnp.exp(t - m_t)
        ebt[n] = e_t
        lt = m_t + jnp.log(jnp.sum(e_t, axis=0, keepdims=True))
        for k in range(2):
            mloc[2 * n + k:2 * n + k + 1, :] = m_t[:, 128 * k:128 * k + 128]
            stat_t[me, 2 * n + k:2 * n + k + 1, :] = lt[:, 128 * k:128 * k + 128]

    def plane_send(buf, base):
        for a, b in FAR_FIRST:
            push(buf.at[me], buf.at[me], base + ((4 - a) % 4) * 4 + (4 - b) % 4, dev_yz(a, b))

    def plane_wait(buf, base):
        for a, b in FAR_FIRST:
            arrive(buf.at[((y + a) % 4) * 4 + (z + b) % 4], base + a * 4 + b)

    s_ta = block(16)
    plane_send(stat_t, s_ta)
    for step in (0, 1, 3, 2):
        arrive(rbuf.at[r_sib(step)], s_rs + step, (u + 2 + step) % 4 != 3)

    r_all = jnp.concatenate([rbuf[k] for k in (0, 1, 2, 4, 5, 6)], axis=1)
    for n in range(4):
        qc = qbuf[4 * n:4 * n + 4].reshape(256, D)
        s = dot(r_all, qc, NT) * scale
        m_s = jnp.max(s, axis=0, keepdims=True)
        e_s = jnp.exp(s - m_s)
        ebs[n] = e_s
        ls = m_s + jnp.log(jnp.sum(e_s, axis=0, keepdims=True))
        e_t = ebt[n]
        cross = jnp.sum(e_t * (tbuf[n] - s), axis=0, keepdims=True)
        cross = cross / jnp.sum(e_t, axis=0, keepdims=True)
        for k in range(2):
            r = 2 * n + k
            mloc[8 + r:9 + r, :] = m_s[:, 128 * k:128 * k + 128]
            stat[me, r:r + 1, :] = ls[:, 128 * k:128 * k + 128]
            stat[me, 8 + r:9 + r, :] = cross[:, 128 * k:128 * k + 128]

    s_st = block(16)
    plane_send(stat, s_st)
    plane_wait(stat_t, s_ta)
    lt = stat_t[...]
    plane_wait(stat, s_st)
    ls, cx = stat[:, 0:8], stat[:, 8:16]
    top_t = jnp.max(lt, axis=0)
    top_s = jnp.max(ls, axis=0)
    big_t = top_t + jnp.log(jnp.sum(jnp.exp(lt - top_t[None]), axis=0))
    big_s = top_s + jnp.log(jnp.sum(jnp.exp(ls - top_s[None]), axis=0))
    cross = jnp.sum(jnp.exp(lt - big_t[None]) * cx, axis=0)
    divb[xl] = cross - big_t + big_s
    s_d = block(1)
    push(divb.at[xl], divb.at[xl], s_d, dev(x + 1 - 2 * xl, y, z, core))
    f_t = jnp.exp(mloc[0:8, :] - big_t)
    f_s = jnp.exp(mloc[8:16, :] - big_s)
    weight = (PB * 32 / 64.0) * scale

    grads = []
    for n in range(4):
        for k in range(2):
            r = 2 * n + k
            cols = slice(128 * k, 128 * k + 128)
            diff = ebs[n, :, cols] * f_s[r:r + 1] - ebt[n, :, cols] * f_t[r:r + 1]
            grads.append((diff * weight).astype(BF16))
    grad_scores = jnp.concatenate(grads, axis=1)

    def partial(group, d):
        at = pl.multiple_of(group * 384 + jnp.minimum(d, 2) * TILE, TILE)
        return dot(grad_scores, qbuf[:, :, pl.ds(at, TILE)].reshape(QN, TILE), NN)

    s_g = block(4)
    order = (2, 1, 3, 0)
    for k, step in enumerate(order):
        gsrc[k] = partial(1 - core, (u + 2 + step) % 4)
        push(gsrc.at[k], gsib.at[k], s_g + k, sibling)
    for k, step in enumerate(order):
        gown[k] = partial(core, (u + step) % 4)

    s_1 = block(2)
    s_2 = block(4)

    def half(n):
        return pl.ds(128 * n, 128)

    far_ok = (u + 2) % 4 != 3
    arrive(gsib.at[0], s_g)
    gown[0] = gown[0] + gsib[0]
    for part, to in ((0, right), (1, left)):
        push(gown.at[0, half(part), :], rs1.at[part], s_1 + part, to, far_ok)
    for part, to, step in ((0, right, 1), (1, left, 3)):
        k = 1 + part
        arrive(gsib.at[k], s_g + k)
        gown[k] = gown[k] + gsib[k]
        push(
            gown.at[k, half(1 - part), :], rs2.at[part, half(1 - part), :],
            s_2 + 2 * part, to, (u + step) % 4 != 3,
        )
    arrive(gsib.at[3], s_g + 3)
    gown[3] = gown[3] + gsib[3]
    for part, to, step in ((0, right, 1), (1, left, 3)):
        k = 1 + part
        ok = (u + step) % 4 != 3
        arrive(rs1.at[part], s_1 + part, ok)
        rs2s[part] = gown[k, half(part), :] + rs1[part]
        push(rs2s.at[part], rs2.at[part, half(part), :], s_2 + 2 * part + 1, to, ok)
    for part in range(2):
        arrive(rs2.at[part, half(1 - part), :], s_2 + 2 * part, owner)
        arrive(rs2.at[part, half(part), :], s_2 + 2 * part + 1, owner)
    g = gown[3] + rs2[0] + rs2[1]

    xt = xtb[...].reshape(ROWS, TILE)
    gt = (g.T).reshape(GROUPS, SUB, ROWS) * inv[...]
    g1t, g2t = split2(gt)
    gl[...] = jnp.concatenate([g1t.astype(F32), g2t.astype(F32)], axis=1).astype(BF16)
    ts[...] = jnp.sum(gt * rt[...], axis=1, keepdims=True)
    xlt[...] = jnp.concatenate(
        [xt.astype(F32).T.reshape(GROUPS, SUB, ROWS), jnp.full((GROUPS, SUB, ROWS), 1.0, F32)], axis=1
    ).astype(BF16)
    back = gt.reshape(TILE, ROWS).T
    for n, part in enumerate(split2(back)):
        packs = dot(part, select, NN).astype(BF16)
        for k in range(4):
            gpack[k, :, TILE * n:TILE * n + TILE] = packs[:, TILE * k:TILE * k + TILE]

    s_c = block(16)
    first_c = len(sends)
    sends.extend([None] * 15)

    def piece_copy(n):
        other = (me + 1 + n) % 16
        return pltpu.make_async_remote_copy(
            src_ref=dcs.at[other], dst_ref=dcr.at[me], send_sem=send_sem.at[first_c + n],
            recv_sem=recv_sem.at[s_c + me], device_id=dev(x, other // 4, other % 4, core),
            device_id_type=MESH,
        )

    def grad_step(n, carry):
        i = (me + 1 + n) % 16

        @pl.when(n > 0)
        def _():
            piece_copy(n - 1).start()

        p, j = i // 4, i % 4
        lp = lhs_f[p]
        mask = pack_mask(j)
        diff = dot(
            jnp.concatenate([lp, lp], axis=1),
            gpack[p] * jnp.concatenate([mask, mask], axis=1), NT,
        )
        e1 = a1b[i]
        e2 = a2b[i]
        d1, d2 = split2((e1.astype(F32) + e2.astype(F32)) * (diff - ts[i]))
        ow = dot(gl[i], e1, NT) + dot(gl[i], e2, NT)
        od = dot(xlt[i], d1, NT) + dot(xlt[i], d2, NT)
        code = cb_ref[pl.ds(pl.multiple_of(col + SUB * i, SUB), SUB), :]
        dcs[i] = ow[0:8] + ow[8:16] + od[0:8] - code * od[8:16]
        return carry

    lax.fori_loop(0, GROUPS, grad_step, 0)

    dcr[me] = dcs[me]
    for n in range(15):
        other = (me + 1 + n) % 16
        arrive(dcr.at[other], s_c + other)
    piece[...] = jnp.sum(dcr[...], axis=0)

    s_x = block(4)
    dbuf[me, mine] = piece[...]
    for step in (2, 1, 3):
        push(piece, dbuf.at[me, mine], s_x + 4 - step, dev_x(step), owner)
    for step in (1, 3, 2):
        arrive(dbuf.at[me, r_slot(step)], s_x + step, (u + step) % 4 != 3)

    def trio(s, c):
        return dbuf.at[s, pl.ds(4 * c, 3), :, :]

    s_f = block(16)
    s_fs = block(16)
    for a, b in FAR_FIRST:
        push(trio(me, core), trio(me, core), s_f + ((4 - a) % 4) * 4 + (4 - b) % 4, dev_yz(a, b))
    push(trio(me, core), trio(me, core), s_fs, sibling)
    for a, b in FAR_FIRST[::-1]:
        s = ((y + a) % 4) * 4 + (z + b) % 4
        arrive(trio(s, core), s_f + a * 4 + b)
        push(trio(s, core), trio(s, core), s_fs + a * 4 + b, sibling)
    for a, b in [(0, 0)] + FAR_FIRST[::-1]:
        arrive(trio(((y + a) % 4) * 4 + (z + b) % 4, 1 - core), s_fs + a * 4 + b)
    for t in range(6):
        for p in range(PLANE):
            out_ref[t * TILE + p * SUB:t * TILE + (p + 1) * SUB, :] = dbuf[p, t + (t // 3)]

    arrive(divb.at[1 - xl], s_d)
    for k in range(4):
        for h in range(2):
            div_ref[4 * k + 2 * h:4 * k + 2 * h + 2, :] = divb[h, 2 * k:2 * k + 2, :]

    for n in range(15):
        sends[first_c + n] = (piece_copy(n), None)
    for copy, cond in sends:
        guarded(cond, copy.wait_send)


def local(passages, queries, codebook):
    vmem = pl.BlockSpec(memory_space=pltpu.VMEM)
    grad, divergence = pl.pallas_call(
        kernel,
        out_shape=(
            jax.ShapeDtypeStruct((D, CODES), F32),
            jax.ShapeDtypeStruct((16, 128), F32),
        ),
        in_specs=[vmem] * 3,
        out_specs=(vmem, vmem),
        scratch_shapes=[
            pltpu.VMEM((PLANE, QB, D), BF16),
            pltpu.VMEM((2, PB, D), BF16),
            pltpu.VMEM((8, ROWS, TILE), BF16),
            pltpu.VMEM((2, PB, TILE), BF16),
            pltpu.VMEM((4, PB, TILE), BF16),
            pltpu.VMEM((4, CODES, TILE), BF16),
            pltpu.VMEM((8, 64, CODES), BF16),
            pltpu.VMEM((GROUPS, SUB, ROWS), F32),
            pltpu.VMEM((GROUPS, 1, ROWS), F32),
            pltpu.VMEM((GROUPS, CODES, ROWS), BF16),
            pltpu.VMEM((GROUPS, CODES, ROWS), BF16),
            pltpu.VMEM((4, ROWS, 256), F32),
            pltpu.VMEM((4, ROWS, 256), F32),
            pltpu.VMEM((4, ROWS, 256), F32),
            pltpu.VMEM((16, 128), F32),
            pltpu.VMEM((PLANE, 8, 128), F32),
            pltpu.VMEM((PLANE, 16, 128), F32),
            pltpu.VMEM((4, ROWS, TILE), F32),
            pltpu.VMEM((4, ROWS, TILE), F32),
            pltpu.VMEM((4, ROWS, TILE), F32),
            pltpu.VMEM((2, 128, TILE), F32),
            pltpu.VMEM((2, ROWS, TILE), F32),
            pltpu.VMEM((2, 128, TILE), F32),
            pltpu.VMEM((GROUPS, 16, ROWS), BF16),
            pltpu.VMEM((GROUPS, 1, ROWS), F32),
            pltpu.VMEM((GROUPS, 16, ROWS), BF16),
            pltpu.VMEM((4, ROWS, 2 * TILE), BF16),
            pltpu.VMEM((PLANE, SUB, CODES), F32),
            pltpu.VMEM((PLANE, SUB, CODES), F32),
            pltpu.VMEM((SUB, CODES), F32),
            pltpu.VMEM((PLANE, 8, SUB, CODES), F32),
            pltpu.VMEM((2, 8, 128), F32),
            pltpu.SemaphoreType.DMA((N_SEM,)),
            pltpu.SemaphoreType.DMA((200,)),
        ],
        compiler_params=pltpu.CompilerParams(
            collective_id=0, has_side_effects=True, vmem_limit_bytes=60 * 1024 * 1024
        ),
    )(passages, queries, codebook.reshape(D, CODES))
    return divergence.reshape(2048), grad.reshape(96, SUB, CODES)


def solution(mesh):
    placed = (P("corpus", None), P(("query", "corpus"), None), P())
    return jax.shard_map(
        local, mesh=mesh, in_specs=placed, out_specs=(P("query"), P()), check_vma=False
    )
```

```python
import functools

import jax
import jax.numpy as jnp
from jax import lax
from jax.experimental import pallas as pl
from jax.experimental.pallas import tpu as pltpu
from jax.sharding import PartitionSpec as P

MESH = pl.DeviceIdType.MESH
F32 = jnp.float32
BF16 = jnp.bfloat16
NT = (((1,), (1,)), ((), ()))
NN = (((1,), (0,)), ((), ()))

D = 768
SUB = 8
CODES = 256
QB = 64
PB = 128
PLANE = 16
TILE = 128
GROUPS = 16
ROWS = 256
QN = 1024
BEFORE = 4
N_SEM = 160
FAR_FIRST = [(2, 2), (2, 1), (2, 3), (1, 2), (3, 2), (1, 1), (1, 3), (3, 1), (3, 3), (2, 0), (0, 2), (1, 0), (3, 0), (0, 1), (0, 3)]


def split3(value):
    high = value.astype(BF16)
    rest = value - high.astype(F32)
    mid = rest.astype(BF16)
    low = (rest - mid.astype(F32)).astype(BF16)
    return high, mid, low


def split2(value):
    high = value.astype(BF16)
    low = (value - high.astype(F32)).astype(BF16)
    return high, low


def dot(a, b, dims):
    return lax.dot_general(a, b, dims, preferred_element_type=F32)


def kernel(
    p_ref, q_ref, cb_hbm,
    out_ref, div_ref,
    cb_ref, cb_sem,
    qbuf, pbuf, rbuf,
    xtb, xpack, lhs_f, cp3, rt, inv, a1b, a2b,
    tbuf, ebt, ebs, mloc, stat_t, stat,
    gown, gsib, gsrc, rs1, rs2, rs2s,
    gl, ts, xlt, gpack, dcs, dcr, piece, dbuf, divb,
    send_sem, recv_sem,
):
    qi = lax.axis_index("query")
    ci = lax.axis_index("corpus")
    xh, core = qi // 2, qi % 2
    y, xl, z = ci // 8, (ci // 4) % 2, ci % 4
    x = xh * 2 + xl
    u = (x + 4 - 2 * core) % 4

    def dev(x_, y_, z_, core_):
        return ((x_ // 2) * 2 + core_, y_ * 8 + (x_ % 2) * 4 + z_)

    def dev_x(step, core_=None):
        return dev((x + step) % 4, y, z, core if core_ is None else core_)

    def dev_yz(dy, dz):
        return dev(x, (y + dy) % 4, (z + dz) % 4, core)

    sibling = dev(x, y, z, 1 - core)
    left, right = dev_x(3), dev_x(1)

    sends = []
    count = [0]

    def guarded(cond, action):
        if cond is None:
            action()
        else:
            pl.when(cond)(action)

    def push(src, dst, index, device, cond=None):
        copy = pltpu.make_async_remote_copy(
            src_ref=src, dst_ref=dst, send_sem=send_sem.at[len(sends)],
            recv_sem=recv_sem.at[index], device_id=device, device_id_type=MESH,
        )
        guarded(cond, copy.start)
        sends.append((copy, cond))

    def arrive(dst, index, cond=None):
        guarded(cond, pltpu.make_async_remote_copy(
            src_ref=dst, dst_ref=dst, send_sem=send_sem.at[0],
            recv_sem=recv_sem.at[index], device_id=sibling, device_id_type=MESH,
        ).wait_recv)

    def block(n):
        first = count[0]
        count[0] += n
        return first

    def tile_col(u_):
        return pl.multiple_of((3 * core + jnp.minimum(u_, 2)) * TILE, TILE)

    col = tile_col(u)
    fetch = pltpu.make_async_copy(cb_hbm.at[pl.ds(col, TILE), :], cb_ref, cb_sem)
    fetch.start()

    barrier = pltpu.get_barrier_semaphore()
    peers = [left, right, sibling]
    peers += [dev_yz(a, b) for a, b in ((0, 1), (0, 3), (0, 2), (1, 0), (3, 0), (2, 0))]
    for peer in peers:
        pl.semaphore_signal(barrier, inc=1, device_id=peer, device_id_type=MESH)

    me = y * 4 + z
    qbuf[me] = q_ref[...]
    pbuf[xl] = p_ref[...]

    fetch.wait()
    cb = cb_ref[...]
    grouped = cb.reshape(GROUPS, SUB, CODES)
    bias = -0.5 * jnp.sum(grouped * grouped, axis=1, keepdims=True)
    b_parts = [jnp.broadcast_to(b.astype(F32), grouped.shape) for b in split3(bias)]
    row = lax.broadcasted_iota(jnp.int32, grouped.shape, 1)
    extra = jnp.where(row == 3, 1.0, 0.0)
    for k in range(3):
        extra = jnp.where(row == k, b_parts[k], extra)
    c_parts = [c.astype(F32).reshape(GROUPS, SUB, CODES) for c in split3(cb)]
    packed = jnp.concatenate(c_parts + [extra], axis=1)
    cp3[...] = packed.reshape(8, 64, CODES).astype(BF16)
    for g in range(4):
        lhs_f[g] = packed[4 * g:4 * g + 4].reshape(TILE, CODES).T.astype(BF16)

    lane = lax.broadcasted_iota(jnp.int32, (TILE, 4 * TILE), 1)
    source = lax.broadcasted_iota(jnp.int32, (TILE, 4 * TILE), 0)
    inner_lane = lane % 32
    select = jnp.where(
        (source == (lane // 32) * SUB + lane % SUB) & (inner_lane < 24), 1.0, 0.0
    ).astype(BF16)
    tail_ones = jnp.where(
        (inner_lane[0:1] >= 24) & (inner_lane[0:1] < 27), 1.0, 0.0
    )
    pack_lane = lax.broadcasted_iota(jnp.int32, (1, TILE), 1) // 32

    def pack_mask(j):
        return jnp.where(pack_lane == j, 1.0, 0.0).astype(BF16)

    def pack_rows(h):
        packs = (dot(xtb[h], select, NN) + tail_ones).astype(BF16)
        for g in range(4):
            xpack[g] = packs[:, TILE * g:TILE * g + TILE]

    def assign_step(h):
        lanes = pl.ds(pl.multiple_of(h * 128, 128), 128)

        def step(v, carry):
            g, j = v // 2, 2 * (v % 2)
            xp = xpack[g]
            rhs = jnp.concatenate([xp * pack_mask(j), xp * pack_mask(j + 1)], axis=0)
            logits = dot(lhs_f[g], rhs, NT)
            e1, e2 = split2(jnp.exp(logits - jnp.max(logits, axis=0, keepdims=True)))
            got = dot(cp3[v], e1, NN) + dot(cp3[v], e2, NN)
            for k in range(2):
                i = 2 * v + k
                half_lanes = slice(128 * k, 128 * k + 128)
                a1b[i, :, lanes] = e1[:, half_lanes]
                a2b[i, :, lanes] = e2[:, half_lanes]
                part = got[32 * k:32 * k + 32, half_lanes]
                scale_i = 1.0 / part[27:28]
                inv[i, :, lanes] = scale_i
                rt[i, :, lanes] = (part[0:8] + part[8:16] + part[16:24]) * scale_i
            return carry

        return step

    xtb[xl] = p_ref[:, pl.ds(col, TILE)]
    pack_rows(xl)
    lax.fori_loop(0, BEFORE, assign_step(xl), 0, unroll=2)
    pl.semaphore_wait(barrier, len(peers))

    def gather_plane(own, piece_of, base):
        def rel(h, a, b):
            return (a, b) if h == 0 else (b, a)

        def slot(dy, dz):
            return ((y + dy) % 4) * 4 + (z + dz) % 4

        def sem(dy, dz, h, part):
            return base + (((dy % 4) * 4 + dz % 4) * 2 + h) * 2 + (part or 0)

        def send(h, a, b, part, first_axis, step):
            dy, dz = rel(h, a, b)
            sy, sz = rel(h, step, 0) if first_axis else rel(h, 0, step)
            dst = piece_of(slot(dy, dz), h, part)
            src = own(h) if (a, b) == (0, 0) else dst
            push(src, dst, sem(dy - sy, dz - sz, h, part), dev_yz(sy % 4, sz % 4))

        def wait(h, a, b, part):
            dy, dz = rel(h, a, b)
            arrive(piece_of(slot(dy, dz), h, part), sem(dy, dz, h, part))

        def wave0():
            for h in range(2):
                for step in (1, 3, 2):
                    send(h, 0, 0, None, True, step)
            for h in range(2):
                for step in (1, 3):
                    send(h, 0, 0, None, False, step)

        def wave1():
            for h in range(2):
                for a in (3, 1):
                    wait(h, a, 0, None)
                    send(h, a, 0, None, False, 1)
                    send(h, a, 0, None, False, 3)
            for h in range(2):
                for b, part, step in ((3, 0, 1), (1, 1, 3)):
                    wait(h, 0, b, None)
                    send(h, 0, b, part, False, step)

        def wave2():
            for h in range(2):
                wait(h, 2, 0, None)
                for step in (2, 1, 3):
                    send(h, 2, 0, None, False, step)

        def wave2b():
            for h in range(2):
                for a in (3, 1):
                    for b, part, step in ((3, 0, 1), (1, 1, 3)):
                        wait(h, a, b, None)
                        send(h, a, b, part, False, step)

        def wave3():
            for h in range(2):
                for a in (0, 1, 3):
                    wait(h, a, 2, 0)
                    wait(h, a, 2, 1)
                for b in (1, 3, 2):
                    wait(h, 2, b, None)

        return wave0, wave1, wave2, wave2b, wave3

    def q_piece(s, h, part):
        if part is None:
            return qbuf.at[s, pl.ds(32 * h, 32), :]
        return qbuf.at[s, pl.ds(32 * h + 16 * part, 16), :]

    qw = gather_plane(lambda h: q_ref.at[pl.ds(32 * h, 32), :], q_piece, block(64))
    s_p = block(2)
    x_to = (x + 3 + 2 * core) % 4
    p_to = dev(x_to, y, z, core)
    col_to = tile_col((x_to + 4 - 2 * core) % 4)
    push(p_ref.at[:, pl.ds(col_to, TILE)], xtb.at[xl], s_p, p_to)
    qw[0]()
    push(p_ref, pbuf.at[xl], s_p + 1, p_to)

    lax.fori_loop(BEFORE, 8, assign_step(xl), 0, unroll=2)
    qw[1]()
    arrive(xtb.at[1 - xl], s_p)
    pack_rows(1 - xl)
    lax.fori_loop(0, 4, assign_step(1 - xl), 0, unroll=2)
    qw[2]()
    lax.fori_loop(4, 8, assign_step(1 - xl), 0, unroll=2)

    mine = core * 4 + u
    rbuf[mine] = rt[...].reshape(TILE, ROWS).T.astype(BF16)

    def r_slot(step):
        return core * 4 + (u + step) % 4

    def r_sib(step):
        return (1 - core) * 4 + (u + 2 + step) % 4

    s_r = block(4)
    s_rs = block(4)
    owner = u != 3
    for step in (2, 1, 3):
        push(rbuf.at[mine], rbuf.at[mine], s_r + 4 - step, dev_x(step), owner)
    push(rbuf.at[mine], rbuf.at[mine], s_rs, sibling, owner)
    qw[3]()
    for step in (1, 3, 2):
        s = r_slot(step)
        real = (u + step) % 4 != 3
        arrive(rbuf.at[s], s_r + step, real)
        push(rbuf.at[s], rbuf.at[s], s_rs + step, sibling, real)
    qw[4]()
    arrive(pbuf.at[1 - xl], s_p + 1)

    p_all = pbuf[...].reshape(ROWS, D)
    scale = float(D) ** (-0.5)
    for n in range(4):
        qc = qbuf[4 * n:4 * n + 4].reshape(256, D)
        t = dot(p_all, qc, NT) * scale
        m_t = jnp.max(t, axis=0, keepdims=True)
        tbuf[n] = t
        e_t = jnp.exp(t - m_t)
        ebt[n] = e_t
        lt = m_t + jnp.log(jnp.sum(e_t, axis=0, keepdims=True))
        for k in range(2):
            mloc[2 * n + k:2 * n + k + 1, :] = m_t[:, 128 * k:128 * k + 128]
            stat_t[me, 2 * n + k:2 * n + k + 1, :] = lt[:, 128 * k:128 * k + 128]

    def plane_send(buf, base):
        for a, b in FAR_FIRST:
            push(buf.at[me], buf.at[me], base + ((4 - a) % 4) * 4 + (4 - b) % 4, dev_yz(a, b))

    def plane_wait(buf, base):
        for a, b in FAR_FIRST:
            arrive(buf.at[((y + a) % 4) * 4 + (z + b) % 4], base + a * 4 + b)

    s_ta = block(16)
    plane_send(stat_t, s_ta)
    for step in (0, 1, 3, 2):
        arrive(rbuf.at[r_sib(step)], s_rs + step, (u + 2 + step) % 4 != 3)

    r_all = jnp.concatenate([rbuf[k] for k in (0, 1, 2, 4, 5, 6)], axis=1)
    for n in range(4):
        qc = qbuf[4 * n:4 * n + 4].reshape(256, D)
        s = dot(r_all, qc, NT) * scale
        m_s = jnp.max(s, axis=0, keepdims=True)
        e_s = jnp.exp(s - m_s)
        ebs[n] = e_s
        ls = m_s + jnp.log(jnp.sum(e_s, axis=0, keepdims=True))
        e_t = ebt[n]
        cross = jnp.sum(e_t * (tbuf[n] - s), axis=0, keepdims=True)
        cross = cross / jnp.sum(e_t, axis=0, keepdims=True)
        for k in range(2):
            r = 2 * n + k
            mloc[8 + r:9 + r, :] = m_s[:, 128 * k:128 * k + 128]
            stat[me, r:r + 1, :] = ls[:, 128 * k:128 * k + 128]
            stat[me, 8 + r:9 + r, :] = cross[:, 128 * k:128 * k + 128]

    s_st = block(16)
    plane_send(stat, s_st)
    plane_wait(stat_t, s_ta)
    lt = stat_t[...]
    plane_wait(stat, s_st)
    ls, cx = stat[:, 0:8], stat[:, 8:16]
    top_t = jnp.max(lt, axis=0)
    top_s = jnp.max(ls, axis=0)
    big_t = top_t + jnp.log(jnp.sum(jnp.exp(lt - top_t[None]), axis=0))
    big_s = top_s + jnp.log(jnp.sum(jnp.exp(ls - top_s[None]), axis=0))
    cross = jnp.sum(jnp.exp(lt - big_t[None]) * cx, axis=0)
    divb[xl] = cross - big_t + big_s
    s_d = block(1)
    push(divb.at[xl], divb.at[xl], s_d, dev(x + 1 - 2 * xl, y, z, core))
    f_t = jnp.exp(mloc[0:8, :] - big_t)
    f_s = jnp.exp(mloc[8:16, :] - big_s)
    weight = (PB * 32 / 64.0) * scale

    grads = []
    for n in range(4):
        for k in range(2):
            r = 2 * n + k
            cols = slice(128 * k, 128 * k + 128)
            diff = ebs[n, :, cols] * f_s[r:r + 1] - ebt[n, :, cols] * f_t[r:r + 1]
            grads.append((diff * weight).astype(BF16))
    grad_scores = jnp.concatenate(grads, axis=1)

    def partial(group, d):
        at = pl.multiple_of(group * 384 + jnp.minimum(d, 2) * TILE, TILE)
        return dot(grad_scores, qbuf[:, :, pl.ds(at, TILE)].reshape(QN, TILE), NN)

    s_g = block(4)
    order = (2, 1, 3, 0)
    for k, step in enumerate(order):
        gsrc[k] = partial(1 - core, (u + 2 + step) % 4)
        push(gsrc.at[k], gsib.at[k], s_g + k, sibling)
    for k, step in enumerate(order):
        gown[k] = partial(core, (u + step) % 4)

    s_1 = block(2)
    s_2 = block(4)

    def half(n):
        return pl.ds(128 * n, 128)

    far_ok = (u + 2) % 4 != 3
    arrive(gsib.at[0], s_g)
    gown[0] = gown[0] + gsib[0]
    for part, to in ((0, right), (1, left)):
        push(gown.at[0, half(part), :], rs1.at[part], s_1 + part, to, far_ok)
    for part, to, step in ((0, right, 1), (1, left, 3)):
        k = 1 + part
        arrive(gsib.at[k], s_g + k)
        gown[k] = gown[k] + gsib[k]
        push(
            gown.at[k, half(1 - part), :], rs2.at[part, half(1 - part), :],
            s_2 + 2 * part, to, (u + step) % 4 != 3,
        )
    arrive(gsib.at[3], s_g + 3)
    gown[3] = gown[3] + gsib[3]
    for part, to, step in ((0, right, 1), (1, left, 3)):
        k = 1 + part
        ok = (u + step) % 4 != 3
        arrive(rs1.at[part], s_1 + part, ok)
        rs2s[part] = gown[k, half(part), :] + rs1[part]
        push(rs2s.at[part], rs2.at[part, half(part), :], s_2 + 2 * part + 1, to, ok)
    for part in range(2):
        arrive(rs2.at[part, half(1 - part), :], s_2 + 2 * part, owner)
        arrive(rs2.at[part, half(part), :], s_2 + 2 * part + 1, owner)
    g = gown[3] + rs2[0] + rs2[1]

    xt = xtb[...].reshape(ROWS, TILE)
    gt = (g.T).reshape(GROUPS, SUB, ROWS) * inv[...]
    g1t, g2t = split2(gt)
    gl[...] = jnp.concatenate([g1t.astype(F32), g2t.astype(F32)], axis=1).astype(BF16)
    ts[...] = jnp.sum(gt * rt[...], axis=1, keepdims=True)
    xlt[...] = jnp.concatenate(
        [xt.astype(F32).T.reshape(GROUPS, SUB, ROWS), jnp.full((GROUPS, SUB, ROWS), 1.0, F32)], axis=1
    ).astype(BF16)
    back = gt.reshape(TILE, ROWS).T
    for n, part in enumerate(split2(back)):
        packs = dot(part, select, NN).astype(BF16)
        for k in range(4):
            gpack[k, :, TILE * n:TILE * n + TILE] = packs[:, TILE * k:TILE * k + TILE]

    s_c = block(16)
    first_c = len(sends)
    sends.extend([None] * 15)

    def piece_copy(n):
        other = (me + 1 + n) % 16
        return pltpu.make_async_remote_copy(
            src_ref=dcs.at[other], dst_ref=dcr.at[me], send_sem=send_sem.at[first_c + n],
            recv_sem=recv_sem.at[s_c + me], device_id=dev(x, other // 4, other % 4, core),
            device_id_type=MESH,
        )

    def grad_step(n, carry):
        i = (me + 1 + n) % 16

        @pl.when(n > 0)
        def _():
            piece_copy(n - 1).start()

        p, j = i // 4, i % 4
        lp = lhs_f[p]
        mask = pack_mask(j)
        diff = dot(
            jnp.concatenate([lp, lp], axis=1),
            gpack[p] * jnp.concatenate([mask, mask], axis=1), NT,
        )
        e1 = a1b[i]
        e2 = a2b[i]
        d1, d2 = split2((e1.astype(F32) + e2.astype(F32)) * (diff - ts[i]))
        ow = dot(gl[i], e1, NT) + dot(gl[i], e2, NT)
        od = dot(xlt[i], d1, NT) + dot(xlt[i], d2, NT)
        code = cb_ref[pl.ds(pl.multiple_of(SUB * i, SUB), SUB), :]
        dcs[i] = ow[0:8] + ow[8:16] + od[0:8] - code * od[8:16]
        return carry

    lax.fori_loop(0, GROUPS, grad_step, 0)

    dcr[me] = dcs[me]
    for n in range(15):
        other = (me + 1 + n) % 16
        arrive(dcr.at[other], s_c + other)
    piece[...] = jnp.sum(dcr[...], axis=0)

    s_x = block(4)
    dbuf[me, mine] = piece[...]
    for step in (2, 1, 3):
        push(piece, dbuf.at[me, mine], s_x + 4 - step, dev_x(step), owner)
    for step in (1, 3, 2):
        arrive(dbuf.at[me, r_slot(step)], s_x + step, (u + step) % 4 != 3)

    def trio(s, c):
        return dbuf.at[s, pl.ds(4 * c, 3), :, :]

    s_f = block(16)
    s_fs = block(16)
    for a, b in FAR_FIRST:
        push(trio(me, core), trio(me, core), s_f + ((4 - a) % 4) * 4 + (4 - b) % 4, dev_yz(a, b))
    push(trio(me, core), trio(me, core), s_fs, sibling)
    for a, b in FAR_FIRST[::-1]:
        s = ((y + a) % 4) * 4 + (z + b) % 4
        arrive(trio(s, core), s_f + a * 4 + b)
        push(trio(s, core), trio(s, core), s_fs + a * 4 + b, sibling)
    for a, b in [(0, 0)] + FAR_FIRST[::-1]:
        arrive(trio(((y + a) % 4) * 4 + (z + b) % 4, 1 - core), s_fs + a * 4 + b)
    for t in range(6):
        for p in range(PLANE):
            out_ref[t * TILE + p * SUB:t * TILE + (p + 1) * SUB, :] = dbuf[p, t + (t // 3)]

    arrive(divb.at[1 - xl], s_d)
    for k in range(4):
        for h in range(2):
            div_ref[4 * k + 2 * h:4 * k + 2 * h + 2, :] = divb[h, 2 * k:2 * k + 2, :]

    for n in range(15):
        sends[first_c + n] = (piece_copy(n), None)
    for copy, cond in sends:
        guarded(cond, copy.wait_send)


def local(passages, queries, codebook):
    vmem = pl.BlockSpec(memory_space=pltpu.VMEM)
    grad, divergence = pl.pallas_call(
        kernel,
        out_shape=(
            pltpu.VMEM((D, CODES), F32),
            pltpu.VMEM((16, 128), F32),
        ),
        in_specs=[vmem, vmem, pl.BlockSpec(memory_space=pl.ANY)],
        out_specs=(vmem, vmem),
        scratch_shapes=[
            pltpu.VMEM((TILE, CODES), F32),
            pltpu.SemaphoreType.DMA,
            pltpu.VMEM((PLANE, QB, D), BF16),
            pltpu.VMEM((2, PB, D), BF16),
            pltpu.VMEM((8, ROWS, TILE), BF16),
            pltpu.VMEM((2, PB, TILE), BF16),
            pltpu.VMEM((4, PB, TILE), BF16),
            pltpu.VMEM((4, CODES, TILE), BF16),
            pltpu.VMEM((8, 64, CODES), BF16),
            pltpu.VMEM((GROUPS, SUB, ROWS), F32),
            pltpu.VMEM((GROUPS, 1, ROWS), F32),
            pltpu.VMEM((GROUPS, CODES, ROWS), BF16),
            pltpu.VMEM((GROUPS, CODES, ROWS), BF16),
            pltpu.VMEM((4, ROWS, 256), F32),
            pltpu.VMEM((4, ROWS, 256), F32),
            pltpu.VMEM((4, ROWS, 256), F32),
            pltpu.VMEM((16, 128), F32),
            pltpu.VMEM((PLANE, 8, 128), F32),
            pltpu.VMEM((PLANE, 16, 128), F32),
            pltpu.VMEM((4, ROWS, TILE), F32),
            pltpu.VMEM((4, ROWS, TILE), F32),
            pltpu.VMEM((4, ROWS, TILE), F32),
            pltpu.VMEM((2, 128, TILE), F32),
            pltpu.VMEM((2, ROWS, TILE), F32),
            pltpu.VMEM((2, 128, TILE), F32),
            pltpu.VMEM((GROUPS, 16, ROWS), BF16),
            pltpu.VMEM((GROUPS, 1, ROWS), F32),
            pltpu.VMEM((GROUPS, 16, ROWS), BF16),
            pltpu.VMEM((4, ROWS, 2 * TILE), BF16),
            pltpu.VMEM((PLANE, SUB, CODES), F32),
            pltpu.VMEM((PLANE, SUB, CODES), F32),
            pltpu.VMEM((SUB, CODES), F32),
            pltpu.VMEM((PLANE, 8, SUB, CODES), F32),
            pltpu.VMEM((2, 8, 128), F32),
            pltpu.SemaphoreType.DMA((N_SEM,)),
            pltpu.SemaphoreType.DMA((200,)),
        ],
        compiler_params=pltpu.CompilerParams(
            collective_id=0, has_side_effects=True, vmem_limit_bytes=60 * 1024 * 1024
        ),
    )(passages, queries, codebook.reshape(D, CODES))
    return divergence.reshape(2048), grad.reshape(96, SUB, CODES)


def solution(mesh):
    placed = (P("corpus", None), P(("query", "corpus"), None), P())
    return jax.shard_map(
        local, mesh=mesh, in_specs=placed, out_specs=(P("query"), P()), check_vma=False
    )
```

```python
import functools

import jax
import jax.numpy as jnp
from jax import lax
from jax.experimental import pallas as pl
from jax.experimental.pallas import tpu as pltpu
from jax.sharding import PartitionSpec as P

MESH = pl.DeviceIdType.MESH
F32 = jnp.float32
BF16 = jnp.bfloat16
NT = (((1,), (1,)), ((), ()))
NN = (((1,), (0,)), ((), ()))

D = 768
SUB = 8
CODES = 256
QB = 64
PB = 128
PLANE = 16
TILE = 128
GROUPS = 16
ROWS = 256
QN = 1024
BEFORE = 4
N_SEM = 224
LOG2E = 1.4426950408889634
FAR_FIRST = [(2, 2), (2, 1), (2, 3), (1, 2), (3, 2), (1, 1), (1, 3), (3, 1), (3, 3), (2, 0), (0, 2), (1, 0), (3, 0), (0, 1), (0, 3)]


def split3(value):
    high = value.astype(BF16)
    rest = value - high.astype(F32)
    mid = rest.astype(BF16)
    low = (rest - mid.astype(F32)).astype(BF16)
    return high, mid, low


def split2(value):
    high = value.astype(BF16)
    low = (value - high.astype(F32)).astype(BF16)
    return high, low


def dot(a, b, dims):
    return lax.dot_general(a, b, dims, preferred_element_type=F32)


def kernel(
    p_ref, q_ref, cb_hbm,
    out_ref, div_ref,
    cb_ref, cb_sem,
    qbuf, pbuf, rbuf,
    xtb, xpack, lhs_f, cp3, rt, inv, a1b, a2b,
    tbuf, ebt, ebs, mloc, stat_t, stat,
    gown, gsib, gsrc, rs1, rs2, rs2s,
    gl, ts, xlt, gpack, dcs, dcr, divb,
    send_sem, recv_sem,
):
    qi = lax.axis_index("query")
    ci = lax.axis_index("corpus")
    xh, core = qi // 2, qi % 2
    y, xl, z = ci // 8, (ci // 4) % 2, ci % 4
    x = xh * 2 + xl
    u = (x + 4 - 2 * core) % 4

    def dev(x_, y_, z_, core_):
        return ((x_ // 2) * 2 + core_, y_ * 8 + (x_ % 2) * 4 + z_)

    def dev_x(step, core_=None):
        return dev((x + step) % 4, y, z, core if core_ is None else core_)

    def dev_yz(dy, dz):
        return dev(x, (y + dy) % 4, (z + dz) % 4, core)

    sibling = dev(x, y, z, 1 - core)
    left, right = dev_x(3), dev_x(1)

    sends = []
    count = [0]

    def guarded(cond, action):
        if cond is None:
            action()
        else:
            pl.when(cond)(action)

    def push(src, dst, index, device, cond=None):
        copy = pltpu.make_async_remote_copy(
            src_ref=src, dst_ref=dst, send_sem=send_sem.at[len(sends)],
            recv_sem=recv_sem.at[index], device_id=device, device_id_type=MESH,
        )
        guarded(cond, copy.start)
        sends.append((copy, cond))

    def arrive(dst, index, cond=None):
        guarded(cond, pltpu.make_async_remote_copy(
            src_ref=dst, dst_ref=dst, send_sem=send_sem.at[0],
            recv_sem=recv_sem.at[index], device_id=sibling, device_id_type=MESH,
        ).wait_recv)

    def block(n):
        first = count[0]
        count[0] += n
        return first

    def tile_col(u_):
        return pl.multiple_of((3 * core + jnp.minimum(u_, 2)) * TILE, TILE)

    col = tile_col(u)
    fetch = pltpu.make_async_copy(cb_hbm.at[pl.ds(col, TILE), :], cb_ref, cb_sem)
    fetch.start()

    barrier = pltpu.get_barrier_semaphore()
    peers = [left, right, sibling]
    peers += [dev_yz(a, b) for a, b in ((0, 1), (0, 3), (0, 2), (1, 0), (3, 0), (2, 0))]
    for peer in peers:
        pl.semaphore_signal(barrier, inc=1, device_id=peer, device_id_type=MESH)

    me = y * 4 + z
    qbuf[me] = q_ref[...]
    pbuf[xl] = p_ref[...]

    fetch.wait()
    cb = cb_ref[...]
    grouped = cb.reshape(GROUPS, SUB, CODES)
    bias = -0.5 * jnp.sum(grouped * grouped, axis=1, keepdims=True)
    b_parts = [jnp.broadcast_to(b.astype(F32), grouped.shape) for b in split3(bias)]
    row = lax.broadcasted_iota(jnp.int32, grouped.shape, 1)
    extra = jnp.where(row == 3, 1.0, 0.0)
    for k in range(3):
        extra = jnp.where(row == k, b_parts[k], extra)
    c_parts = [c.astype(F32).reshape(GROUPS, SUB, CODES) for c in split3(cb)]
    packed = jnp.concatenate(c_parts + [extra], axis=1)
    cp3[...] = packed.reshape(8, 64, CODES).astype(BF16)
    for g in range(4):
        lhs_f[g] = packed[4 * g:4 * g + 4].reshape(TILE, CODES).T.astype(BF16)

    lane = lax.broadcasted_iota(jnp.int32, (TILE, 4 * TILE), 1)
    source = lax.broadcasted_iota(jnp.int32, (TILE, 4 * TILE), 0)
    inner_lane = lane % 32
    select = jnp.where(
        (source == (lane // 32) * SUB + lane % SUB) & (inner_lane < 24), 1.0, 0.0
    ).astype(BF16)
    tail_ones = jnp.where(
        (inner_lane[0:1] >= 24) & (inner_lane[0:1] < 27), 1.0, 0.0
    )
    pack_lane = lax.broadcasted_iota(jnp.int32, (1, TILE), 1) // 32

    def pack_mask(j):
        return jnp.where(pack_lane == j, 1.0, 0.0).astype(BF16)

    def pack_rows(h):
        packs = (dot(xtb[h], select, NN) + tail_ones).astype(BF16)
        for g in range(4):
            xpack[g] = packs[:, TILE * g:TILE * g + TILE]

    def assign_step(h):
        lanes = pl.ds(pl.multiple_of(h * 128, 128), 128)

        def step(v, carry):
            g, j = v // 2, 2 * (v % 2)
            xp = xpack[g]
            rhs = jnp.concatenate([xp * pack_mask(j), xp * pack_mask(j + 1)], axis=0)
            logits = dot(lhs_f[g], rhs, NT)
            e1, e2 = split2(jnp.exp(logits - jnp.max(logits, axis=0, keepdims=True)))
            got = dot(cp3[v], e1, NN) + dot(cp3[v], e2, NN)
            for k in range(2):
                i = 2 * v + k
                half_lanes = slice(128 * k, 128 * k + 128)
                a1b[i, :, lanes] = e1[:, half_lanes]
                a2b[i, :, lanes] = e2[:, half_lanes]
                part = got[32 * k:32 * k + 32, half_lanes]
                scale_i = 1.0 / part[27:28]
                inv[i, :, lanes] = scale_i
                rt[i, :, lanes] = (part[0:8] + part[8:16] + part[16:24]) * scale_i
            return carry

        return step

    xtb[xl] = p_ref[:, pl.ds(col, TILE)]
    pack_rows(xl)
    lax.fori_loop(0, BEFORE, assign_step(xl), 0, unroll=2)
    pl.semaphore_wait(barrier, len(peers))

    def gather_plane(own, piece_of, base):
        def rel(h, a, b):
            return (a, b) if h == 0 else (b, a)

        def slot(dy, dz):
            return ((y + dy) % 4) * 4 + (z + dz) % 4

        def sem(dy, dz, h, part):
            return base + (((dy % 4) * 4 + dz % 4) * 2 + h) * 2 + (part or 0)

        def send(h, a, b, part, first_axis, step):
            dy, dz = rel(h, a, b)
            sy, sz = rel(h, step, 0) if first_axis else rel(h, 0, step)
            dst = piece_of(slot(dy, dz), h, part)
            src = own(h) if (a, b) == (0, 0) else dst
            push(src, dst, sem(dy - sy, dz - sz, h, part), dev_yz(sy % 4, sz % 4))

        def wait(h, a, b, part):
            dy, dz = rel(h, a, b)
            arrive(piece_of(slot(dy, dz), h, part), sem(dy, dz, h, part))

        def wave0():
            for h in range(2):
                for step in (1, 3, 2):
                    send(h, 0, 0, None, True, step)
            for h in range(2):
                for step in (1, 3):
                    send(h, 0, 0, None, False, step)

        def wave1():
            for h in range(2):
                for a in (3, 1):
                    wait(h, a, 0, None)
                    send(h, a, 0, None, False, 1)
                    send(h, a, 0, None, False, 3)
            for h in range(2):
                for b, part, step in ((3, 0, 1), (1, 1, 3)):
                    wait(h, 0, b, None)
                    send(h, 0, b, part, False, step)

        def wave2():
            for h in range(2):
                wait(h, 2, 0, None)
                for step in (2, 1, 3):
                    send(h, 2, 0, None, False, step)

        def wave2b():
            for h in range(2):
                for a in (3, 1):
                    for b, part, step in ((3, 0, 1), (1, 1, 3)):
                        wait(h, a, b, None)
                        send(h, a, b, part, False, step)

        def wave3():
            for h in range(2):
                for a in (0, 1, 3):
                    wait(h, a, 2, 0)
                    wait(h, a, 2, 1)
                for b in (1, 3, 2):
                    wait(h, 2, b, None)

        return wave0, wave1, wave2, wave2b, wave3

    def q_piece(s, h, part):
        if part is None:
            return qbuf.at[s, pl.ds(32 * h, 32), :]
        return qbuf.at[s, pl.ds(32 * h + 16 * part, 16), :]

    qw = gather_plane(lambda h: q_ref.at[pl.ds(32 * h, 32), :], q_piece, block(64))
    s_p = block(2)
    x_to = (x + 3 + 2 * core) % 4
    p_to = dev(x_to, y, z, core)
    col_to = tile_col((x_to + 4 - 2 * core) % 4)
    push(p_ref.at[:, pl.ds(col_to, TILE)], xtb.at[xl], s_p, p_to)
    qw[0]()
    push(p_ref, pbuf.at[xl], s_p + 1, p_to)

    lax.fori_loop(BEFORE, 8, assign_step(xl), 0, unroll=2)
    qw[1]()
    arrive(xtb.at[1 - xl], s_p)
    pack_rows(1 - xl)
    lax.fori_loop(0, 4, assign_step(1 - xl), 0, unroll=2)
    qw[2]()
    lax.fori_loop(4, 8, assign_step(1 - xl), 0, unroll=2)

    mine = core * 4 + u
    rbuf[mine] = rt[...].reshape(TILE, ROWS).T.astype(BF16)

    def r_slot(step):
        return core * 4 + (u + step) % 4

    def r_sib(step):
        return (1 - core) * 4 + (u + 2 + step) % 4

    s_r = block(4)
    s_rs = block(4)
    owner = u != 3
    for step in (2, 1, 3):
        push(rbuf.at[mine], rbuf.at[mine], s_r + 4 - step, dev_x(step), owner)
    push(rbuf.at[mine], rbuf.at[mine], s_rs, sibling, owner)
    qw[3]()
    for step in (1, 3, 2):
        s = r_slot(step)
        real = (u + step) % 4 != 3
        arrive(rbuf.at[s], s_r + step, real)
        push(rbuf.at[s], rbuf.at[s], s_rs + step, sibling, real)
    qw[4]()
    arrive(pbuf.at[1 - xl], s_p + 1)

    p_all = pbuf[...].reshape(ROWS, D)
    scale = float(D) ** (-0.5)
    scale2 = scale * LOG2E
    sum_t = []
    for n in range(4):
        qc = qbuf[4 * n:4 * n + 4].reshape(256, D)
        t = dot(p_all, qc, NT)
        m_t = jnp.max(t, axis=0, keepdims=True)
        tbuf[n] = t
        e_t = jnp.exp2((t - m_t) * scale2)
        ebt[n] = e_t
        s_t = jnp.sum(e_t, axis=0, keepdims=True)
        m_t = m_t * scale
        lt = m_t + jnp.log(s_t)
        sum_t.append(s_t)
        for k in range(2):
            mloc[2 * n + k:2 * n + k + 1, :] = m_t[:, 128 * k:128 * k + 128]
            stat_t[me, 2 * n + k:2 * n + k + 1, :] = lt[:, 128 * k:128 * k + 128]

    def plane_send(buf, base):
        for a, b in FAR_FIRST:
            push(buf.at[me], buf.at[me], base + ((4 - a) % 4) * 4 + (4 - b) % 4, dev_yz(a, b))

    def plane_wait(buf, base):
        for a, b in FAR_FIRST:
            arrive(buf.at[((y + a) % 4) * 4 + (z + b) % 4], base + a * 4 + b)

    s_ta = block(16)
    plane_send(stat_t, s_ta)
    for step in (0, 1, 3, 2):
        arrive(rbuf.at[r_sib(step)], s_rs + step, (u + 2 + step) % 4 != 3)

    r_all = jnp.concatenate([rbuf[k] for k in (0, 1, 2, 4, 5, 6)], axis=1)
    for n in range(4):
        qc = qbuf[4 * n:4 * n + 4].reshape(256, D)
        s = dot(r_all, qc, NT)
        m_s = jnp.max(s, axis=0, keepdims=True)
        e_s = jnp.exp2((s - m_s) * scale2)
        ebs[n] = e_s
        m_s = m_s * scale
        ls = m_s + jnp.log(jnp.sum(e_s, axis=0, keepdims=True))
        cross = jnp.sum(ebt[n] * (tbuf[n] - s), axis=0, keepdims=True) * scale / sum_t[n]
        for k in range(2):
            r = 2 * n + k
            mloc[8 + r:9 + r, :] = m_s[:, 128 * k:128 * k + 128]
            stat[me, r:r + 1, :] = ls[:, 128 * k:128 * k + 128]
            stat[me, 8 + r:9 + r, :] = cross[:, 128 * k:128 * k + 128]

    s_st = block(16)
    plane_send(stat, s_st)
    plane_wait(stat_t, s_ta)
    lt = stat_t[...]
    plane_wait(stat, s_st)
    ls, cx = stat[:, 0:8], stat[:, 8:16]
    top_t = jnp.max(lt, axis=0)
    top_s = jnp.max(ls, axis=0)
    big_t = top_t + jnp.log(jnp.sum(jnp.exp(lt - top_t[None]), axis=0))
    big_s = top_s + jnp.log(jnp.sum(jnp.exp(ls - top_s[None]), axis=0))
    cross = jnp.sum(jnp.exp(lt - big_t[None]) * cx, axis=0)
    divb[xl] = cross - big_t + big_s
    s_d = block(1)
    push(divb.at[xl], divb.at[xl], s_d, dev(x + 1 - 2 * xl, y, z, core))
    weight = (PB * 32 / 64.0) * scale
    f_t = jnp.exp(mloc[0:8, :] - big_t) * weight
    f_s = jnp.exp(mloc[8:16, :] - big_s) * weight

    grads = []
    for n in range(4):
        for k in range(2):
            r = 2 * n + k
            cols = slice(128 * k, 128 * k + 128)
            diff = ebs[n, :, cols] * f_s[r:r + 1] - ebt[n, :, cols] * f_t[r:r + 1]
            grads.append(diff.astype(BF16))
    grad_scores = jnp.concatenate(grads, axis=1)

    def partial(group, first, tiles):
        at = pl.multiple_of(group * 384 + first * TILE, TILE)
        return dot(grad_scores, qbuf[:, :, pl.ds(at, TILE * tiles)].reshape(QN, TILE * tiles), NN)

    s_g = block(3)
    for group, dest in ((1 - core, gsrc), (core, gown)):
        two = partial(group, 0, 2)
        dest[0] = two[:, :TILE]
        dest[1] = two[:, TILE:]
        if dest is gsrc:
            push(gsrc.at[0], gsib.at[0], s_g, sibling)
            push(gsrc.at[1], gsib.at[1], s_g + 1, sibling)
        dest[2] = partial(group, 2, 1)
        if dest is gsrc:
            push(gsrc.at[2], gsib.at[2], s_g + 2, sibling)

    s_1 = block(2)
    s_2 = block(4)

    def half(n):
        return pl.ds(128 * n, 128)

    def near(step):
        return jnp.minimum((u + step) % 4, 2)

    for k in range(3):
        arrive(gsib.at[k], s_g + k)
        gown[k] = gown[k] + gsib[k]
    for part, to in ((0, right), (1, left)):
        push(gown.at[near(2), half(part), :], rs1.at[part], s_1 + part, to, (u + 2) % 4 != 3)
    for part, to, step in ((0, right, 1), (1, left, 3)):
        push(
            gown.at[near(step), half(1 - part), :], rs2.at[part, half(1 - part), :],
            s_2 + 2 * part, to, (u + step) % 4 != 3,
        )
    for part, to, step in ((0, right, 1), (1, left, 3)):
        ok = (u + step) % 4 != 3
        arrive(rs1.at[part], s_1 + part, ok)
        rs2s[part] = gown[near(step), half(part), :] + rs1[part]
        push(rs2s.at[part], rs2.at[part, half(part), :], s_2 + 2 * part + 1, to, ok)
    for part in range(2):
        arrive(rs2.at[part, half(1 - part), :], s_2 + 2 * part, owner)
        arrive(rs2.at[part, half(part), :], s_2 + 2 * part + 1, owner)
    g = gown[near(0)] + rs2[0] + rs2[1]

    xt = xtb[...].reshape(ROWS, TILE)
    gt = (g.T).reshape(GROUPS, SUB, ROWS) * inv[...]
    g1t, g2t = split2(gt)
    gl[...] = jnp.concatenate([g1t.astype(F32), g2t.astype(F32)], axis=1).astype(BF16)
    ts[...] = jnp.sum(gt * rt[...], axis=1, keepdims=True)
    xlt[...] = jnp.concatenate(
        [xt.astype(F32).T.reshape(GROUPS, SUB, ROWS), jnp.full((GROUPS, SUB, ROWS), 1.0, F32)], axis=1
    ).astype(BF16)
    back = gt.reshape(TILE, ROWS).T
    for n, part in enumerate(split2(back)):
        packs = dot(part, select, NN).astype(BF16)
        for k in range(4):
            gpack[k, :, TILE * n:TILE * n + TILE] = packs[:, TILE * k:TILE * k + TILE]

    s_c = block(64)
    first_c = len(sends)
    sends.extend([None] * 63)

    def piece_copy(n, step):
        other = (me + 1 + n) % 16
        return pltpu.make_async_remote_copy(
            src_ref=dcs.at[other], dst_ref=dcr.at[u, me],
            send_sem=send_sem.at[first_c + 4 * n + step - jnp.where(n == 15, 1, 0)],
            recv_sem=recv_sem.at[s_c + 16 * u + me],
            device_id=dev((x + step) % 4, other // 4, other % 4, core), device_id_type=MESH,
        )

    def grad_step(n, carry):
        i = (me + 1 + n) % 16

        @pl.when((n > 0) & owner)
        def _():
            for step in range(4):
                piece_copy(n - 1, step).start()

        p, j = i // 4, i % 4
        lp = lhs_f[p]
        mask = pack_mask(j)
        diff = dot(
            jnp.concatenate([lp, lp], axis=1),
            gpack[p] * jnp.concatenate([mask, mask], axis=1), NT,
        )
        e1 = a1b[i]
        e2 = a2b[i]
        d1, d2 = split2((e1.astype(F32) + e2.astype(F32)) * (diff - ts[i]))
        ow = dot(gl[i], e1, NT) + dot(gl[i], e2, NT)
        od = dot(xlt[i], d1, NT) + dot(xlt[i], d2, NT)
        code = cb_ref[pl.ds(pl.multiple_of(SUB * i, SUB), SUB), :]
        dcs[i] = ow[0:8] + ow[8:16] + od[0:8] - code * od[8:16]
        return carry

    lax.fori_loop(0, GROUPS, grad_step, 0)

    for step in (2, 1, 3):
        guarded(owner, piece_copy(15, step).start)
    dcr[u, me] = dcs[me]
    for k in range(3):
        arrive(dcr.at[k, me], s_c + 16 * k + me, u != k)

    def piece_wait(n, carry):
        other = (me + n) % 16
        for k in range(3):
            arrive(dcr.at[k, other], s_c + 16 * k + other)
        return carry

    lax.fori_loop(1, 16, piece_wait, 0)

    for k in range(3):
        out_ref[3 * core + k, me] = jnp.sum(dcr[k], axis=0)

    def trio(s, c):
        return out_ref.at[pl.ds(3 * c, 3), s]

    s_f = block(16)
    s_fs = block(16)
    for a, b in FAR_FIRST:
        push(trio(me, core), trio(me, core), s_f + ((4 - a) % 4) * 4 + (4 - b) % 4, dev_yz(a, b))
    push(trio(me, core), trio(me, core), s_fs, sibling)
    for a, b in FAR_FIRST[::-1]:
        s = ((y + a) % 4) * 4 + (z + b) % 4
        arrive(trio(s, core), s_f + a * 4 + b)
        push(trio(s, core), trio(s, core), s_fs + a * 4 + b, sibling)
    for a, b in [(0, 0)] + FAR_FIRST[::-1]:
        arrive(trio(((y + a) % 4) * 4 + (z + b) % 4, 1 - core), s_fs + a * 4 + b)

    arrive(divb.at[1 - xl], s_d)
    for k in range(4):
        for h in range(2):
            div_ref[4 * k + 2 * h:4 * k + 2 * h + 2, :] = divb[h, 2 * k:2 * k + 2, :]

    def piece_sent(n, carry):
        for step in range(4):
            piece_copy(n, step).wait_send()
        return carry

    @pl.when(owner)
    def _():
        lax.fori_loop(0, 15, piece_sent, 0)
        for step in (2, 1, 3):
            piece_copy(15, step).wait_send()

    for entry in sends:
        if entry is not None:
            guarded(entry[1], entry[0].wait_send)


def local(passages, queries, codebook):
    vmem = pl.BlockSpec(memory_space=pltpu.VMEM)
    grad, divergence = pl.pallas_call(
        kernel,
        out_shape=(
            pltpu.VMEM((6, PLANE, SUB, CODES), F32),
            pltpu.VMEM((16, 128), F32),
        ),
        in_specs=[vmem, vmem, pl.BlockSpec(memory_space=pl.ANY)],
        out_specs=(vmem, vmem),
        scratch_shapes=[
            pltpu.VMEM((TILE, CODES), F32),
            pltpu.SemaphoreType.DMA,
            pltpu.VMEM((PLANE, QB, D), BF16),
            pltpu.VMEM((2, PB, D), BF16),
            pltpu.VMEM((8, ROWS, TILE), BF16),
            pltpu.VMEM((2, PB, TILE), BF16),
            pltpu.VMEM((4, PB, TILE), BF16),
            pltpu.VMEM((4, CODES, TILE), BF16),
            pltpu.VMEM((8, 64, CODES), BF16),
            pltpu.VMEM((GROUPS, SUB, ROWS), F32),
            pltpu.VMEM((GROUPS, 1, ROWS), F32),
            pltpu.VMEM((GROUPS, CODES, ROWS), BF16),
            pltpu.VMEM((GROUPS, CODES, ROWS), BF16),
            pltpu.VMEM((4, ROWS, 256), F32),
            pltpu.VMEM((4, ROWS, 256), F32),
            pltpu.VMEM((4, ROWS, 256), F32),
            pltpu.VMEM((16, 128), F32),
            pltpu.VMEM((PLANE, 8, 128), F32),
            pltpu.VMEM((PLANE, 16, 128), F32),
            pltpu.VMEM((3, ROWS, TILE), F32),
            pltpu.VMEM((3, ROWS, TILE), F32),
            pltpu.VMEM((3, ROWS, TILE), F32),
            pltpu.VMEM((2, 128, TILE), F32),
            pltpu.VMEM((2, ROWS, TILE), F32),
            pltpu.VMEM((2, 128, TILE), F32),
            pltpu.VMEM((GROUPS, 16, ROWS), BF16),
            pltpu.VMEM((GROUPS, 1, ROWS), F32),
            pltpu.VMEM((GROUPS, 16, ROWS), BF16),
            pltpu.VMEM((4, ROWS, 2 * TILE), BF16),
            pltpu.VMEM((PLANE, SUB, CODES), F32),
            pltpu.VMEM((4, PLANE, SUB, CODES), F32),
            pltpu.VMEM((2, 8, 128), F32),
            pltpu.SemaphoreType.DMA((N_SEM,)),
            pltpu.SemaphoreType.DMA((240,)),
        ],
        compiler_params=pltpu.CompilerParams(
            collective_id=0, has_side_effects=True, vmem_limit_bytes=60 * 1024 * 1024
        ),
    )(passages, queries, codebook.reshape(D, CODES))
    return divergence.reshape(2048), grad.reshape(96, SUB, CODES)


def solution(mesh):
    placed = (P("corpus", None), P(("query", "corpus"), None), P())
    return jax.shard_map(
        local, mesh=mesh, in_specs=placed, out_specs=(P("query"), P()), check_vma=False
    )
```

```python
import functools

import jax
import jax.numpy as jnp
from jax import lax
from jax.experimental import pallas as pl
from jax.experimental.pallas import tpu as pltpu
from jax.sharding import PartitionSpec as P

MESH = pl.DeviceIdType.MESH
F32 = jnp.float32
BF16 = jnp.bfloat16
NT = (((1,), (1,)), ((), ()))
NN = (((1,), (0,)), ((), ()))

D = 768
SUB = 8
CODES = 256
QB = 64
PB = 128
PLANE = 16
TILE = 128
GROUPS = 16
ROWS = 256
QN = 1024
BEFORE = 4
UNROLL = 1
N_SEM = 224
LOG2E = 1.4426950408889634
FAR_FIRST = [(2, 2), (2, 1), (2, 3), (1, 2), (3, 2), (1, 1), (1, 3), (3, 1), (3, 3), (2, 0), (0, 2), (1, 0), (3, 0), (0, 1), (0, 3)]


def rem(a, b):
    return a % b if isinstance(a, int) else lax.rem(a, b)


def quo(a, b):
    return a // b if isinstance(a, int) else lax.div(a, b)


def split3(value):
    high = value.astype(BF16)
    rest = value - high.astype(F32)
    mid = rest.astype(BF16)
    low = (rest - mid.astype(F32)).astype(BF16)
    return high, mid, low


def split2(value):
    high = value.astype(BF16)
    low = (value - high.astype(F32)).astype(BF16)
    return high, low


def dot(a, b, dims):
    return lax.dot_general(a, b, dims, preferred_element_type=F32)


def kernel(
    p_ref, q_ref, cb_hbm,
    out_ref, div_ref,
    cb_ref, cb_sem,
    qbuf, pbuf, rbuf,
    xtb, raw, xpack, lhs_f, lhs_b, cp3, rt, inv, a1b, a2b,
    tbuf, ebt, ebs, sumt, mloc, stat_t, stat,
    gown, gsib, gsrc, rs1, rs2, rs2s,
    gl, dbuf, xlt, gpack, dcs, dcr, divb,
    send_sem, recv_sem,
):
    qi = lax.axis_index("query")
    ci = lax.axis_index("corpus")
    xh, core = quo(qi, 2), rem(qi, 2)
    y, xl, z = quo(ci, 8), rem(quo(ci, 4), 2), rem(ci, 4)
    x = xh * 2 + xl
    u = rem(x + 4 - 2 * core, 4)

    def dev(x_, y_, z_, core_):
        return (quo(x_, 2) * 2 + core_, y_ * 8 + rem(x_, 2) * 4 + z_)

    def dev_x(step, core_=None):
        return dev(rem(x + step, 4), y, z, core if core_ is None else core_)

    def dev_yz(dy, dz):
        return dev(x, rem(y + dy, 4), rem(z + dz, 4), core)

    sibling = dev(x, y, z, 1 - core)
    left, right = dev_x(3), dev_x(1)

    sends = []
    count = [0]

    def guarded(cond, action):
        if cond is None:
            action()
        else:
            pl.when(cond)(action)

    def push(src, dst, index, device, cond=None):
        copy = pltpu.make_async_remote_copy(
            src_ref=src, dst_ref=dst, send_sem=send_sem.at[len(sends)],
            recv_sem=recv_sem.at[index], device_id=device, device_id_type=MESH,
        )
        guarded(cond, copy.start)
        sends.append((copy, cond))

    def arrive(dst, index, cond=None):
        guarded(cond, pltpu.make_async_remote_copy(
            src_ref=dst, dst_ref=dst, send_sem=send_sem.at[0],
            recv_sem=recv_sem.at[index], device_id=sibling, device_id_type=MESH,
        ).wait_recv)

    def block(n):
        first = count[0]
        count[0] += n
        return first

    def tile_col(u_):
        return pl.multiple_of((3 * core + jnp.minimum(u_, 2)) * TILE, TILE)

    col = tile_col(u)
    fetch = pltpu.make_async_copy(cb_hbm.at[pl.ds(col, TILE), :], cb_ref, cb_sem)
    fetch.start()

    barrier = pltpu.get_barrier_semaphore()
    peers = [left, right, sibling]
    peers += [dev_yz(a, b) for a, b in ((0, 1), (0, 3), (0, 2), (1, 0), (3, 0), (2, 0))]
    for peer in peers:
        pl.semaphore_signal(barrier, inc=1, device_id=peer, device_id_type=MESH)

    me = y * 4 + z
    qbuf[me] = q_ref[...]
    pbuf[xl] = p_ref[...]

    fetch.wait()
    cb = cb_ref[...]
    grouped = cb.reshape(GROUPS, SUB, CODES)
    bias = -0.5 * jnp.sum(grouped * grouped, axis=1, keepdims=True)
    b_parts = [jnp.broadcast_to(b.astype(F32), grouped.shape) for b in split3(bias)]
    row = lax.broadcasted_iota(jnp.int32, grouped.shape, 1)
    extra = jnp.where(row == 3, 1.0, 0.0)
    for k in range(3):
        extra = jnp.where(row == k, b_parts[k], extra)
    c_parts = [c.astype(F32).reshape(GROUPS, SUB, CODES) for c in split3(cb)]
    packed = jnp.concatenate(c_parts + [extra], axis=1)
    cp3[...] = packed.reshape(8, 64, CODES).astype(BF16)
    ones3 = jnp.where(row < 3, 1.0, 0.0)
    packed_b = jnp.concatenate([c_parts[0], c_parts[1], c_parts[0], ones3], axis=1)
    for g in range(4):
        lhs_f[g] = packed[4 * g:4 * g + 4].reshape(TILE, CODES).T.astype(BF16)
        lhs_b[g] = packed_b[4 * g:4 * g + 4].reshape(TILE, CODES).T.astype(BF16)

    lane = lax.broadcasted_iota(jnp.int32, (TILE, 4 * TILE), 1)
    source = lax.broadcasted_iota(jnp.int32, (TILE, 4 * TILE), 0)
    inner_lane = lane % 32
    select = jnp.where(
        (source == (lane // 32) * SUB + lane % SUB) & (inner_lane < 24), 1.0, 0.0
    ).astype(BF16)
    tail_ones = jnp.where(
        (inner_lane[0:1] >= 24) & (inner_lane[0:1] < 27), 1.0, 0.0
    )
    pack_lane = lax.broadcasted_iota(jnp.int32, (1, TILE), 1) // 32

    def pack_mask(j):
        return jnp.where(pack_lane == j, 1.0, 0.0).astype(BF16)

    def pack_rows(h):
        packs = (dot(xtb[h], select, NN) + tail_ones).astype(BF16)
        for g in range(4):
            xpack[g] = packs[:, TILE * g:TILE * g + TILE]

    def half_lanes(h):
        return pl.ds(pl.multiple_of(h * 128, 128), 128)

    def logits_of(v):
        g, j = quo(v, 2), 2 * rem(v, 2)
        xp = xpack[g]
        rhs = jnp.concatenate([xp * pack_mask(j), xp * pack_mask(j + 1)], axis=0)
        raw[...] = dot(lhs_f[g], rhs, NT)

    def weigh(h, v):
        lanes = half_lanes(h)
        logits = raw[...]
        e1, e2 = split2(jnp.exp(logits - jnp.max(logits, axis=0, keepdims=True)))
        for k in range(2):
            a1b[2 * v + k, :, lanes] = e1[:, 128 * k:128 * k + 128]
            a2b[2 * v + k, :, lanes] = e2[:, 128 * k:128 * k + 128]

    def rebuild(h, v):
        lanes = half_lanes(h)
        got = sum(
            dot(cp3[v], jnp.concatenate([b[2 * v, :, lanes], b[2 * v + 1, :, lanes]], axis=1), NN)
            for b in (a1b, a2b)
        )
        for k in range(2):
            part = got[32 * k:32 * k + 32, 128 * k:128 * k + 128]
            scale_i = 1.0 / part[27:28]
            inv[2 * v + k, :, lanes] = scale_i
            rt[2 * v + k, :, lanes] = (part[0:8] + part[8:16] + part[16:24]) * scale_i

    def assign_steps(h, first, last):
        def step(v, carry):
            rebuild(h, v)
            weigh(h, v + 1)
            logits_of(v + 2)
            return carry

        lax.fori_loop(first, last, step, 0, unroll=UNROLL)

    xtb[xl] = p_ref[:, pl.ds(col, TILE)]
    pack_rows(xl)
    def assign_open(h):
        logits_of(0)
        weigh(h, 0)
        logits_of(1)

    def assign_close(h):
        rebuild(h, 6)
        weigh(h, 7)
        rebuild(h, 7)

    assign_open(xl)
    assign_steps(xl, 0, BEFORE)
    pl.semaphore_wait(barrier, len(peers))

    def gather_plane(own, piece_of, base):
        def rel(h, a, b):
            return (a, b) if h == 0 else (b, a)

        def slot(dy, dz):
            return (rem(y + dy, 4)) * 4 + rem(z + dz, 4)

        def sem(dy, dz, h, part):
            return base + (((dy % 4) * 4 + dz % 4) * 2 + h) * 2 + (part or 0)

        def send(h, a, b, part, first_axis, step):
            dy, dz = rel(h, a, b)
            sy, sz = rel(h, step, 0) if first_axis else rel(h, 0, step)
            dst = piece_of(slot(dy, dz), h, part)
            src = own(h) if (a, b) == (0, 0) else dst
            push(src, dst, sem(dy - sy, dz - sz, h, part), dev_yz(sy % 4, sz % 4))

        def wait(h, a, b, part):
            dy, dz = rel(h, a, b)
            arrive(piece_of(slot(dy, dz), h, part), sem(dy, dz, h, part))

        def wave0():
            for h in range(2):
                for step in (1, 3, 2):
                    send(h, 0, 0, None, True, step)
            for h in range(2):
                for step in (1, 3):
                    send(h, 0, 0, None, False, step)

        def wave1():
            for h in range(2):
                for a in (3, 1):
                    wait(h, a, 0, None)
                    send(h, a, 0, None, False, 1)
                    send(h, a, 0, None, False, 3)
            for h in range(2):
                for b, part, step in ((3, 0, 1), (1, 1, 3)):
                    wait(h, 0, b, None)
                    send(h, 0, b, part, False, step)

        def wave2():
            for h in range(2):
                wait(h, 2, 0, None)
                for step in (2, 1, 3):
                    send(h, 2, 0, None, False, step)

        def wave2b():
            for h in range(2):
                for a in (3, 1):
                    for b, part, step in ((3, 0, 1), (1, 1, 3)):
                        wait(h, a, b, None)
                        send(h, a, b, part, False, step)

        def row_wait(dy):
            for h in range(2):
                for dz in (0, 1, 3, 2):
                    a, b = (dy, dz) if h == 0 else (dz, dy)
                    if b == 2 and a != 2:
                        wait(h, a, b, 0)
                        wait(h, a, b, 1)
                    elif a == 2 and b != 0:
                        wait(h, a, b, None)

        return wave0, wave1, wave2, wave2b, row_wait

    def q_piece(s, h, part):
        if part is None:
            return qbuf.at[s, pl.ds(32 * h, 32), :]
        return qbuf.at[s, pl.ds(32 * h + 16 * part, 16), :]

    qw = gather_plane(lambda h: q_ref.at[pl.ds(32 * h, 32), :], q_piece, block(64))
    s_p = block(2)
    x_to = rem(x + 3 + 2 * core, 4)
    p_to = dev(x_to, y, z, core)
    col_to = tile_col(rem(x_to + 4 - 2 * core, 4))
    push(p_ref.at[:, pl.ds(col_to, TILE)], xtb.at[xl], s_p, p_to)
    qw[0]()
    push(p_ref, pbuf.at[xl], s_p + 1, p_to)

    assign_steps(xl, BEFORE, 6)
    assign_close(xl)
    qw[1]()
    arrive(xtb.at[1 - xl], s_p)
    pack_rows(1 - xl)
    assign_open(1 - xl)
    assign_steps(1 - xl, 0, 3)
    qw[2]()
    assign_steps(1 - xl, 3, 6)
    assign_close(1 - xl)

    mine = core * 4 + u
    rbuf[mine] = rt[...].reshape(TILE, ROWS).T.astype(BF16)

    def r_slot(step):
        return core * 4 + rem(u + step, 4)

    def r_sib(step):
        return (1 - core) * 4 + rem(u + 2 + step, 4)

    s_r = block(4)
    s_rs = block(4)
    owner = u != 3
    for step in (2, 1, 3):
        push(rbuf.at[mine], rbuf.at[mine], s_r + 4 - step, dev_x(step), owner)
    push(rbuf.at[mine], rbuf.at[mine], s_rs, sibling, owner)
    qw[3]()
    for step in (1, 3, 2):
        s = r_slot(step)
        real = rem(u + step, 4) != 3
        arrive(rbuf.at[s], s_r + step, real)
        push(rbuf.at[s], rbuf.at[s], s_rs + step, sibling, real)
    arrive(pbuf.at[1 - xl], s_p + 1)

    for dy in (0, 1, 3, 2):
        qw[4](dy)

    p_all = pbuf[...].reshape(ROWS, D)
    scale = float(D) ** (-0.5)
    scale2 = scale * LOG2E
    for n in range(4):
        qc = qbuf[4 * n:4 * n + 4].reshape(256, D)
        t = dot(p_all, qc, NT)
        m_t = jnp.max(t, axis=0, keepdims=True)
        tbuf[n] = t
        e_t = jnp.exp2((t - m_t) * scale2)
        ebt[n] = e_t
        s_t = jnp.sum(e_t, axis=0, keepdims=True)
        m_t = m_t * scale
        lt = m_t + jnp.log(s_t)
        sumt[n] = s_t
        for k in range(2):
            mloc[2 * n + k:2 * n + k + 1, :] = m_t[:, 128 * k:128 * k + 128]
            stat_t[me, 2 * n + k:2 * n + k + 1, :] = lt[:, 128 * k:128 * k + 128]

    def plane_send(buf, base):
        for a, b in FAR_FIRST:
            push(buf.at[me], buf.at[me], base + (rem(4 - a, 4)) * 4 + rem(4 - b, 4), dev_yz(a, b))

    def plane_wait(buf, base):
        for a, b in FAR_FIRST:
            arrive(buf.at[(rem(y + a, 4)) * 4 + rem(z + b, 4)], base + a * 4 + b)

    s_ta = block(16)
    plane_send(stat_t, s_ta)
    for step in (0, 1, 3, 2):
        arrive(rbuf.at[r_sib(step)], s_rs + step, rem(u + 2 + step, 4) != 3)

    r_all = jnp.concatenate([rbuf[k] for k in (0, 1, 2, 4, 5, 6)], axis=1)
    for n in range(4):
        qc = qbuf[4 * n:4 * n + 4].reshape(256, D)
        s = dot(r_all, qc, NT)
        m_s = jnp.max(s, axis=0, keepdims=True)
        e_s = jnp.exp2((s - m_s) * scale2)
        ebs[n] = e_s
        m_s = m_s * scale
        ls = m_s + jnp.log(jnp.sum(e_s, axis=0, keepdims=True))
        cross = jnp.sum(ebt[n] * (tbuf[n] - s), axis=0, keepdims=True) * scale / sumt[n]
        for k in range(2):
            r = 2 * n + k
            mloc[8 + r:9 + r, :] = m_s[:, 128 * k:128 * k + 128]
            stat[me, r:r + 1, :] = ls[:, 128 * k:128 * k + 128]
            stat[me, 8 + r:9 + r, :] = cross[:, 128 * k:128 * k + 128]

    s_st = block(16)
    plane_send(stat, s_st)
    plane_wait(stat_t, s_ta)
    lt = stat_t[...]
    plane_wait(stat, s_st)
    ls, cx = stat[:, 0:8], stat[:, 8:16]
    top_t = jnp.max(lt, axis=0)
    top_s = jnp.max(ls, axis=0)
    big_t = top_t + jnp.log(jnp.sum(jnp.exp(lt - top_t[None]), axis=0))
    big_s = top_s + jnp.log(jnp.sum(jnp.exp(ls - top_s[None]), axis=0))
    cross = jnp.sum(jnp.exp(lt - big_t[None]) * cx, axis=0)
    divb[xl] = cross - big_t + big_s
    s_d = block(1)
    push(divb.at[xl], divb.at[xl], s_d, dev(x + 1 - 2 * xl, y, z, core))
    weight = (PB * 32 / 64.0) * scale
    f_t = jnp.exp(mloc[0:8, :] - big_t) * weight
    f_s = jnp.exp(mloc[8:16, :] - big_s) * weight

    grads = []
    for n in range(4):
        for k in range(2):
            r = 2 * n + k
            cols = slice(128 * k, 128 * k + 128)
            diff = ebs[n, :, cols] * f_s[r:r + 1] - ebt[n, :, cols] * f_t[r:r + 1]
            grads.append(diff.astype(BF16))
    grad_scores = jnp.concatenate(grads, axis=1)

    def partial(group, first, tiles):
        at = pl.multiple_of(group * 384 + first * TILE, TILE)
        return dot(grad_scores, qbuf[:, :, pl.ds(at, TILE * tiles)].reshape(QN, TILE * tiles), NN)

    s_g = block(3)
    for group, dest in ((1 - core, gsrc), (core, gown)):
        two = partial(group, 0, 2)
        dest[0] = two[:, :TILE]
        dest[1] = two[:, TILE:]
        if dest is gsrc:
            push(gsrc.at[0], gsib.at[0], s_g, sibling)
            push(gsrc.at[1], gsib.at[1], s_g + 1, sibling)
        dest[2] = partial(group, 2, 1)
        if dest is gsrc:
            push(gsrc.at[2], gsib.at[2], s_g + 2, sibling)

    s_1 = block(2)
    s_2 = block(4)

    def half(n):
        return pl.ds(128 * n, 128)

    def near(step):
        return jnp.minimum(rem(u + step, 4), 2)

    for k in range(3):
        arrive(gsib.at[k], s_g + k)
        gown[k] = gown[k] + gsib[k]
    for part, to in ((0, right), (1, left)):
        push(gown.at[near(2), half(part), :], rs1.at[part], s_1 + part, to, rem(u + 2, 4) != 3)
    for part, to, step in ((0, right, 1), (1, left, 3)):
        push(
            gown.at[near(step), half(1 - part), :], rs2.at[part, half(1 - part), :],
            s_2 + 2 * part, to, rem(u + step, 4) != 3,
        )
    for part, to, step in ((0, right, 1), (1, left, 3)):
        ok = rem(u + step, 4) != 3
        arrive(rs1.at[part], s_1 + part, ok)
        rs2s[part] = gown[near(step), half(part), :] + rs1[part]
        push(rs2s.at[part], rs2.at[part, half(part), :], s_2 + 2 * part + 1, to, ok)
    for part in range(2):
        arrive(rs2.at[part, half(1 - part), :], s_2 + 2 * part, owner)
        arrive(rs2.at[part, half(part), :], s_2 + 2 * part + 1, owner)
    s_c = block(64)
    s_o = block(1)
    first_c = len(sends)
    sends.extend([None] * 64)

    def plane_order(n):
        y_n = rem(y + rem(n, 4), 4)
        return y_n * 4 + rem(y_n + quo(n, 4), 4)

    def piece_copy(n, step):
        other = plane_order(n)
        who, slot, sem = core, u, s_c + 16 * u + me
        if step == 0:
            own = 1 - jnp.minimum(jnp.abs(other - me), 1)
            who = core + own * (1 - 2 * core)
            slot = u + own * (3 - u)
            sem = sem + own * (s_o - sem)
        return pltpu.make_async_remote_copy(
            src_ref=dcs.at[other], dst_ref=dcr.at[slot, me],
            send_sem=send_sem.at[first_c + 4 * n + step], recv_sem=recv_sem.at[sem],
            device_id=dev(rem(x + step, 4), quo(other, 4), rem(other, 4), who), device_id_type=MESH,
        )

    def piece_send(n):
        for step in (2, 1, 3, 0):
            piece_copy(n, step).start()

    def piece_sent(n, carry):
        for step in (2, 1, 3, 0):
            piece_copy(n, step).wait_send()
        return carry

    def diff_of(n):
        i = plane_order(n)
        p, j = quo(i, 4), rem(i, 4)
        return dot(lhs_b[p], gpack[p] * pack_mask(j), NT)

    def differ(n, diff):
        i = plane_order(n)
        d1, d2 = split2((a1b[i].astype(F32) + a2b[i].astype(F32)) * diff)
        dbuf[0] = d1
        dbuf[1] = d2

    def contract(n):
        i = plane_order(n)
        ow = dot(gl[i], a1b[i], NT) + dot(gl[i], a2b[i], NT)
        od = dot(xlt[i], dbuf[0], NT) + dot(xlt[i], dbuf[1], NT)
        code = cb_ref[pl.ds(pl.multiple_of(SUB * i, SUB), SUB), :]
        dcs[i] = ow[0:8] + ow[8:16] + od[0:8] - code * od[8:16]

    def next_step(n, carry):
        diff = diff_of(n + 1)
        contract(n)
        differ(n + 1, diff)
        piece_send(n - 1)
        return carry

    @pl.when(owner)
    def _():
        g = gown[near(0)] + rs2[0] + rs2[1]
        xt = xtb[...].reshape(ROWS, TILE)
        gt = (g.T).reshape(GROUPS, SUB, ROWS) * inv[...]
        g1t, g2t = split2(gt)
        gl[...] = jnp.concatenate([g1t.astype(F32), g2t.astype(F32)], axis=1).astype(BF16)
        inner = -jnp.sum(gt * rt[...], axis=1, keepdims=True)
        t_parts = [jnp.broadcast_to(t.astype(F32), gt.shape) for t in split3(inner)]
        at_row = lax.broadcasted_iota(jnp.int32, gt.shape, 1)
        last = jnp.zeros_like(gt)
        for k in range(3):
            last = jnp.where(at_row == k, t_parts[k], last)
        g1f = g1t.astype(F32)
        stacked = jnp.concatenate([g1f, g1f, g2t.astype(F32), last], axis=1)
        for k in range(4):
            gpack[k] = stacked[4 * k:4 * k + 4].reshape(TILE, ROWS).T.astype(BF16)
        xlt[...] = jnp.concatenate(
            [xt.astype(F32).T.reshape(GROUPS, SUB, ROWS), jnp.full((GROUPS, SUB, ROWS), 1.0, F32)],
            axis=1,
        ).astype(BF16)

        differ(0, diff_of(0))
        contract(0)
        differ(1, diff_of(1))
        lax.fori_loop(1, 15, next_step, 0)
        piece_send(14)
        contract(15)
        piece_send(15)
        dcr[u, me] = dcs[me]

    for k in range(3):
        arrive(dcr.at[k, me], s_c + 16 * k + me, u != k)

    def piece_wait(n, carry):
        other = rem(me + n, 16)
        for k in range(3):
            arrive(dcr.at[k, other], s_c + 16 * k + other)
        return carry

    lax.fori_loop(1, 16, piece_wait, 0)
    arrive(dcr.at[3, me], s_o, rem(u + 2, 4) != 3)

    for k in range(3):
        out_ref[3 * core + k, me] = jnp.sum(dcr[k], axis=0)

    def trio(s, c):
        return out_ref.at[pl.ds(3 * c, 3), s]

    s_f = block(16)
    s_fs = block(16)
    for a, b in FAR_FIRST:
        push(trio(me, core), trio(me, core), s_f + me, dev_yz(a, b))
    push(trio(me, core), trio(me, core), s_fs + me, sibling)
    first_r = len(sends)
    sends.extend([None] * 16)

    def relay(n, carry):
        other = plane_order(n)

        @pl.when(other != me)
        def _():
            arrive(trio(other, core), s_f + other)
            pltpu.make_async_remote_copy(
                src_ref=trio(other, core), dst_ref=trio(other, core),
                send_sem=send_sem.at[first_r + n], recv_sem=recv_sem.at[s_fs + other],
                device_id=sibling, device_id_type=MESH,
            ).start()

        return carry

    def relay_wait(n, carry):
        other = plane_order(n)
        arrive(trio(other, 1 - core), s_fs + other)

        @pl.when(other != me)
        def _():
            pltpu.make_async_remote_copy(
                src_ref=trio(other, core), dst_ref=trio(other, core),
                send_sem=send_sem.at[first_r + n], recv_sem=recv_sem.at[s_fs + other],
                device_id=sibling, device_id_type=MESH,
            ).wait_send()

        return carry

    lax.fori_loop(0, 16, relay, 0)
    lax.fori_loop(0, 16, relay_wait, 0)

    arrive(divb.at[1 - xl], s_d)
    for k in range(4):
        for h in range(2):
            div_ref[4 * k + 2 * h:4 * k + 2 * h + 2, :] = divb[h, 2 * k:2 * k + 2, :]

    @pl.when(owner)
    def _():
        lax.fori_loop(0, 16, piece_sent, 0)

    for entry in sends:
        if entry is not None:
            guarded(entry[1], entry[0].wait_send)


def local(passages, queries, codebook):
    vmem = pl.BlockSpec(memory_space=pltpu.VMEM)
    grad, divergence = pl.pallas_call(
        kernel,
        out_shape=(
            pltpu.VMEM((6, PLANE, SUB, CODES), F32),
            pltpu.VMEM((16, 128), F32),
        ),
        in_specs=[vmem, vmem, pl.BlockSpec(memory_space=pl.ANY)],
        out_specs=(vmem, vmem),
        scratch_shapes=[
            pltpu.VMEM((TILE, CODES), F32),
            pltpu.SemaphoreType.DMA,
            pltpu.VMEM((PLANE, QB, D), BF16),
            pltpu.VMEM((2, PB, D), BF16),
            pltpu.VMEM((8, ROWS, TILE), BF16),
            pltpu.VMEM((2, PB, TILE), BF16),
            pltpu.VMEM((CODES, ROWS), F32),
            pltpu.VMEM((4, PB, TILE), BF16),
            pltpu.VMEM((4, CODES, TILE), BF16),
            pltpu.VMEM((4, CODES, TILE), BF16),
            pltpu.VMEM((8, 64, CODES), BF16),
            pltpu.VMEM((GROUPS, SUB, ROWS), F32),
            pltpu.VMEM((GROUPS, 1, ROWS), F32),
            pltpu.VMEM((GROUPS, CODES, ROWS), BF16),
            pltpu.VMEM((GROUPS, CODES, ROWS), BF16),
            pltpu.VMEM((4, ROWS, 256), F32),
            pltpu.VMEM((4, ROWS, 256), F32),
            pltpu.VMEM((4, ROWS, 256), F32),
            pltpu.VMEM((4, 1, 256), F32),
            pltpu.VMEM((16, 128), F32),
            pltpu.VMEM((PLANE, 8, 128), F32),
            pltpu.VMEM((PLANE, 16, 128), F32),
            pltpu.VMEM((3, ROWS, TILE), F32),
            pltpu.VMEM((3, ROWS, TILE), F32),
            pltpu.VMEM((3, ROWS, TILE), F32),
            pltpu.VMEM((2, 128, TILE), F32),
            pltpu.VMEM((2, ROWS, TILE), F32),
            pltpu.VMEM((2, 128, TILE), F32),
            pltpu.VMEM((GROUPS, 16, ROWS), BF16),
            pltpu.VMEM((2, CODES, ROWS), BF16),
            pltpu.VMEM((GROUPS, 16, ROWS), BF16),
            pltpu.VMEM((4, ROWS, TILE), BF16),
            pltpu.VMEM((PLANE, SUB, CODES), F32),
            pltpu.VMEM((4, PLANE, SUB, CODES), F32),
            pltpu.VMEM((2, 8, 128), F32),
            pltpu.SemaphoreType.DMA((N_SEM,)),
            pltpu.SemaphoreType.DMA((240,)),
        ],
        compiler_params=pltpu.CompilerParams(
            collective_id=0, has_side_effects=True, vmem_limit_bytes=60 * 1024 * 1024
        ),
    )(passages, queries, codebook.reshape(D, CODES))
    return divergence.reshape(2048), grad.reshape(96, SUB, CODES)


def solution(mesh):
    placed = (P("corpus", None), P(("query", "corpus"), None), P())
    return jax.shard_map(
        local, mesh=mesh, in_specs=placed, out_specs=(P("query"), P()), check_vma=False
    )
```

```python
import functools

import jax
import jax.numpy as jnp
from jax import lax
from jax.experimental import pallas as pl
from jax.experimental.pallas import tpu as pltpu
from jax.sharding import PartitionSpec as P

MESH = pl.DeviceIdType.MESH
F32 = jnp.float32
BF16 = jnp.bfloat16
NT = (((1,), (1,)), ((), ()))
NN = (((1,), (0,)), ((), ()))

D = 768
SUB = 8
CODES = 256
QB = 64
PB = 128
PLANE = 16
TILE = 128
GROUPS = 16
ROWS = 256
QN = 1024
BEFORE = 4
UNROLL = 1
N_SEM = 224
LOG2E = 1.4426950408889634
FAR_FIRST = [(2, 2), (2, 1), (2, 3), (1, 2), (3, 2), (1, 1), (1, 3), (3, 1), (3, 3), (2, 0), (0, 2), (1, 0), (3, 0), (0, 1), (0, 3)]


def rem(a, b):
    return a % b if isinstance(a, int) else lax.rem(a, b)


def quo(a, b):
    return a // b if isinstance(a, int) else lax.div(a, b)


def split3(value):
    high = value.astype(BF16)
    rest = value - high.astype(F32)
    mid = rest.astype(BF16)
    low = (rest - mid.astype(F32)).astype(BF16)
    return high, mid, low


def split2(value):
    high = value.astype(BF16)
    low = (value - high.astype(F32)).astype(BF16)
    return high, low


def dot(a, b, dims):
    return lax.dot_general(a, b, dims, preferred_element_type=F32)


def kernel(
    p_ref, q_ref, cb_hbm,
    out_ref, div_ref,
    cb_ref, cb_sem,
    qbuf, pbuf, rbuf,
    xtb, raw, xpack, lhs_f, lhs_b, cp3, rt, inv, a1b, a2b,
    tbuf, ebt, ebs, sumt, mloc, stat_t, stat,
    gown, gsib, gsrc, rs1, rs2, rs2s,
    gl, dbuf, xlt, gpack, dcs, dcr, divb,
    send_sem, recv_sem,
):
    qi = lax.axis_index("query")
    ci = lax.axis_index("corpus")
    xh, core = quo(qi, 2), rem(qi, 2)
    y, xl, z = quo(ci, 8), rem(quo(ci, 4), 2), rem(ci, 4)
    x = xh * 2 + xl
    u = rem(x + 4 - 2 * core, 4)

    def dev(x_, y_, z_, core_):
        return (quo(x_, 2) * 2 + core_, y_ * 8 + rem(x_, 2) * 4 + z_)

    def dev_x(step, core_=None):
        return dev(rem(x + step, 4), y, z, core if core_ is None else core_)

    def dev_yz(dy, dz):
        return dev(x, rem(y + dy, 4), rem(z + dz, 4), core)

    sibling = dev(x, y, z, 1 - core)
    left, right = dev_x(3), dev_x(1)

    sends = []
    count = [0]

    def guarded(cond, action):
        if cond is None:
            action()
        else:
            pl.when(cond)(action)

    def push(src, dst, index, device, cond=None):
        copy = pltpu.make_async_remote_copy(
            src_ref=src, dst_ref=dst, send_sem=send_sem.at[len(sends)],
            recv_sem=recv_sem.at[index], device_id=device, device_id_type=MESH,
        )
        guarded(cond, copy.start)
        sends.append((copy, cond))

    def arrive(dst, index, cond=None):
        guarded(cond, pltpu.make_async_remote_copy(
            src_ref=dst, dst_ref=dst, send_sem=send_sem.at[0],
            recv_sem=recv_sem.at[index], device_id=sibling, device_id_type=MESH,
        ).wait_recv)

    def block(n):
        first = count[0]
        count[0] += n
        return first

    def tile_col(u_):
        return pl.multiple_of((3 * core + jnp.minimum(u_, 2)) * TILE, TILE)

    col = tile_col(u)
    fetch = pltpu.make_async_copy(cb_hbm.at[pl.ds(col, TILE), :], cb_ref, cb_sem)
    fetch.start()

    barrier = pltpu.get_barrier_semaphore()
    peers = [left, right, sibling]
    peers += [dev_yz(a, b) for a, b in ((0, 1), (0, 3), (0, 2), (1, 0), (3, 0), (2, 0))]
    for peer in peers:
        pl.semaphore_signal(barrier, inc=1, device_id=peer, device_id_type=MESH)

    me = y * 4 + z
    qbuf[me] = q_ref[...]
    pbuf[xl] = p_ref[...]

    fetch.wait()
    cb = cb_ref[...]
    grouped = cb.reshape(GROUPS, SUB, CODES)
    bias = -0.5 * jnp.sum(grouped * grouped, axis=1, keepdims=True)
    b_parts = [jnp.broadcast_to(b.astype(F32), grouped.shape) for b in split3(bias)]
    row = lax.broadcasted_iota(jnp.int32, grouped.shape, 1)
    extra = jnp.where(row == 3, 1.0, 0.0)
    for k in range(3):
        extra = jnp.where(row == k, b_parts[k], extra)
    c_parts = [c.astype(F32).reshape(GROUPS, SUB, CODES) for c in split3(cb)]
    packed = jnp.concatenate(c_parts + [extra], axis=1)
    cp3[...] = packed.reshape(8, 64, CODES).astype(BF16)
    for g in range(4):
        lhs_f[g] = packed[4 * g:4 * g + 4].reshape(TILE, CODES).T.astype(BF16)

    lane = lax.broadcasted_iota(jnp.int32, (TILE, 4 * TILE), 1)
    source = lax.broadcasted_iota(jnp.int32, (TILE, 4 * TILE), 0)
    inner_lane = lane % 32
    select = jnp.where(
        (source == (lane // 32) * SUB + lane % SUB) & (inner_lane < 24), 1.0, 0.0
    ).astype(BF16)
    tail_ones = jnp.where(
        (inner_lane[0:1] >= 24) & (inner_lane[0:1] < 27), 1.0, 0.0
    )
    pack_lane = lax.broadcasted_iota(jnp.int32, (1, TILE), 1) // 32

    def pack_mask(j):
        return jnp.where(pack_lane == j, 1.0, 0.0).astype(BF16)

    def pack_rows(h):
        packs = (dot(xtb[h], select, NN) + tail_ones).astype(BF16)
        for g in range(4):
            xpack[g] = packs[:, TILE * g:TILE * g + TILE]

    def half_lanes(h):
        return pl.ds(pl.multiple_of(h * 128, 128), 128)

    def logits_of(v):
        g, j = quo(v, 2), 2 * rem(v, 2)
        xp = xpack[g]
        rhs = jnp.concatenate([xp * pack_mask(j), xp * pack_mask(j + 1)], axis=0)
        raw[...] = dot(lhs_f[g], rhs, NT)

    def weigh(h, v):
        lanes = half_lanes(h)
        logits = raw[...]
        e1, e2 = split2(jnp.exp(logits - jnp.max(logits, axis=0, keepdims=True)))
        for k in range(2):
            a1b[2 * v + k, :, lanes] = e1[:, 128 * k:128 * k + 128]
            a2b[2 * v + k, :, lanes] = e2[:, 128 * k:128 * k + 128]

    def rebuild(h, v):
        lanes = half_lanes(h)
        got = sum(
            dot(cp3[v], jnp.concatenate([b[2 * v, :, lanes], b[2 * v + 1, :, lanes]], axis=1), NN)
            for b in (a1b, a2b)
        )
        for k in range(2):
            part = got[32 * k:32 * k + 32, 128 * k:128 * k + 128]
            scale_i = 1.0 / part[27:28]
            inv[2 * v + k, :, lanes] = scale_i
            rt[2 * v + k, :, lanes] = (part[0:8] + part[8:16] + part[16:24]) * scale_i

    def assign_steps(h, first, last):
        def step(v, carry):
            rebuild(h, v)
            weigh(h, v + 1)
            logits_of(v + 2)
            return carry

        lax.fori_loop(first, last, step, 0, unroll=UNROLL)

    xtb[xl] = p_ref[:, pl.ds(col, TILE)]
    pack_rows(xl)
    def assign_open(h):
        logits_of(0)
        weigh(h, 0)
        logits_of(1)

    def assign_close(h):
        rebuild(h, 6)
        weigh(h, 7)
        rebuild(h, 7)

    assign_open(xl)
    assign_steps(xl, 0, BEFORE)
    pl.semaphore_wait(barrier, len(peers))

    def gather_plane(own, piece_of, base):
        def rel(h, a, b):
            return (a, b) if h == 0 else (b, a)

        def slot(dy, dz):
            return (rem(y + dy, 4)) * 4 + rem(z + dz, 4)

        def sem(dy, dz, h, part):
            return base + (((dy % 4) * 4 + dz % 4) * 2 + h) * 2 + (part or 0)

        def send(h, a, b, part, first_axis, step):
            dy, dz = rel(h, a, b)
            sy, sz = rel(h, step, 0) if first_axis else rel(h, 0, step)
            dst = piece_of(slot(dy, dz), h, part)
            src = own(h) if (a, b) == (0, 0) else dst
            push(src, dst, sem(dy - sy, dz - sz, h, part), dev_yz(sy % 4, sz % 4))

        def wait(h, a, b, part):
            dy, dz = rel(h, a, b)
            arrive(piece_of(slot(dy, dz), h, part), sem(dy, dz, h, part))

        def wave0():
            for h in range(2):
                for step in (2, 1, 3):
                    send(h, 0, 0, None, True, step)
            for h in range(2):
                for step in (2, 1, 3):
                    send(h, 0, 0, None, False, step)

        def onward(h, a):
            wait(h, a, 0, None)
            for step in (2, 1, 3):
                send(h, a, 0, None, False, step)

        def wave1():
            for h in range(2):
                onward(h, 1)
                onward(h, 3)

        def wave2():
            for h in range(2):
                onward(h, 2)

        def wave3():
            for h in range(2):
                for b in (1, 3, 2):
                    for a in (0, 1, 3, 2):
                        wait(h, a, b, None)

        return wave0, wave1, wave2, wave3

    def q_piece(s, h, part):
        if part is None:
            return qbuf.at[s, pl.ds(32 * h, 32), :]
        return qbuf.at[s, pl.ds(32 * h + 16 * part, 16), :]

    qw = gather_plane(lambda h: q_ref.at[pl.ds(32 * h, 32), :], q_piece, block(64))
    s_p = block(2)
    x_to = rem(x + 3 + 2 * core, 4)
    p_to = dev(x_to, y, z, core)
    col_to = tile_col(rem(x_to + 4 - 2 * core, 4))
    push(p_ref.at[:, pl.ds(col_to, TILE)], xtb.at[xl], s_p, p_to)
    qw[0]()
    push(p_ref, pbuf.at[xl], s_p + 1, p_to)

    assign_steps(xl, BEFORE, 6)
    assign_close(xl)
    qw[1]()
    arrive(xtb.at[1 - xl], s_p)
    pack_rows(1 - xl)
    assign_open(1 - xl)
    qw[2]()
    assign_steps(1 - xl, 0, 3)
    assign_steps(1 - xl, 3, 6)
    assign_close(1 - xl)

    mine = core * 4 + u
    rbuf[mine] = rt[...].reshape(TILE, ROWS).T.astype(BF16)

    def r_slot(step):
        return core * 4 + rem(u + step, 4)

    def r_sib(step):
        return (1 - core) * 4 + rem(u + 2 + step, 4)

    s_r = block(4)
    s_rs = block(4)
    owner = u != 3
    for step in (2, 1, 3):
        push(rbuf.at[mine], rbuf.at[mine], s_r + 4 - step, dev_x(step), owner)
    push(rbuf.at[mine], rbuf.at[mine], s_rs, sibling, owner)

    xt = xtb[...].reshape(ROWS, TILE)
    xlt[...] = jnp.concatenate(
        [xt.astype(F32).T.reshape(GROUPS, SUB, ROWS), jnp.full((GROUPS, SUB, ROWS), 1.0, F32)], axis=1
    ).astype(BF16)
    code1, code2 = (c.astype(F32).reshape(GROUPS, SUB, CODES) for c in split2(cb_ref[...]))
    ones3 = jnp.where(lax.broadcasted_iota(jnp.int32, code1.shape, 1) < 3, 1.0, 0.0)
    packed_b = jnp.concatenate([code1, code2, code1, ones3], axis=1)
    for g in range(4):
        lhs_b[g] = packed_b[4 * g:4 * g + 4].reshape(TILE, CODES).T.astype(BF16)

    for step in (1, 3, 2):
        s = r_slot(step)
        real = rem(u + step, 4) != 3
        arrive(rbuf.at[s], s_r + step, real)
        push(rbuf.at[s], rbuf.at[s], s_rs + step, sibling, real)
    arrive(pbuf.at[1 - xl], s_p + 1)

    qw[3]()

    p_all = pbuf[...].reshape(ROWS, D)
    scale = float(D) ** (-0.5)
    scale2 = scale * LOG2E
    for n in range(4):
        qc = qbuf[4 * n:4 * n + 4].reshape(256, D)
        t = dot(p_all, qc, NT)
        m_t = jnp.max(t, axis=0, keepdims=True)
        tbuf[n] = t
        e_t = jnp.exp2((t - m_t) * scale2)
        ebt[n] = e_t
        s_t = jnp.sum(e_t, axis=0, keepdims=True)
        m_t = m_t * scale
        lt = m_t + jnp.log(s_t)
        sumt[n] = s_t
        for k in range(2):
            mloc[2 * n + k:2 * n + k + 1, :] = m_t[:, 128 * k:128 * k + 128]
            stat_t[me, 2 * n + k:2 * n + k + 1, :] = lt[:, 128 * k:128 * k + 128]

    def plane_send(buf, base):
        for a, b in FAR_FIRST:
            push(buf.at[me], buf.at[me], base + (rem(4 - a, 4)) * 4 + rem(4 - b, 4), dev_yz(a, b))

    def plane_wait(buf, base):
        for a, b in FAR_FIRST:
            arrive(buf.at[(rem(y + a, 4)) * 4 + rem(z + b, 4)], base + a * 4 + b)

    s_ta = block(16)
    plane_send(stat_t, s_ta)
    for step in (0, 1, 3, 2):
        arrive(rbuf.at[r_sib(step)], s_rs + step, rem(u + 2 + step, 4) != 3)

    r_all = jnp.concatenate([rbuf[k] for k in (0, 1, 2, 4, 5, 6)], axis=1)
    for n in range(4):
        qc = qbuf[4 * n:4 * n + 4].reshape(256, D)
        s = dot(r_all, qc, NT)
        m_s = jnp.max(s, axis=0, keepdims=True)
        e_s = jnp.exp2((s - m_s) * scale2)
        ebs[n] = e_s
        m_s = m_s * scale
        ls = m_s + jnp.log(jnp.sum(e_s, axis=0, keepdims=True))
        cross = jnp.sum(ebt[n] * (tbuf[n] - s), axis=0, keepdims=True) * scale / sumt[n]
        for k in range(2):
            r = 2 * n + k
            mloc[8 + r:9 + r, :] = m_s[:, 128 * k:128 * k + 128]
            stat[me, r:r + 1, :] = ls[:, 128 * k:128 * k + 128]
            stat[me, 8 + r:9 + r, :] = cross[:, 128 * k:128 * k + 128]

    s_st = block(16)
    plane_send(stat, s_st)
    plane_wait(stat_t, s_ta)
    lt = stat_t[...]
    plane_wait(stat, s_st)
    ls, cx = stat[:, 0:8], stat[:, 8:16]
    top_t = jnp.max(lt, axis=0)
    top_s = jnp.max(ls, axis=0)
    big_t = top_t + jnp.log(jnp.sum(jnp.exp(lt - top_t[None]), axis=0))
    big_s = top_s + jnp.log(jnp.sum(jnp.exp(ls - top_s[None]), axis=0))
    cross = jnp.sum(jnp.exp(lt - big_t[None]) * cx, axis=0)
    divb[xl] = cross - big_t + big_s
    s_d = block(1)
    push(divb.at[xl], divb.at[xl], s_d, dev(x + 1 - 2 * xl, y, z, core))
    weight = (PB * 32 / 64.0) * scale
    f_t = jnp.exp(mloc[0:8, :] - big_t) * weight
    f_s = jnp.exp(mloc[8:16, :] - big_s) * weight

    grads = []
    for n in range(4):
        for k in range(2):
            r = 2 * n + k
            cols = slice(128 * k, 128 * k + 128)
            diff = ebs[n, :, cols] * f_s[r:r + 1] - ebt[n, :, cols] * f_t[r:r + 1]
            grads.append(diff.astype(BF16))
    grad_scores = jnp.concatenate(grads, axis=1)

    def partial(group, first, tiles):
        at = pl.multiple_of(group * 384 + first * TILE, TILE)
        return dot(grad_scores, qbuf[:, :, pl.ds(at, TILE * tiles)].reshape(QN, TILE * tiles), NN)

    s_g = block(3)
    for group, dest in ((1 - core, gsrc), (core, gown)):
        two = partial(group, 0, 2)
        dest[0] = two[:, :TILE]
        dest[1] = two[:, TILE:]
        if dest is gsrc:
            push(gsrc.at[0], gsib.at[0], s_g, sibling)
            push(gsrc.at[1], gsib.at[1], s_g + 1, sibling)
        dest[2] = partial(group, 2, 1)
        if dest is gsrc:
            push(gsrc.at[2], gsib.at[2], s_g + 2, sibling)

    s_1 = block(2)
    s_2 = block(4)

    def half(n):
        return pl.ds(128 * n, 128)

    def near(step):
        return jnp.minimum(rem(u + step, 4), 2)

    for k in range(3):
        arrive(gsib.at[k], s_g + k)
        gown[k] = gown[k] + gsib[k]
    for part, to in ((0, right), (1, left)):
        push(gown.at[near(2), half(part), :], rs1.at[part], s_1 + part, to, rem(u + 2, 4) != 3)
    for part, to, step in ((0, right, 1), (1, left, 3)):
        push(
            gown.at[near(step), half(1 - part), :], rs2.at[part, half(1 - part), :],
            s_2 + 2 * part, to, rem(u + step, 4) != 3,
        )
    for part, to, step in ((0, right, 1), (1, left, 3)):
        ok = rem(u + step, 4) != 3
        arrive(rs1.at[part], s_1 + part, ok)
        rs2s[part] = gown[near(step), half(part), :] + rs1[part]
        push(rs2s.at[part], rs2.at[part, half(part), :], s_2 + 2 * part + 1, to, ok)
    for part in range(2):
        arrive(rs2.at[part, half(1 - part), :], s_2 + 2 * part, owner)
        arrive(rs2.at[part, half(part), :], s_2 + 2 * part + 1, owner)
    s_c = block(64)
    s_o = block(1)
    first_c = len(sends)
    sends.extend([None] * 64)

    def plane_order(n):
        y_n = rem(y + rem(n, 4), 4)
        return y_n * 4 + rem(y_n + quo(n, 4), 4)

    def piece_copy(n, step):
        other = plane_order(n)
        who, slot, sem = core, u, s_c + 16 * u + me
        if step == 0:
            own = 1 - jnp.minimum(jnp.abs(other - me), 1)
            who = core + own * (1 - 2 * core)
            slot = u + own * (3 - u)
            sem = sem + own * (s_o - sem)
        return pltpu.make_async_remote_copy(
            src_ref=dcs.at[other], dst_ref=dcr.at[slot, me],
            send_sem=send_sem.at[first_c + 4 * n + step], recv_sem=recv_sem.at[sem],
            device_id=dev(rem(x + step, 4), quo(other, 4), rem(other, 4), who), device_id_type=MESH,
        )

    def piece_send(n):
        for step in (2, 1, 3, 0):
            piece_copy(n, step).start()

    def piece_sent(n, carry):
        for step in (2, 1, 3, 0):
            piece_copy(n, step).wait_send()
        return carry

    def diff_of(n):
        i = plane_order(n)
        p, j = quo(i, 4), rem(i, 4)
        return dot(lhs_b[p], gpack[p] * pack_mask(j), NT)

    def differ(n, diff):
        i = plane_order(n)
        d1, d2 = split2((a1b[i].astype(F32) + a2b[i].astype(F32)) * diff)
        dbuf[0] = d1
        dbuf[1] = d2

    def contract(n):
        i = plane_order(n)
        ow = dot(gl[i], a1b[i], NT) + dot(gl[i], a2b[i], NT)
        od = dot(xlt[i], dbuf[0], NT) + dot(xlt[i], dbuf[1], NT)
        code = cb_ref[pl.ds(pl.multiple_of(SUB * i, SUB), SUB), :]
        dcs[i] = ow[0:8] + ow[8:16] + od[0:8] - code * od[8:16]

    def next_step(n, carry):
        diff = diff_of(n + 1)
        contract(n)
        differ(n + 1, diff)
        piece_send(n - 1)
        return carry

    @pl.when(owner)
    def _():
        g = gown[near(0)] + rs2[0] + rs2[1]
        gt = (g.T).reshape(GROUPS, SUB, ROWS) * inv[...]
        g1t, g2t = split2(gt)
        gl[...] = jnp.concatenate([g1t.astype(F32), g2t.astype(F32)], axis=1).astype(BF16)
        inner = -jnp.sum(gt * rt[...], axis=1, keepdims=True)
        t_parts = [jnp.broadcast_to(t.astype(F32), gt.shape) for t in split3(inner)]
        at_row = lax.broadcasted_iota(jnp.int32, gt.shape, 1)
        last = jnp.zeros_like(gt)
        for k in range(3):
            last = jnp.where(at_row == k, t_parts[k], last)
        g1f = g1t.astype(F32)
        stacked = jnp.concatenate([g1f, g1f, g2t.astype(F32), last], axis=1)
        for k in range(4):
            gpack[k] = stacked[4 * k:4 * k + 4].reshape(TILE, ROWS).T.astype(BF16)

        differ(0, diff_of(0))
        contract(0)
        differ(1, diff_of(1))
        lax.fori_loop(1, 15, next_step, 0)
        piece_send(14)
        contract(15)
        piece_send(15)
        dcr[u, me] = dcs[me]

    for k in range(3):
        arrive(dcr.at[k, me], s_c + 16 * k + me, u != k)

    def piece_wait(n, carry):
        other = rem(me + n, 16)
        for k in range(3):
            arrive(dcr.at[k, other], s_c + 16 * k + other)
        return carry

    lax.fori_loop(1, 16, piece_wait, 0)
    arrive(dcr.at[3, me], s_o, rem(u + 2, 4) != 3)

    for k in range(3):
        out_ref[3 * core + k, me] = jnp.sum(dcr[k], axis=0)

    def trio(s, c):
        return out_ref.at[pl.ds(3 * c, 3), s]

    s_f = block(16)
    s_fs = block(16)
    for a, b in FAR_FIRST:
        push(trio(me, core), trio(me, core), s_f + me, dev_yz(a, b))
    push(trio(me, core), trio(me, core), s_fs + me, sibling)
    first_r = len(sends)
    sends.extend([None] * 16)

    def relay(n, carry):
        other = plane_order(n)

        @pl.when(other != me)
        def _():
            arrive(trio(other, core), s_f + other)
            pltpu.make_async_remote_copy(
                src_ref=trio(other, core), dst_ref=trio(other, core),
                send_sem=send_sem.at[first_r + n], recv_sem=recv_sem.at[s_fs + other],
                device_id=sibling, device_id_type=MESH,
            ).start()

        return carry

    def relay_wait(n, carry):
        other = plane_order(n)
        arrive(trio(other, 1 - core), s_fs + other)

        @pl.when(other != me)
        def _():
            pltpu.make_async_remote_copy(
                src_ref=trio(other, core), dst_ref=trio(other, core),
                send_sem=send_sem.at[first_r + n], recv_sem=recv_sem.at[s_fs + other],
                device_id=sibling, device_id_type=MESH,
            ).wait_send()

        return carry

    lax.fori_loop(0, 16, relay, 0)
    lax.fori_loop(0, 16, relay_wait, 0)

    arrive(divb.at[1 - xl], s_d)
    for k in range(4):
        for h in range(2):
            div_ref[4 * k + 2 * h:4 * k + 2 * h + 2, :] = divb[h, 2 * k:2 * k + 2, :]

    @pl.when(owner)
    def _():
        lax.fori_loop(0, 16, piece_sent, 0)

    for entry in sends:
        if entry is not None:
            guarded(entry[1], entry[0].wait_send)


def local(passages, queries, codebook):
    vmem = pl.BlockSpec(memory_space=pltpu.VMEM)
    grad, divergence = pl.pallas_call(
        kernel,
        out_shape=(
            pltpu.VMEM((6, PLANE, SUB, CODES), F32),
            pltpu.VMEM((16, 128), F32),
        ),
        in_specs=[vmem, vmem, pl.BlockSpec(memory_space=pl.ANY)],
        out_specs=(vmem, vmem),
        scratch_shapes=[
            pltpu.VMEM((TILE, CODES), F32),
            pltpu.SemaphoreType.DMA,
            pltpu.VMEM((PLANE, QB, D), BF16),
            pltpu.VMEM((2, PB, D), BF16),
            pltpu.VMEM((8, ROWS, TILE), BF16),
            pltpu.VMEM((2, PB, TILE), BF16),
            pltpu.VMEM((CODES, ROWS), F32),
            pltpu.VMEM((4, PB, TILE), BF16),
            pltpu.VMEM((4, CODES, TILE), BF16),
            pltpu.VMEM((4, CODES, TILE), BF16),
            pltpu.VMEM((8, 64, CODES), BF16),
            pltpu.VMEM((GROUPS, SUB, ROWS), F32),
            pltpu.VMEM((GROUPS, 1, ROWS), F32),
            pltpu.VMEM((GROUPS, CODES, ROWS), BF16),
            pltpu.VMEM((GROUPS, CODES, ROWS), BF16),
            pltpu.VMEM((4, ROWS, 256), F32),
            pltpu.VMEM((4, ROWS, 256), F32),
            pltpu.VMEM((4, ROWS, 256), F32),
            pltpu.VMEM((4, 1, 256), F32),
            pltpu.VMEM((16, 128), F32),
            pltpu.VMEM((PLANE, 8, 128), F32),
            pltpu.VMEM((PLANE, 16, 128), F32),
            pltpu.VMEM((3, ROWS, TILE), F32),
            pltpu.VMEM((3, ROWS, TILE), F32),
            pltpu.VMEM((3, ROWS, TILE), F32),
            pltpu.VMEM((2, 128, TILE), F32),
            pltpu.VMEM((2, ROWS, TILE), F32),
            pltpu.VMEM((2, 128, TILE), F32),
            pltpu.VMEM((GROUPS, 16, ROWS), BF16),
            pltpu.VMEM((2, CODES, ROWS), BF16),
            pltpu.VMEM((GROUPS, 16, ROWS), BF16),
            pltpu.VMEM((4, ROWS, TILE), BF16),
            pltpu.VMEM((PLANE, SUB, CODES), F32),
            pltpu.VMEM((4, PLANE, SUB, CODES), F32),
            pltpu.VMEM((2, 8, 128), F32),
            pltpu.SemaphoreType.DMA((N_SEM,)),
            pltpu.SemaphoreType.DMA((240,)),
        ],
        compiler_params=pltpu.CompilerParams(
            collective_id=0, has_side_effects=True, vmem_limit_bytes=60 * 1024 * 1024
        ),
    )(passages, queries, codebook.reshape(D, CODES))
    return divergence.reshape(2048), grad.reshape(96, SUB, CODES)


def solution(mesh):
    placed = (P("corpus", None), P(("query", "corpus"), None), P())
    return jax.shard_map(
        local, mesh=mesh, in_specs=placed, out_specs=(P("query"), P()), check_vma=False
    )
```

```python
import functools

import jax
import jax.numpy as jnp
from jax import lax
from jax.experimental import pallas as pl
from jax.experimental.pallas import tpu as pltpu
from jax.sharding import PartitionSpec as P

MESH = pl.DeviceIdType.MESH
F32 = jnp.float32
BF16 = jnp.bfloat16
NT = (((1,), (1,)), ((), ()))
NN = (((1,), (0,)), ((), ()))

D = 768
SUB = 8
CODES = 256
QB = 64
PB = 128
PLANE = 16
TILE = 128
GROUPS = 16
ROWS = 256
QN = 1024
UNROLL = 1
N_SEM = 224
LOG2E = 1.4426950408889634
FAR_FIRST = [(2, 2), (2, 1), (2, 3), (1, 2), (3, 2), (1, 1), (1, 3), (3, 1), (3, 3), (2, 0), (0, 2), (1, 0), (3, 0), (0, 1), (0, 3)]


def rem(a, b):
    return a % b if isinstance(a, int) else lax.rem(a, b)


def quo(a, b):
    return a // b if isinstance(a, int) else lax.div(a, b)


def split3(value):
    high = value.astype(BF16)
    rest = value - high.astype(F32)
    mid = rest.astype(BF16)
    low = (rest - mid.astype(F32)).astype(BF16)
    return high, mid, low


def split2(value):
    high = value.astype(BF16)
    low = (value - high.astype(F32)).astype(BF16)
    return high, low


def dot(a, b, dims):
    return lax.dot_general(a, b, dims, preferred_element_type=F32)


def kernel(
    p_ref, q_ref, cb_hbm,
    out_ref, div_ref,
    cb_ref, cb_sem,
    qbuf, pbuf, rbuf,
    xtb, raw, xpack, lhs_f, lhs_b, cp3, rt, inv, a1b, a2b,
    tbuf, ebt, ebs, sumt, mloc, stat_t, stat,
    gown, gsib, gsrc, rs1, rs2, rs2s,
    gl, dbuf, xlt, gpack, dcs, dcr, divb,
    send_sem, recv_sem,
):
    qi = lax.axis_index("query")
    ci = lax.axis_index("corpus")
    xh, core = quo(qi, 2), rem(qi, 2)
    y, xl, z = quo(ci, 8), rem(quo(ci, 4), 2), rem(ci, 4)
    x = xh * 2 + xl
    u = rem(x + 4 - 2 * core, 4)

    def dev(x_, y_, z_, core_):
        return (quo(x_, 2) * 2 + core_, y_ * 8 + rem(x_, 2) * 4 + z_)

    def dev_x(step, core_=None):
        return dev(rem(x + step, 4), y, z, core if core_ is None else core_)

    def dev_yz(dy, dz):
        return dev(x, rem(y + dy, 4), rem(z + dz, 4), core)

    sibling = dev(x, y, z, 1 - core)
    left, right = dev_x(3), dev_x(1)

    sends = []
    count = [0]

    def guarded(cond, action):
        if cond is None:
            action()
        else:
            pl.when(cond)(action)

    def push(src, dst, index, device, cond=None):
        copy = pltpu.make_async_remote_copy(
            src_ref=src, dst_ref=dst, send_sem=send_sem.at[len(sends)],
            recv_sem=recv_sem.at[index], device_id=device, device_id_type=MESH,
        )
        guarded(cond, copy.start)
        sends.append((copy, cond))

    def arrive(dst, index, cond=None):
        guarded(cond, pltpu.make_async_remote_copy(
            src_ref=dst, dst_ref=dst, send_sem=send_sem.at[0],
            recv_sem=recv_sem.at[index], device_id=sibling, device_id_type=MESH,
        ).wait_recv)

    def block(n):
        first = count[0]
        count[0] += n
        return first

    def tile_col(u_):
        return pl.multiple_of((3 * core + jnp.minimum(u_, 2)) * TILE, TILE)

    col = tile_col(u)
    fetch = pltpu.make_async_copy(cb_hbm.at[pl.ds(col, TILE), :], cb_ref, cb_sem)
    fetch.start()

    barrier = pltpu.get_barrier_semaphore()
    peers = [left, right, sibling]
    peers += [dev_yz(a, b) for a, b in ((0, 1), (0, 3), (0, 2), (1, 0), (3, 0), (2, 0))]
    for peer in peers:
        pl.semaphore_signal(barrier, inc=1, device_id=peer, device_id_type=MESH)

    me = y * 4 + z
    qbuf[me] = q_ref[...]
    pbuf[xl] = p_ref[...]

    pl.semaphore_wait(barrier, len(peers))

    def gather_plane(own, piece_of, base):
        def rel(h, a, b):
            return (a, b) if h == 0 else (b, a)

        def slot(dy, dz):
            return (rem(y + dy, 4)) * 4 + rem(z + dz, 4)

        def sem(dy, dz, h, part):
            return base + (((dy % 4) * 4 + dz % 4) * 2 + h) * 2 + (part or 0)

        def send(h, a, b, part, first_axis, step):
            dy, dz = rel(h, a, b)
            sy, sz = rel(h, step, 0) if first_axis else rel(h, 0, step)
            dst = piece_of(slot(dy, dz), h, part)
            src = own(h) if (a, b) == (0, 0) else dst
            push(src, dst, sem(dy - sy, dz - sz, h, part), dev_yz(sy % 4, sz % 4))

        def wait(h, a, b, part):
            dy, dz = rel(h, a, b)
            arrive(piece_of(slot(dy, dz), h, part), sem(dy, dz, h, part))

        def wave0():
            for h in range(2):
                for step in (2, 1, 3):
                    send(h, 0, 0, None, True, step)
            for h in range(2):
                for step in (2, 1, 3):
                    send(h, 0, 0, None, False, step)

        def onward(h, a):
            wait(h, a, 0, None)
            for step in (2, 1, 3):
                send(h, a, 0, None, False, step)

        def wave1():
            for h in range(2):
                onward(h, 1)
                onward(h, 3)

        def wave2():
            for h in range(2):
                onward(h, 2)

        def wave3():
            for h in range(2):
                for b in (1, 3, 2):
                    for a in (0, 1, 3, 2):
                        wait(h, a, b, None)

        return wave0, wave1, wave2, wave3

    def q_piece(s, h, part):
        if part is None:
            return qbuf.at[s, pl.ds(32 * h, 32), :]
        return qbuf.at[s, pl.ds(32 * h + 16 * part, 16), :]

    qw = gather_plane(lambda h: q_ref.at[pl.ds(32 * h, 32), :], q_piece, block(64))
    s_p = block(2)
    x_to = rem(x + 3 + 2 * core, 4)
    p_to = dev(x_to, y, z, core)
    col_to = tile_col(rem(x_to + 4 - 2 * core, 4))
    push(p_ref.at[:, pl.ds(col_to, TILE)], xtb.at[xl], s_p, p_to)
    qw[0]()
    push(p_ref, pbuf.at[xl], s_p + 1, p_to)

    fetch.wait()
    cb = cb_ref[...]
    grouped = cb.reshape(GROUPS, SUB, CODES)
    bias = -0.5 * jnp.sum(grouped * grouped, axis=1, keepdims=True)
    b_parts = [jnp.broadcast_to(b.astype(F32), grouped.shape) for b in split3(bias)]
    row = lax.broadcasted_iota(jnp.int32, grouped.shape, 1)
    extra = jnp.where(row == 3, 1.0, 0.0)
    for k in range(3):
        extra = jnp.where(row == k, b_parts[k], extra)
    c_parts = [c.astype(F32).reshape(GROUPS, SUB, CODES) for c in split3(cb)]
    packed = jnp.concatenate(c_parts + [extra], axis=1)
    cp3[...] = packed.reshape(8, 64, CODES).astype(BF16)
    for g in range(4):
        lhs_f[g] = packed[4 * g:4 * g + 4].reshape(TILE, CODES).T.astype(BF16)

    lane = lax.broadcasted_iota(jnp.int32, (TILE, 4 * TILE), 1)
    source = lax.broadcasted_iota(jnp.int32, (TILE, 4 * TILE), 0)
    inner_lane = lane % 32
    select = jnp.where(
        (source == (lane // 32) * SUB + lane % SUB) & (inner_lane < 24), 1.0, 0.0
    ).astype(BF16)
    tail_ones = jnp.where(
        (inner_lane[0:1] >= 24) & (inner_lane[0:1] < 27), 1.0, 0.0
    )
    pack_lane = lax.broadcasted_iota(jnp.int32, (1, TILE), 1) // 32

    def pack_mask(j):
        return jnp.where(pack_lane == j, 1.0, 0.0).astype(BF16)

    def pack_rows(h):
        packs = (dot(xtb[h], select, NN) + tail_ones).astype(BF16)
        for g in range(4):
            xpack[g] = packs[:, TILE * g:TILE * g + TILE]

    def half_lanes(h):
        return pl.ds(pl.multiple_of(h * 128, 128), 128)

    def logits_of(v):
        g, j = quo(v, 2), 2 * rem(v, 2)
        xp = xpack[g]
        rhs = jnp.concatenate([xp * pack_mask(j), xp * pack_mask(j + 1)], axis=0)
        raw[...] = dot(lhs_f[g], rhs, NT)

    def weigh(h, v):
        lanes = half_lanes(h)
        logits = raw[...]
        e1, e2 = split2(jnp.exp(logits - jnp.max(logits, axis=0, keepdims=True)))
        for k in range(2):
            a1b[2 * v + k, :, lanes] = e1[:, 128 * k:128 * k + 128]
            a2b[2 * v + k, :, lanes] = e2[:, 128 * k:128 * k + 128]

    def rebuild(h, v):
        lanes = half_lanes(h)
        got = sum(
            dot(cp3[v], jnp.concatenate([b[2 * v, :, lanes], b[2 * v + 1, :, lanes]], axis=1), NN)
            for b in (a1b, a2b)
        )
        for k in range(2):
            part = got[32 * k:32 * k + 32, 128 * k:128 * k + 128]
            scale_i = 1.0 / part[27:28]
            inv[2 * v + k, :, lanes] = scale_i
            rt[2 * v + k, :, lanes] = (part[0:8] + part[8:16] + part[16:24]) * scale_i

    def assign_steps(h, first, last):
        def step(v, carry):
            rebuild(h, v)
            weigh(h, v + 1)
            logits_of(v + 2)
            return carry

        lax.fori_loop(first, last, step, 0, unroll=UNROLL)

    xtb[xl] = p_ref[:, pl.ds(col, TILE)]
    pack_rows(xl)
    def assign_open(h):
        logits_of(0)
        weigh(h, 0)
        logits_of(1)

    def assign_close(h):
        rebuild(h, 6)
        weigh(h, 7)
        rebuild(h, 7)

    assign_open(xl)
    assign_steps(xl, 0, 6)
    assign_close(xl)
    arrive(xtb.at[1 - xl], s_p)
    pack_rows(1 - xl)
    assign_open(1 - xl)
    qw[1]()
    assign_steps(1 - xl, 0, 3)
    qw[2]()
    assign_steps(1 - xl, 3, 6)
    assign_close(1 - xl)

    mine = core * 4 + u
    rbuf[mine] = rt[...].reshape(TILE, ROWS).T.astype(BF16)

    def r_slot(step):
        return core * 4 + rem(u + step, 4)

    def r_sib(step):
        return (1 - core) * 4 + rem(u + 2 + step, 4)

    s_r = block(4)
    s_rs = block(4)
    owner = u != 3
    for step in (2, 1, 3):
        push(rbuf.at[mine], rbuf.at[mine], s_r + 4 - step, dev_x(step), owner)
    push(rbuf.at[mine], rbuf.at[mine], s_rs, sibling, owner)

    xt = xtb[...].reshape(ROWS, TILE)
    xlt[...] = jnp.concatenate(
        [xt.astype(F32).T.reshape(GROUPS, SUB, ROWS), jnp.full((GROUPS, SUB, ROWS), 1.0, F32)], axis=1
    ).astype(BF16)
    code1, code2 = (c.astype(F32).reshape(GROUPS, SUB, CODES) for c in split2(cb_ref[...]))
    ones3 = jnp.where(lax.broadcasted_iota(jnp.int32, code1.shape, 1) < 3, 1.0, 0.0)
    packed_b = jnp.concatenate([code1, code2, code1, ones3], axis=1)
    for g in range(4):
        lhs_b[g] = packed_b[4 * g:4 * g + 4].reshape(TILE, CODES).T.astype(BF16)

    for step in (1, 3, 2):
        s = r_slot(step)
        real = rem(u + step, 4) != 3
        arrive(rbuf.at[s], s_r + step, real)
        push(rbuf.at[s], rbuf.at[s], s_rs + step, sibling, real)
    arrive(pbuf.at[1 - xl], s_p + 1)

    qw[3]()

    p_all = pbuf[...].reshape(ROWS, D)
    scale = float(D) ** (-0.5)
    scale2 = scale * LOG2E
    for n in range(4):
        qc = qbuf[4 * n:4 * n + 4].reshape(256, D)
        t = dot(p_all, qc, NT)
        m_t = jnp.max(t, axis=0, keepdims=True)
        tbuf[n] = t
        e_t = jnp.exp2((t - m_t) * scale2)
        ebt[n] = e_t
        s_t = jnp.sum(e_t, axis=0, keepdims=True)
        m_t = m_t * scale
        lt = m_t + jnp.log(s_t)
        sumt[n] = s_t
        for k in range(2):
            mloc[2 * n + k:2 * n + k + 1, :] = m_t[:, 128 * k:128 * k + 128]
            stat_t[me, 2 * n + k:2 * n + k + 1, :] = lt[:, 128 * k:128 * k + 128]

    def plane_send(buf, base):
        for a, b in FAR_FIRST:
            push(buf.at[me], buf.at[me], base + (rem(4 - a, 4)) * 4 + rem(4 - b, 4), dev_yz(a, b))

    def plane_wait(buf, base):
        for a, b in FAR_FIRST:
            arrive(buf.at[(rem(y + a, 4)) * 4 + rem(z + b, 4)], base + a * 4 + b)

    s_ta = block(16)
    plane_send(stat_t, s_ta)
    for step in (0, 1, 3, 2):
        arrive(rbuf.at[r_sib(step)], s_rs + step, rem(u + 2 + step, 4) != 3)

    r_all = jnp.concatenate([rbuf[k] for k in (0, 1, 2, 4, 5, 6)], axis=1)
    for n in range(4):
        qc = qbuf[4 * n:4 * n + 4].reshape(256, D)
        s = dot(r_all, qc, NT)
        m_s = jnp.max(s, axis=0, keepdims=True)
        e_s = jnp.exp2((s - m_s) * scale2)
        ebs[n] = e_s
        m_s = m_s * scale
        ls = m_s + jnp.log(jnp.sum(e_s, axis=0, keepdims=True))
        cross = jnp.sum(ebt[n] * (tbuf[n] - s), axis=0, keepdims=True) * scale / sumt[n]
        for k in range(2):
            r = 2 * n + k
            mloc[8 + r:9 + r, :] = m_s[:, 128 * k:128 * k + 128]
            stat[me, r:r + 1, :] = ls[:, 128 * k:128 * k + 128]
            stat[me, 8 + r:9 + r, :] = cross[:, 128 * k:128 * k + 128]

    s_st = block(16)
    plane_send(stat, s_st)
    plane_wait(stat_t, s_ta)
    lt = stat_t[...]
    plane_wait(stat, s_st)
    ls, cx = stat[:, 0:8], stat[:, 8:16]
    top_t = jnp.max(lt, axis=0)
    top_s = jnp.max(ls, axis=0)
    big_t = top_t + jnp.log(jnp.sum(jnp.exp(lt - top_t[None]), axis=0))
    big_s = top_s + jnp.log(jnp.sum(jnp.exp(ls - top_s[None]), axis=0))
    cross = jnp.sum(jnp.exp(lt - big_t[None]) * cx, axis=0)
    divb[xl] = cross - big_t + big_s
    s_d = block(1)
    push(divb.at[xl], divb.at[xl], s_d, dev(x + 1 - 2 * xl, y, z, core))
    weight = (PB * 32 / 64.0) * scale
    f_t = jnp.exp(mloc[0:8, :] - big_t) * weight
    f_s = jnp.exp(mloc[8:16, :] - big_s) * weight

    grads = []
    for n in range(4):
        for k in range(2):
            r = 2 * n + k
            cols = slice(128 * k, 128 * k + 128)
            diff = ebs[n, :, cols] * f_s[r:r + 1] - ebt[n, :, cols] * f_t[r:r + 1]
            grads.append(diff.astype(BF16))
    grad_scores = jnp.concatenate(grads, axis=1)

    def partial(group, first, tiles):
        at = pl.multiple_of(group * 384 + first * TILE, TILE)
        return dot(grad_scores, qbuf[:, :, pl.ds(at, TILE * tiles)].reshape(QN, TILE * tiles), NN)

    s_g = block(3)
    for group, dest in ((1 - core, gsrc), (core, gown)):
        two = partial(group, 0, 2)
        dest[0] = two[:, :TILE]
        dest[1] = two[:, TILE:]
        if dest is gsrc:
            push(gsrc.at[0], gsib.at[0], s_g, sibling)
            push(gsrc.at[1], gsib.at[1], s_g + 1, sibling)
        dest[2] = partial(group, 2, 1)
        if dest is gsrc:
            push(gsrc.at[2], gsib.at[2], s_g + 2, sibling)

    s_1 = block(2)
    s_2 = block(4)

    def half(n):
        return pl.ds(128 * n, 128)

    def near(step):
        return jnp.minimum(rem(u + step, 4), 2)

    for k in range(3):
        arrive(gsib.at[k], s_g + k)
        gown[k] = gown[k] + gsib[k]
    for part, to in ((0, right), (1, left)):
        push(gown.at[near(2), half(part), :], rs1.at[part], s_1 + part, to, rem(u + 2, 4) != 3)
    for part, to, step in ((0, right, 1), (1, left, 3)):
        push(
            gown.at[near(step), half(1 - part), :], rs2.at[part, half(1 - part), :],
            s_2 + 2 * part, to, rem(u + step, 4) != 3,
        )
    for part, to, step in ((0, right, 1), (1, left, 3)):
        ok = rem(u + step, 4) != 3
        arrive(rs1.at[part], s_1 + part, ok)
        rs2s[part] = gown[near(step), half(part), :] + rs1[part]
        push(rs2s.at[part], rs2.at[part, half(part), :], s_2 + 2 * part + 1, to, ok)
    for part in range(2):
        arrive(rs2.at[part, half(1 - part), :], s_2 + 2 * part, owner)
        arrive(rs2.at[part, half(part), :], s_2 + 2 * part + 1, owner)
    s_c = block(64)
    s_o = block(1)
    first_c = len(sends)
    sends.extend([None] * 64)

    def plane_order(n):
        y_n = rem(y + rem(n, 4), 4)
        return y_n * 4 + rem(y_n + quo(n, 4), 4)

    def piece_copy(n, step):
        other = plane_order(n)
        who, slot, sem = core, u, s_c + 16 * u + me
        if step == 0:
            own = 1 - jnp.minimum(jnp.abs(other - me), 1)
            who = core + own * (1 - 2 * core)
            slot = u + own * (3 - u)
            sem = sem + own * (s_o - sem)
        return pltpu.make_async_remote_copy(
            src_ref=dcs.at[other], dst_ref=dcr.at[slot, me],
            send_sem=send_sem.at[first_c + 4 * n + step], recv_sem=recv_sem.at[sem],
            device_id=dev(rem(x + step, 4), quo(other, 4), rem(other, 4), who), device_id_type=MESH,
        )

    def piece_send(n):
        for step in (2, 1, 3, 0):
            piece_copy(n, step).start()

    def piece_sent(n, carry):
        for step in (2, 1, 3, 0):
            piece_copy(n, step).wait_send()
        return carry

    def diff_of(n):
        i = plane_order(n)
        p, j = quo(i, 4), rem(i, 4)
        return dot(lhs_b[p], gpack[p] * pack_mask(j), NT)

    def differ(n, diff):
        i = plane_order(n)
        d1, d2 = split2((a1b[i].astype(F32) + a2b[i].astype(F32)) * diff)
        dbuf[0] = d1
        dbuf[1] = d2

    def contract(n):
        i = plane_order(n)
        ow = dot(gl[i], a1b[i], NT) + dot(gl[i], a2b[i], NT)
        od = dot(xlt[i], dbuf[0], NT) + dot(xlt[i], dbuf[1], NT)
        code = cb_ref[pl.ds(pl.multiple_of(SUB * i, SUB), SUB), :]
        dcs[i] = ow[0:8] + ow[8:16] + od[0:8] - code * od[8:16]

    def next_step(n, carry):
        diff = diff_of(n + 1)
        contract(n)
        differ(n + 1, diff)
        piece_send(n - 1)
        return carry

    @pl.when(owner)
    def _():
        g = gown[near(0)] + rs2[0] + rs2[1]
        gt = (g.T).reshape(GROUPS, SUB, ROWS) * inv[...]
        g1t, g2t = split2(gt)
        gl[...] = jnp.concatenate([g1t.astype(F32), g2t.astype(F32)], axis=1).astype(BF16)
        inner = -jnp.sum(gt * rt[...], axis=1, keepdims=True)
        t_parts = [jnp.broadcast_to(t.astype(F32), gt.shape) for t in split3(inner)]
        at_row = lax.broadcasted_iota(jnp.int32, gt.shape, 1)
        last = jnp.zeros_like(gt)
        for k in range(3):
            last = jnp.where(at_row == k, t_parts[k], last)
        g1f = g1t.astype(F32)
        stacked = jnp.concatenate([g1f, g1f, g2t.astype(F32), last], axis=1)
        for k in range(4):
            gpack[k] = stacked[4 * k:4 * k + 4].reshape(TILE, ROWS).T.astype(BF16)

        differ(0, diff_of(0))
        contract(0)
        differ(1, diff_of(1))
        lax.fori_loop(1, 15, next_step, 0)
        piece_send(14)
        contract(15)
        piece_send(15)
        dcr[u, me] = dcs[me]

    for entry in sends[:first_c]:
        guarded(entry[1], entry[0].wait_send)
    arrive(divb.at[1 - xl], s_d)
    for k in range(4):
        for h in range(2):
            div_ref[4 * k + 2 * h:4 * k + 2 * h + 2, :] = divb[h, 2 * k:2 * k + 2, :]

    for k in range(3):
        arrive(dcr.at[k, me], s_c + 16 * k + me, u != k)

    def piece_wait(n, carry):
        other = rem(me + n, 16)
        for k in range(3):
            arrive(dcr.at[k, other], s_c + 16 * k + other)
        return carry

    lax.fori_loop(1, 16, piece_wait, 0)
    arrive(dcr.at[3, me], s_o, rem(u + 2, 4) != 3)

    for k in range(3):
        out_ref[3 * core + k, me] = jnp.sum(dcr[k], axis=0)

    def trio(s, c):
        return out_ref.at[pl.ds(3 * c, 3), s]

    s_f = block(16)
    s_fs = block(16)
    for a, b in FAR_FIRST:
        push(trio(me, core), trio(me, core), s_f + me, dev_yz(a, b))
    push(trio(me, core), trio(me, core), s_fs + me, sibling)
    first_r = len(sends)
    sends.extend([None] * 16)

    def relay(n, carry):
        other = plane_order(n)

        @pl.when(other != me)
        def _():
            arrive(trio(other, core), s_f + other)
            pltpu.make_async_remote_copy(
                src_ref=trio(other, core), dst_ref=trio(other, core),
                send_sem=send_sem.at[first_r + n], recv_sem=recv_sem.at[s_fs + other],
                device_id=sibling, device_id_type=MESH,
            ).start()

        return carry

    def relay_wait(n, carry):
        other = plane_order(n)
        arrive(trio(other, 1 - core), s_fs + other)

        @pl.when(other != me)
        def _():
            pltpu.make_async_remote_copy(
                src_ref=trio(other, core), dst_ref=trio(other, core),
                send_sem=send_sem.at[first_r + n], recv_sem=recv_sem.at[s_fs + other],
                device_id=sibling, device_id_type=MESH,
            ).wait_send()

        return carry

    @pl.when(owner)
    def _():
        lax.fori_loop(0, 16, piece_sent, 0)

    lax.fori_loop(0, 16, relay, 0)
    lax.fori_loop(0, 16, relay_wait, 0)

    for entry in sends[first_c:]:
        if entry is not None:
            guarded(entry[1], entry[0].wait_send)


def local(passages, queries, codebook):
    vmem = pl.BlockSpec(memory_space=pltpu.VMEM)
    grad, divergence = pl.pallas_call(
        kernel,
        out_shape=(
            pltpu.VMEM((6, PLANE, SUB, CODES), F32),
            pltpu.VMEM((16, 128), F32),
        ),
        in_specs=[vmem, vmem, pl.BlockSpec(memory_space=pl.ANY)],
        out_specs=(vmem, vmem),
        scratch_shapes=[
            pltpu.VMEM((TILE, CODES), F32),
            pltpu.SemaphoreType.DMA,
            pltpu.VMEM((PLANE, QB, D), BF16),
            pltpu.VMEM((2, PB, D), BF16),
            pltpu.VMEM((8, ROWS, TILE), BF16),
            pltpu.VMEM((2, PB, TILE), BF16),
            pltpu.VMEM((CODES, ROWS), F32),
            pltpu.VMEM((4, PB, TILE), BF16),
            pltpu.VMEM((4, CODES, TILE), BF16),
            pltpu.VMEM((4, CODES, TILE), BF16),
            pltpu.VMEM((8, 64, CODES), BF16),
            pltpu.VMEM((GROUPS, SUB, ROWS), F32),
            pltpu.VMEM((GROUPS, 1, ROWS), F32),
            pltpu.VMEM((GROUPS, CODES, ROWS), BF16),
            pltpu.VMEM((GROUPS, CODES, ROWS), BF16),
            pltpu.VMEM((4, ROWS, 256), F32),
            pltpu.VMEM((4, ROWS, 256), F32),
            pltpu.VMEM((4, ROWS, 256), F32),
            pltpu.VMEM((4, 1, 256), F32),
            pltpu.VMEM((16, 128), F32),
            pltpu.VMEM((PLANE, 8, 128), F32),
            pltpu.VMEM((PLANE, 16, 128), F32),
            pltpu.VMEM((3, ROWS, TILE), F32),
            pltpu.VMEM((3, ROWS, TILE), F32),
            pltpu.VMEM((3, ROWS, TILE), F32),
            pltpu.VMEM((2, 128, TILE), F32),
            pltpu.VMEM((2, ROWS, TILE), F32),
            pltpu.VMEM((2, 128, TILE), F32),
            pltpu.VMEM((GROUPS, 16, ROWS), BF16),
            pltpu.VMEM((2, CODES, ROWS), BF16),
            pltpu.VMEM((GROUPS, 16, ROWS), BF16),
            pltpu.VMEM((4, ROWS, TILE), BF16),
            pltpu.VMEM((PLANE, SUB, CODES), F32),
            pltpu.VMEM((4, PLANE, SUB, CODES), F32),
            pltpu.VMEM((2, 8, 128), F32),
            pltpu.SemaphoreType.DMA((N_SEM,)),
            pltpu.SemaphoreType.DMA((240,)),
        ],
        compiler_params=pltpu.CompilerParams(
            collective_id=0, has_side_effects=True, vmem_limit_bytes=60 * 1024 * 1024
        ),
    )(passages, queries, codebook.reshape(D, CODES))
    return divergence.reshape(2048), grad.reshape(96, SUB, CODES)


def solution(mesh):
    placed = (P("corpus", None), P(("query", "corpus"), None), P())
    return jax.shard_map(
        local, mesh=mesh, in_specs=placed, out_specs=(P("query"), P()), check_vma=False
    )
```

```python
import functools

import jax
import jax.numpy as jnp
from jax import lax
from jax.experimental import pallas as pl
from jax.experimental.pallas import tpu as pltpu
from jax.sharding import PartitionSpec as P

MESH = pl.DeviceIdType.MESH
F32 = jnp.float32
BF16 = jnp.bfloat16
NT = (((1,), (1,)), ((), ()))
NN = (((1,), (0,)), ((), ()))

D = 768
SUB = 8
CODES = 256
QB = 64
PB = 128
PLANE = 16
TILE = 128
GROUPS = 16
ROWS = 256
QN = 1024
UNROLL = 1
N_SEM = 224
LOG2E = 1.4426950408889634
FAR_FIRST = [(2, 2), (2, 1), (2, 3), (1, 2), (3, 2), (1, 1), (1, 3), (3, 1), (3, 3), (2, 0), (0, 2), (1, 0), (3, 0), (0, 1), (0, 3)]


def rem(a, b):
    return a % b if isinstance(a, int) else lax.rem(a, b)


def quo(a, b):
    return a // b if isinstance(a, int) else lax.div(a, b)


def split3(value):
    high = value.astype(BF16)
    rest = value - high.astype(F32)
    mid = rest.astype(BF16)
    low = (rest - mid.astype(F32)).astype(BF16)
    return high, mid, low


def split2(value):
    high = value.astype(BF16)
    low = (value - high.astype(F32)).astype(BF16)
    return high, low


def dot(a, b, dims):
    return lax.dot_general(a, b, dims, preferred_element_type=F32)


def kernel(
    p_ref, q_ref, cb_hbm,
    out_ref, div_ref,
    cb_ref, cb_sem,
    qbuf, pbuf, rbuf,
    xtb, raw, xpack, lhs_f, lhs_b, cp3, rt, inv, a1b, a2b,
    tbuf, ebt, ebs, sumt, mloc, stat_t, stat,
    gown, gsib, gsrc, rs1, rs2, rs2s,
    gl, dbuf, xlt, gpack, dcs, dcr, divb,
    send_sem, recv_sem,
):
    qi = lax.axis_index("query")
    ci = lax.axis_index("corpus")
    xh, core = quo(qi, 2), rem(qi, 2)
    y, xl, z = quo(ci, 8), rem(quo(ci, 4), 2), rem(ci, 4)
    x = xh * 2 + xl
    u = rem(x + 4 - 2 * core, 4)

    def dev(x_, y_, z_, core_):
        return (quo(x_, 2) * 2 + core_, y_ * 8 + rem(x_, 2) * 4 + z_)

    def dev_x(step, core_=None):
        return dev(rem(x + step, 4), y, z, core if core_ is None else core_)

    def dev_yz(dy, dz):
        return dev(x, rem(y + dy, 4), rem(z + dz, 4), core)

    sibling = dev(x, y, z, 1 - core)
    left, right = dev_x(3), dev_x(1)

    sends = []
    count = [0]

    def guarded(cond, action):
        if cond is None:
            action()
        else:
            pl.when(cond)(action)

    def push(src, dst, index, device, cond=None):
        copy = pltpu.make_async_remote_copy(
            src_ref=src, dst_ref=dst, send_sem=send_sem.at[len(sends)],
            recv_sem=recv_sem.at[index], device_id=device, device_id_type=MESH,
        )
        guarded(cond, copy.start)
        sends.append((copy, cond))

    def arrive(dst, index, cond=None):
        guarded(cond, pltpu.make_async_remote_copy(
            src_ref=dst, dst_ref=dst, send_sem=send_sem.at[0],
            recv_sem=recv_sem.at[index], device_id=sibling, device_id_type=MESH,
        ).wait_recv)

    def block(n):
        first = count[0]
        count[0] += n
        return first

    def tile_col(u_):
        return pl.multiple_of((3 * core + jnp.minimum(u_, 2)) * TILE, TILE)

    col = tile_col(u)
    me = y * 4 + z
    fetch = pltpu.make_async_copy(cb_hbm.at[pl.ds(col, TILE), :], cb_ref, cb_sem.at[0])
    fetch_x = pltpu.make_async_copy(p_ref.at[:, pl.ds(col, TILE)], xtb.at[xl], cb_sem.at[1])
    fetch_p = pltpu.make_async_copy(p_ref, pbuf.at[xl], cb_sem.at[2])
    fetch_q = pltpu.make_async_copy(q_ref, qbuf.at[me], cb_sem.at[3])
    for copy in (fetch, fetch_x, fetch_p, fetch_q):
        copy.start()

    barrier = pltpu.get_barrier_semaphore()
    peers = [left, right, sibling]
    peers += [dev_yz(a, b) for a, b in ((0, 1), (0, 3), (0, 2), (1, 0), (3, 0), (2, 0))]
    for peer in peers:
        pl.semaphore_signal(barrier, inc=1, device_id=peer, device_id_type=MESH)


    pl.semaphore_wait(barrier, len(peers))

    def gather_plane(own, piece_of, base):
        def rel(h, a, b):
            return (a, b) if h == 0 else (b, a)

        def slot(dy, dz):
            return (rem(y + dy, 4)) * 4 + rem(z + dz, 4)

        def sem(dy, dz, h, part):
            return base + (((dy % 4) * 4 + dz % 4) * 2 + h) * 2 + (part or 0)

        def send(h, a, b, part, first_axis, step):
            dy, dz = rel(h, a, b)
            sy, sz = rel(h, step, 0) if first_axis else rel(h, 0, step)
            dst = piece_of(slot(dy, dz), h, part)
            src = own(h) if (a, b) == (0, 0) else dst
            push(src, dst, sem(dy - sy, dz - sz, h, part), dev_yz(sy % 4, sz % 4))

        def wait(h, a, b, part):
            dy, dz = rel(h, a, b)
            arrive(piece_of(slot(dy, dz), h, part), sem(dy, dz, h, part))

        def wave0():
            for h in range(2):
                for step in (2, 1, 3):
                    send(h, 0, 0, None, True, step)
            for h in range(2):
                for step in (2, 1, 3):
                    send(h, 0, 0, None, False, step)

        def onward(h, a):
            wait(h, a, 0, None)
            for step in (2, 1, 3):
                send(h, a, 0, None, False, step)

        def wave1():
            for h in range(2):
                onward(h, 1)
                onward(h, 3)

        def wave2():
            for h in range(2):
                onward(h, 2)

        def wave3():
            for h in range(2):
                for b in (1, 3, 2):
                    for a in (0, 1, 3, 2):
                        wait(h, a, b, None)

        return wave0, wave1, wave2, wave3

    def q_piece(s, h, part):
        if part is None:
            return qbuf.at[s, pl.ds(32 * h, 32), :]
        return qbuf.at[s, pl.ds(32 * h + 16 * part, 16), :]

    qw = gather_plane(lambda h: q_ref.at[pl.ds(32 * h, 32), :], q_piece, block(64))
    s_p = block(2)
    x_to = rem(x + 3 + 2 * core, 4)
    p_to = dev(x_to, y, z, core)
    col_to = tile_col(rem(x_to + 4 - 2 * core, 4))
    push(p_ref.at[:, pl.ds(col_to, TILE)], xtb.at[xl], s_p, p_to)
    qw[0]()
    push(p_ref, pbuf.at[xl], s_p + 1, p_to)

    fetch.wait()
    cb = cb_ref[...]
    grouped = cb.reshape(GROUPS, SUB, CODES)
    bias = -0.5 * jnp.sum(grouped * grouped, axis=1, keepdims=True)
    b_parts = [jnp.broadcast_to(b.astype(F32), grouped.shape) for b in split3(bias)]
    row = lax.broadcasted_iota(jnp.int32, grouped.shape, 1)
    extra = jnp.where(row == 3, 1.0, 0.0)
    for k in range(3):
        extra = jnp.where(row == k, b_parts[k], extra)
    c_parts = [c.astype(F32).reshape(GROUPS, SUB, CODES) for c in split3(cb)]
    packed = jnp.concatenate(c_parts + [extra], axis=1)
    cp3[...] = packed.reshape(8, 64, CODES).astype(BF16)
    for g in range(4):
        lhs_f[g] = packed[4 * g:4 * g + 4].reshape(TILE, CODES).T.astype(BF16)

    lane = lax.broadcasted_iota(jnp.int32, (TILE, 4 * TILE), 1)
    source = lax.broadcasted_iota(jnp.int32, (TILE, 4 * TILE), 0)
    inner_lane = lane % 32
    select = jnp.where(
        (source == (lane // 32) * SUB + lane % SUB) & (inner_lane < 24), 1.0, 0.0
    ).astype(BF16)
    tail_ones = jnp.where(
        (inner_lane[0:1] >= 24) & (inner_lane[0:1] < 27), 1.0, 0.0
    )
    pack_lane = lax.broadcasted_iota(jnp.int32, (1, TILE), 1) // 32

    def pack_mask(j):
        return jnp.where(pack_lane == j, 1.0, 0.0).astype(BF16)

    def pack_rows(h):
        packs = (dot(xtb[h], select, NN) + tail_ones).astype(BF16)
        for g in range(4):
            xpack[g] = packs[:, TILE * g:TILE * g + TILE]

    def half_lanes(h):
        return pl.ds(pl.multiple_of(h * 128, 128), 128)

    def logits_of(v):
        g, j = quo(v, 2), 2 * rem(v, 2)
        xp = xpack[g]
        rhs = jnp.concatenate([xp * pack_mask(j), xp * pack_mask(j + 1)], axis=0)
        raw[...] = dot(lhs_f[g], rhs, NT)

    def weigh(h, v):
        lanes = half_lanes(h)
        logits = raw[...]
        e1, e2 = split2(jnp.exp(logits - jnp.max(logits, axis=0, keepdims=True)))
        for k in range(2):
            a1b[2 * v + k, :, lanes] = e1[:, 128 * k:128 * k + 128]
            a2b[2 * v + k, :, lanes] = e2[:, 128 * k:128 * k + 128]

    def rebuild(h, v):
        lanes = half_lanes(h)
        got = sum(
            dot(cp3[v], jnp.concatenate([b[2 * v, :, lanes], b[2 * v + 1, :, lanes]], axis=1), NN)
            for b in (a1b, a2b)
        )
        for k in range(2):
            part = got[32 * k:32 * k + 32, 128 * k:128 * k + 128]
            scale_i = 1.0 / part[27:28]
            inv[2 * v + k, :, lanes] = scale_i
            rt[2 * v + k, :, lanes] = (part[0:8] + part[8:16] + part[16:24]) * scale_i

    def assign_steps(h, first, last):
        def step(v, carry):
            rebuild(h, v)
            weigh(h, v + 1)
            logits_of(v + 2)
            return carry

        lax.fori_loop(first, last, step, 0, unroll=UNROLL)

    fetch_x.wait()
    pack_rows(xl)
    def assign_open(h):
        logits_of(0)
        weigh(h, 0)
        logits_of(1)

    def assign_close(h):
        rebuild(h, 6)
        weigh(h, 7)
        rebuild(h, 7)

    assign_open(xl)
    assign_steps(xl, 0, 6)
    assign_close(xl)
    arrive(xtb.at[1 - xl], s_p)
    pack_rows(1 - xl)
    assign_open(1 - xl)
    qw[1]()
    assign_steps(1 - xl, 0, 3)
    qw[2]()
    assign_steps(1 - xl, 3, 6)
    assign_close(1 - xl)

    mine = core * 4 + u
    rbuf[mine] = rt[...].reshape(TILE, ROWS).T.astype(BF16)

    def r_slot(step):
        return core * 4 + rem(u + step, 4)

    def r_sib(step):
        return (1 - core) * 4 + rem(u + 2 + step, 4)

    s_r = block(4)
    s_rs = block(4)
    owner = u != 3
    for step in (2, 1, 3):
        push(rbuf.at[mine], rbuf.at[mine], s_r + 4 - step, dev_x(step), owner)
    push(rbuf.at[mine], rbuf.at[mine], s_rs, sibling, owner)

    xt = xtb[...].reshape(ROWS, TILE)
    xlt[...] = jnp.concatenate(
        [xt.astype(F32).T.reshape(GROUPS, SUB, ROWS), jnp.full((GROUPS, SUB, ROWS), 1.0, F32)], axis=1
    ).astype(BF16)
    code1, code2 = (c.astype(F32).reshape(GROUPS, SUB, CODES) for c in split2(cb_ref[...]))
    ones3 = jnp.where(lax.broadcasted_iota(jnp.int32, code1.shape, 1) < 3, 1.0, 0.0)
    packed_b = jnp.concatenate([code1, code2, code1, ones3], axis=1)
    for g in range(4):
        lhs_b[g] = packed_b[4 * g:4 * g + 4].reshape(TILE, CODES).T.astype(BF16)

    for step in (1, 3, 2):
        s = r_slot(step)
        real = rem(u + step, 4) != 3
        arrive(rbuf.at[s], s_r + step, real)
        push(rbuf.at[s], rbuf.at[s], s_rs + step, sibling, real)
    arrive(pbuf.at[1 - xl], s_p + 1)
    fetch_p.wait()
    fetch_q.wait()

    qw[3]()

    p_all = pbuf[...].reshape(ROWS, D)
    scale = float(D) ** (-0.5)
    scale2 = scale * LOG2E
    for n in range(4):
        qc = qbuf[4 * n:4 * n + 4].reshape(256, D)
        t = dot(p_all, qc, NT)
        m_t = jnp.max(t, axis=0, keepdims=True)
        tbuf[n] = t
        e_t = jnp.exp2((t - m_t) * scale2)
        ebt[n] = e_t
        s_t = jnp.sum(e_t, axis=0, keepdims=True)
        m_t = m_t * scale
        lt = m_t + jnp.log(s_t)
        sumt[n] = s_t
        for k in range(2):
            mloc[2 * n + k:2 * n + k + 1, :] = m_t[:, 128 * k:128 * k + 128]
            stat_t[me, 2 * n + k:2 * n + k + 1, :] = lt[:, 128 * k:128 * k + 128]

    def plane_send(buf, base):
        for a, b in FAR_FIRST:
            push(buf.at[me], buf.at[me], base + (rem(4 - a, 4)) * 4 + rem(4 - b, 4), dev_yz(a, b))

    def plane_wait(buf, base):
        for a, b in FAR_FIRST:
            arrive(buf.at[(rem(y + a, 4)) * 4 + rem(z + b, 4)], base + a * 4 + b)

    s_ta = block(16)
    plane_send(stat_t, s_ta)
    for step in (0, 1, 3, 2):
        arrive(rbuf.at[r_sib(step)], s_rs + step, rem(u + 2 + step, 4) != 3)

    r_all = jnp.concatenate([rbuf[k] for k in (0, 1, 2, 4, 5, 6)], axis=1)
    for n in range(4):
        qc = qbuf[4 * n:4 * n + 4].reshape(256, D)
        s = dot(r_all, qc, NT)
        m_s = jnp.max(s, axis=0, keepdims=True)
        e_s = jnp.exp2((s - m_s) * scale2)
        ebs[n] = e_s
        m_s = m_s * scale
        ls = m_s + jnp.log(jnp.sum(e_s, axis=0, keepdims=True))
        cross = jnp.sum(ebt[n] * (tbuf[n] - s), axis=0, keepdims=True) * scale / sumt[n]
        for k in range(2):
            r = 2 * n + k
            mloc[8 + r:9 + r, :] = m_s[:, 128 * k:128 * k + 128]
            stat[me, r:r + 1, :] = ls[:, 128 * k:128 * k + 128]
            stat[me, 8 + r:9 + r, :] = cross[:, 128 * k:128 * k + 128]

    s_st = block(16)
    plane_send(stat, s_st)
    plane_wait(stat_t, s_ta)
    lt = stat_t[...]
    plane_wait(stat, s_st)
    ls, cx = stat[:, 0:8], stat[:, 8:16]
    top_t = jnp.max(lt, axis=0)
    top_s = jnp.max(ls, axis=0)
    big_t = top_t + jnp.log(jnp.sum(jnp.exp(lt - top_t[None]), axis=0))
    big_s = top_s + jnp.log(jnp.sum(jnp.exp(ls - top_s[None]), axis=0))
    cross = jnp.sum(jnp.exp(lt - big_t[None]) * cx, axis=0)
    divb[xl] = cross - big_t + big_s
    s_d = block(1)
    push(divb.at[xl], divb.at[xl], s_d, dev(x + 1 - 2 * xl, y, z, core))
    weight = (PB * 32 / 64.0) * scale
    f_t = jnp.exp(mloc[0:8, :] - big_t) * weight
    f_s = jnp.exp(mloc[8:16, :] - big_s) * weight

    grads = []
    for n in range(4):
        for k in range(2):
            r = 2 * n + k
            cols = slice(128 * k, 128 * k + 128)
            diff = ebs[n, :, cols] * f_s[r:r + 1] - ebt[n, :, cols] * f_t[r:r + 1]
            grads.append(diff.astype(BF16))
    grad_scores = jnp.concatenate(grads, axis=1)

    def partial(group, first, tiles):
        at = pl.multiple_of(group * 384 + first * TILE, TILE)
        return dot(grad_scores, qbuf[:, :, pl.ds(at, TILE * tiles)].reshape(QN, TILE * tiles), NN)

    s_g = block(3)
    for group, dest in ((1 - core, gsrc), (core, gown)):
        two = partial(group, 0, 2)
        dest[0] = two[:, :TILE]
        dest[1] = two[:, TILE:]
        if dest is gsrc:
            push(gsrc.at[0], gsib.at[0], s_g, sibling)
            push(gsrc.at[1], gsib.at[1], s_g + 1, sibling)
        dest[2] = partial(group, 2, 1)
        if dest is gsrc:
            push(gsrc.at[2], gsib.at[2], s_g + 2, sibling)

    s_1 = block(2)
    s_2 = block(4)

    def half(n):
        return pl.ds(128 * n, 128)

    def near(step):
        return jnp.minimum(rem(u + step, 4), 2)

    for k in range(3):
        arrive(gsib.at[k], s_g + k)
        gown[k] = gown[k] + gsib[k]
    for part, to in ((0, right), (1, left)):
        push(gown.at[near(2), half(part), :], rs1.at[part], s_1 + part, to, rem(u + 2, 4) != 3)
    for part, to, step in ((0, right, 1), (1, left, 3)):
        push(
            gown.at[near(step), half(1 - part), :], rs2.at[part, half(1 - part), :],
            s_2 + 2 * part, to, rem(u + step, 4) != 3,
        )
    for part, to, step in ((0, right, 1), (1, left, 3)):
        ok = rem(u + step, 4) != 3
        arrive(rs1.at[part], s_1 + part, ok)
        rs2s[part] = gown[near(step), half(part), :] + rs1[part]
        push(rs2s.at[part], rs2.at[part, half(part), :], s_2 + 2 * part + 1, to, ok)
    for part in range(2):
        arrive(rs2.at[part, half(1 - part), :], s_2 + 2 * part, owner)
        arrive(rs2.at[part, half(part), :], s_2 + 2 * part + 1, owner)
    s_c = block(64)
    s_o = block(1)
    first_c = len(sends)
    sends.extend([None] * 64)

    def plane_order(n):
        y_n = rem(y + rem(n, 4), 4)
        return y_n * 4 + rem(y_n + quo(n, 4), 4)

    def piece_copy(n, step):
        other = plane_order(n)
        who, slot, sem = core, u, s_c + 16 * u + me
        if step == 0:
            own = 1 - jnp.minimum(jnp.abs(other - me), 1)
            who = core + own * (1 - 2 * core)
            slot = u + own * (3 - u)
            sem = sem + own * (s_o - sem)
        return pltpu.make_async_remote_copy(
            src_ref=dcs.at[other], dst_ref=dcr.at[slot, me],
            send_sem=send_sem.at[first_c + 4 * n + step], recv_sem=recv_sem.at[sem],
            device_id=dev(rem(x + step, 4), quo(other, 4), rem(other, 4), who), device_id_type=MESH,
        )

    def piece_send(n):
        for step in (2, 1, 3, 0):
            piece_copy(n, step).start()

    def piece_sent(n, carry):
        for step in (2, 1, 3, 0):
            piece_copy(n, step).wait_send()
        return carry

    def diff_of(n):
        i = plane_order(n)
        p, j = quo(i, 4), rem(i, 4)
        return dot(lhs_b[p], gpack[p] * pack_mask(j), NT)

    def differ(n, diff):
        i = plane_order(n)
        d1, d2 = split2((a1b[i].astype(F32) + a2b[i].astype(F32)) * diff)
        dbuf[0] = d1
        dbuf[1] = d2

    def contract(n):
        i = plane_order(n)
        ow = dot(gl[i], a1b[i], NT) + dot(gl[i], a2b[i], NT)
        od = dot(xlt[i], dbuf[0], NT) + dot(xlt[i], dbuf[1], NT)
        code = cb_ref[pl.ds(pl.multiple_of(SUB * i, SUB), SUB), :]
        dcs[i] = ow[0:8] + ow[8:16] + od[0:8] - code * od[8:16]

    def next_step(n, carry):
        diff = diff_of(n + 1)
        contract(n)
        differ(n + 1, diff)
        piece_send(n - 1)
        return carry

    @pl.when(owner)
    def _():
        g = gown[near(0)] + rs2[0] + rs2[1]
        gt = (g.T).reshape(GROUPS, SUB, ROWS) * inv[...]
        g1t, g2t = split2(gt)
        gl[...] = jnp.concatenate([g1t.astype(F32), g2t.astype(F32)], axis=1).astype(BF16)
        inner = -jnp.sum(gt * rt[...], axis=1, keepdims=True)
        t_parts = [jnp.broadcast_to(t.astype(F32), gt.shape) for t in split3(inner)]
        at_row = lax.broadcasted_iota(jnp.int32, gt.shape, 1)
        last = jnp.zeros_like(gt)
        for k in range(3):
            last = jnp.where(at_row == k, t_parts[k], last)
        g1f = g1t.astype(F32)
        stacked = jnp.concatenate([g1f, g1f, g2t.astype(F32), last], axis=1)
        for k in range(4):
            gpack[k] = stacked[4 * k:4 * k + 4].reshape(TILE, ROWS).T.astype(BF16)

        differ(0, diff_of(0))
        contract(0)
        differ(1, diff_of(1))
        lax.fori_loop(1, 15, next_step, 0)
        piece_send(14)
        contract(15)
        piece_send(15)
        dcr[u, me] = dcs[me]

    for entry in sends[:first_c]:
        guarded(entry[1], entry[0].wait_send)
    arrive(divb.at[1 - xl], s_d)
    for k in range(4):
        for h in range(2):
            div_ref[4 * k + 2 * h:4 * k + 2 * h + 2, :] = divb[h, 2 * k:2 * k + 2, :]

    for k in range(3):
        arrive(dcr.at[k, me], s_c + 16 * k + me, u != k)

    def piece_wait(n, carry):
        other = rem(me + n, 16)
        for k in range(3):
            arrive(dcr.at[k, other], s_c + 16 * k + other)
        return carry

    lax.fori_loop(1, 16, piece_wait, 0)
    arrive(dcr.at[3, me], s_o, rem(u + 2, 4) != 3)

    for k in range(3):
        out_ref[3 * core + k, me] = jnp.sum(dcr[k], axis=0)

    def trio(s, c):
        return out_ref.at[pl.ds(3 * c, 3), s]

    s_f = block(16)
    s_fs = block(16)
    for a, b in FAR_FIRST:
        push(trio(me, core), trio(me, core), s_f + me, dev_yz(a, b))
    push(trio(me, core), trio(me, core), s_fs + me, sibling)
    first_r = len(sends)
    sends.extend([None] * 16)

    def relay(n, carry):
        other = plane_order(n)

        @pl.when(other != me)
        def _():
            arrive(trio(other, core), s_f + other)
            pltpu.make_async_remote_copy(
                src_ref=trio(other, core), dst_ref=trio(other, core),
                send_sem=send_sem.at[first_r + n], recv_sem=recv_sem.at[s_fs + other],
                device_id=sibling, device_id_type=MESH,
            ).start()

        return carry

    def relay_wait(n, carry):
        other = plane_order(n)
        arrive(trio(other, 1 - core), s_fs + other)

        @pl.when(other != me)
        def _():
            pltpu.make_async_remote_copy(
                src_ref=trio(other, core), dst_ref=trio(other, core),
                send_sem=send_sem.at[first_r + n], recv_sem=recv_sem.at[s_fs + other],
                device_id=sibling, device_id_type=MESH,
            ).wait_send()

        return carry

    @pl.when(owner)
    def _():
        lax.fori_loop(0, 16, piece_sent, 0)

    lax.fori_loop(0, 16, relay, 0)
    lax.fori_loop(0, 16, relay_wait, 0)

    for entry in sends[first_c:]:
        if entry is not None:
            guarded(entry[1], entry[0].wait_send)


def local(passages, queries, codebook):
    vmem = pl.BlockSpec(memory_space=pltpu.VMEM)
    grad, divergence = pl.pallas_call(
        kernel,
        out_shape=(
            pltpu.VMEM((6, PLANE, SUB, CODES), F32),
            pltpu.VMEM((16, 128), F32),
        ),
        in_specs=[pl.BlockSpec(memory_space=pl.ANY)] * 3,
        out_specs=(vmem, vmem),
        scratch_shapes=[
            pltpu.VMEM((TILE, CODES), F32),
            pltpu.SemaphoreType.DMA((4,)),
            pltpu.VMEM((PLANE, QB, D), BF16),
            pltpu.VMEM((2, PB, D), BF16),
            pltpu.VMEM((8, ROWS, TILE), BF16),
            pltpu.VMEM((2, PB, TILE), BF16),
            pltpu.VMEM((CODES, ROWS), F32),
            pltpu.VMEM((4, PB, TILE), BF16),
            pltpu.VMEM((4, CODES, TILE), BF16),
            pltpu.VMEM((4, CODES, TILE), BF16),
            pltpu.VMEM((8, 64, CODES), BF16),
            pltpu.VMEM((GROUPS, SUB, ROWS), F32),
            pltpu.VMEM((GROUPS, 1, ROWS), F32),
            pltpu.VMEM((GROUPS, CODES, ROWS), BF16),
            pltpu.VMEM((GROUPS, CODES, ROWS), BF16),
            pltpu.VMEM((4, ROWS, 256), F32),
            pltpu.VMEM((4, ROWS, 256), F32),
            pltpu.VMEM((4, ROWS, 256), F32),
            pltpu.VMEM((4, 1, 256), F32),
            pltpu.VMEM((16, 128), F32),
            pltpu.VMEM((PLANE, 8, 128), F32),
            pltpu.VMEM((PLANE, 16, 128), F32),
            pltpu.VMEM((3, ROWS, TILE), F32),
            pltpu.VMEM((3, ROWS, TILE), F32),
            pltpu.VMEM((3, ROWS, TILE), F32),
            pltpu.VMEM((2, 128, TILE), F32),
            pltpu.VMEM((2, ROWS, TILE), F32),
            pltpu.VMEM((2, 128, TILE), F32),
            pltpu.VMEM((GROUPS, 16, ROWS), BF16),
            pltpu.VMEM((2, CODES, ROWS), BF16),
            pltpu.VMEM((GROUPS, 16, ROWS), BF16),
            pltpu.VMEM((4, ROWS, TILE), BF16),
            pltpu.VMEM((PLANE, SUB, CODES), F32),
            pltpu.VMEM((4, PLANE, SUB, CODES), F32),
            pltpu.VMEM((2, 8, 128), F32),
            pltpu.SemaphoreType.DMA((N_SEM,)),
            pltpu.SemaphoreType.DMA((240,)),
        ],
        compiler_params=pltpu.CompilerParams(
            collective_id=0, has_side_effects=True, vmem_limit_bytes=60 * 1024 * 1024
        ),
    )(passages, queries, codebook.reshape(D, CODES))
    return divergence.reshape(2048), grad.reshape(96, SUB, CODES)


def solution(mesh):
    placed = (P("corpus", None), P(("query", "corpus"), None), P())
    return jax.shard_map(
        local, mesh=mesh, in_specs=placed, out_specs=(P("query"), P()), check_vma=False
    )
```

```python
import functools

import jax
import jax.numpy as jnp
from jax import lax
from jax.experimental import pallas as pl
from jax.experimental.pallas import tpu as pltpu
from jax.sharding import PartitionSpec as P

MESH = pl.DeviceIdType.MESH
F32 = jnp.float32
BF16 = jnp.bfloat16
NT = (((1,), (1,)), ((), ()))
NN = (((1,), (0,)), ((), ()))

D = 768
SUB = 8
CODES = 256
QB = 64
PB = 128
PLANE = 16
TILE = 128
GROUPS = 16
ROWS = 256
QN = 1024
UNROLL = 1
N_SEM = 224
LOG2E = 1.4426950408889634
FAR_FIRST = [(2, 2), (2, 1), (2, 3), (1, 2), (3, 2), (1, 1), (1, 3), (3, 1), (3, 3), (2, 0), (0, 2), (1, 0), (3, 0), (0, 1), (0, 3)]


def rem(a, b):
    return a % b if isinstance(a, int) else lax.rem(a, b)


def quo(a, b):
    return a // b if isinstance(a, int) else lax.div(a, b)


def split3(value):
    high = value.astype(BF16)
    rest = value - high.astype(F32)
    mid = rest.astype(BF16)
    low = (rest - mid.astype(F32)).astype(BF16)
    return high, mid, low


def split2(value):
    high = value.astype(BF16)
    low = (value - high.astype(F32)).astype(BF16)
    return high, low


def dot(a, b, dims):
    return lax.dot_general(a, b, dims, preferred_element_type=F32)


def kernel(
    p_ref, q_ref, cb_hbm,
    out_ref, div_ref,
    cb_ref, cb_sem,
    qbuf, pbuf, rbuf,
    xtb, raw, xpack, lhs_f, lhs_b, cp3, rt, inv, a1b, a2b,
    tbuf, ebt, ebs, sumt, mloc, stat_t, stat,
    gown, gsib, gsrc, rs1, rs2, rs2s,
    gl, dbuf, xlt, gpack, dcs, dcr, divb,
    send_sem, recv_sem,
):
    qi = lax.axis_index("query")
    ci = lax.axis_index("corpus")
    xh, core = quo(qi, 2), rem(qi, 2)
    y, xl, z = quo(ci, 8), rem(quo(ci, 4), 2), rem(ci, 4)
    x = xh * 2 + xl
    u = rem(x + 4 - 2 * core, 4)

    def dev(x_, y_, z_, core_):
        return (quo(x_, 2) * 2 + core_, y_ * 8 + rem(x_, 2) * 4 + z_)

    def dev_x(step, core_=None):
        return dev(rem(x + step, 4), y, z, core if core_ is None else core_)

    def dev_yz(dy, dz):
        return dev(x, rem(y + dy, 4), rem(z + dz, 4), core)

    sibling = dev(x, y, z, 1 - core)
    left, right = dev_x(3), dev_x(1)

    sends = []
    count = [0]

    def guarded(cond, action):
        if cond is None:
            action()
        else:
            pl.when(cond)(action)

    def push(src, dst, index, device, cond=None):
        copy = pltpu.make_async_remote_copy(
            src_ref=src, dst_ref=dst, send_sem=send_sem.at[len(sends)],
            recv_sem=recv_sem.at[index], device_id=device, device_id_type=MESH,
        )
        guarded(cond, copy.start)
        sends.append((copy, cond))

    def arrive(dst, index, cond=None):
        guarded(cond, pltpu.make_async_remote_copy(
            src_ref=dst, dst_ref=dst, send_sem=send_sem.at[0],
            recv_sem=recv_sem.at[index], device_id=sibling, device_id_type=MESH,
        ).wait_recv)

    def block(n):
        first = count[0]
        count[0] += n
        return first

    def tile_col(u_):
        return pl.multiple_of((3 * core + jnp.minimum(u_, 2)) * TILE, TILE)

    col = tile_col(u)
    me = y * 4 + z
    fetch = pltpu.make_async_copy(cb_hbm.at[pl.ds(col, TILE), :], cb_ref, cb_sem.at[0])
    fetch_x = pltpu.make_async_copy(p_ref.at[:, pl.ds(col, TILE)], xtb.at[xl], cb_sem.at[1])
    fetch_p = pltpu.make_async_copy(p_ref, pbuf.at[xl], cb_sem.at[2])
    fetch_q = pltpu.make_async_copy(q_ref, qbuf.at[me], cb_sem.at[3])
    for copy in (fetch, fetch_x, fetch_p, fetch_q):
        copy.start()

    barrier = pltpu.get_barrier_semaphore()
    peers = [left, right, sibling]
    peers += [dev_yz(a, b) for a, b in ((0, 1), (0, 3), (0, 2), (1, 0), (3, 0), (2, 0))]
    for peer in peers:
        pl.semaphore_signal(barrier, inc=1, device_id=peer, device_id_type=MESH)


    pl.semaphore_wait(barrier, len(peers))

    def gather_plane(own, piece_of, base):
        def rel(h, a, b):
            return (a, b) if h == 0 else (b, a)

        def slot(dy, dz):
            return (rem(y + dy, 4)) * 4 + rem(z + dz, 4)

        def sem(dy, dz, h, part):
            return base + (((dy % 4) * 4 + dz % 4) * 2 + h) * 2 + (part or 0)

        def send(h, a, b, part, first_axis, step):
            dy, dz = rel(h, a, b)
            sy, sz = rel(h, step, 0) if first_axis else rel(h, 0, step)
            dst = piece_of(slot(dy, dz), h, part)
            src = own(h) if (a, b) == (0, 0) else dst
            push(src, dst, sem(dy - sy, dz - sz, h, part), dev_yz(sy % 4, sz % 4))

        def wait(h, a, b, part):
            dy, dz = rel(h, a, b)
            arrive(piece_of(slot(dy, dz), h, part), sem(dy, dz, h, part))

        def wave0():
            for h in range(2):
                for step in (2, 1, 3):
                    send(h, 0, 0, None, True, step)
            for h in range(2):
                for step in (2, 1, 3):
                    send(h, 0, 0, None, False, step)

        def onward(h, a):
            wait(h, a, 0, None)
            for step in (2, 1, 3):
                send(h, a, 0, None, False, step)

        def wave1():
            for h in range(2):
                onward(h, 1)
                onward(h, 3)

        def wave2():
            for h in range(2):
                onward(h, 2)

        def wave3():
            for h in range(2):
                for b in (1, 3, 2):
                    for a in (0, 1, 3, 2):
                        wait(h, a, b, None)

        return wave0, wave1, wave2, wave3

    def q_piece(s, h, part):
        if part is None:
            return qbuf.at[s, pl.ds(32 * h, 32), :]
        return qbuf.at[s, pl.ds(32 * h + 16 * part, 16), :]

    qw = gather_plane(lambda h: q_ref.at[pl.ds(32 * h, 32), :], q_piece, block(64))
    s_p = block(2)
    x_to = rem(x + 3 + 2 * core, 4)
    p_to = dev(x_to, y, z, core)
    col_to = tile_col(rem(x_to + 4 - 2 * core, 4))
    push(p_ref.at[:, pl.ds(col_to, TILE)], xtb.at[xl], s_p, p_to)
    qw[0]()
    push(p_ref, pbuf.at[xl], s_p + 1, p_to)

    fetch.wait()
    cb = cb_ref[...]
    grouped = cb.reshape(GROUPS, SUB, CODES)
    bias = -0.5 * jnp.sum(grouped * grouped, axis=1, keepdims=True)
    b_parts = [jnp.broadcast_to(b.astype(F32), grouped.shape) for b in split3(bias)]
    row = lax.broadcasted_iota(jnp.int32, grouped.shape, 1)
    extra = jnp.where(row == 3, 1.0, 0.0)
    for k in range(3):
        extra = jnp.where(row == k, b_parts[k], extra)
    c_parts = [c.astype(F32).reshape(GROUPS, SUB, CODES) for c in split3(cb)]
    packed = jnp.concatenate(c_parts + [extra], axis=1)
    cp3[...] = packed.reshape(8, 64, CODES).astype(BF16)
    for g in range(4):
        lhs_f[g] = packed[4 * g:4 * g + 4].reshape(TILE, CODES).T.astype(BF16)

    lane = lax.broadcasted_iota(jnp.int32, (TILE, 4 * TILE), 1)
    source = lax.broadcasted_iota(jnp.int32, (TILE, 4 * TILE), 0)
    inner_lane = lane % 32
    select = jnp.where(
        (source == (lane // 32) * SUB + lane % SUB) & (inner_lane < 24), 1.0, 0.0
    ).astype(BF16)
    tail_ones = jnp.where(
        (inner_lane[0:1] >= 24) & (inner_lane[0:1] < 27), 1.0, 0.0
    )
    pack_lane = lax.broadcasted_iota(jnp.int32, (1, TILE), 1) // 32

    def pack_mask(j):
        return jnp.where(pack_lane == j, 1.0, 0.0).astype(BF16)

    def pack_rows(h):
        packs = (dot(xtb[h], select, NN) + tail_ones).astype(BF16)
        for g in range(4):
            xpack[g] = packs[:, TILE * g:TILE * g + TILE]

    def half_lanes(h):
        return pl.ds(pl.multiple_of(h * 128, 128), 128)

    def logits_of(v):
        g, j = quo(v, 2), 2 * rem(v, 2)
        xp = xpack[g]
        rhs = jnp.concatenate([xp * pack_mask(j), xp * pack_mask(j + 1)], axis=0)
        raw[...] = dot(lhs_f[g], rhs, NT)

    def weigh(h, v):
        lanes = half_lanes(h)
        logits = raw[...]
        e1, e2 = split2(jnp.exp(logits - jnp.max(logits, axis=0, keepdims=True)))
        for k in range(2):
            a1b[2 * v + k, :, lanes] = e1[:, 128 * k:128 * k + 128]
            a2b[2 * v + k, :, lanes] = e2[:, 128 * k:128 * k + 128]

    def rebuild(h, v):
        lanes = half_lanes(h)
        got = sum(
            dot(cp3[v], jnp.concatenate([b[2 * v, :, lanes], b[2 * v + 1, :, lanes]], axis=1), NN)
            for b in (a1b, a2b)
        )
        for k in range(2):
            part = got[32 * k:32 * k + 32, 128 * k:128 * k + 128]
            scale_i = 1.0 / part[27:28]
            inv[2 * v + k, :, lanes] = scale_i
            rt[2 * v + k, :, lanes] = (part[0:8] + part[8:16] + part[16:24]) * scale_i

    def assign_steps(h, first, last):
        def step(v, carry):
            rebuild(h, v)
            weigh(h, v + 1)
            logits_of(v + 2)
            return carry

        lax.fori_loop(first, last, step, 0, unroll=UNROLL)

    fetch_x.wait()
    pack_rows(xl)
    def assign_open(h):
        logits_of(0)
        weigh(h, 0)
        logits_of(1)

    def assign_close(h):
        rebuild(h, 6)
        weigh(h, 7)
        rebuild(h, 7)

    assign_open(xl)
    assign_steps(xl, 0, 6)
    assign_close(xl)
    arrive(xtb.at[1 - xl], s_p)
    pack_rows(1 - xl)
    assign_open(1 - xl)
    qw[1]()
    assign_steps(1 - xl, 0, 3)
    qw[2]()
    assign_steps(1 - xl, 3, 6)
    assign_close(1 - xl)

    mine = core * 4 + u
    rbuf[mine] = rt[...].reshape(TILE, ROWS).T.astype(BF16)

    def r_slot(step):
        return core * 4 + rem(u + step, 4)

    def r_sib(step):
        return (1 - core) * 4 + rem(u + 2 + step, 4)

    s_r = block(4)
    s_rs = block(4)
    owner = u != 3
    for step in (2, 1, 3):
        push(rbuf.at[mine], rbuf.at[mine], s_r + 4 - step, dev_x(step), owner)
    push(rbuf.at[mine], rbuf.at[mine], s_rs, sibling, owner)

    xt = xtb[...].reshape(ROWS, TILE)
    xlt[...] = jnp.concatenate(
        [xt.astype(F32).T.reshape(GROUPS, SUB, ROWS), jnp.full((GROUPS, SUB, ROWS), 1.0, F32)], axis=1
    ).astype(BF16)
    code1, code2 = (c.astype(F32).reshape(GROUPS, SUB, CODES) for c in split2(cb_ref[...]))
    ones3 = jnp.where(lax.broadcasted_iota(jnp.int32, code1.shape, 1) < 3, 1.0, 0.0)
    packed_b = jnp.concatenate([code1, code2, code1, ones3], axis=1)
    for g in range(4):
        lhs_b[g] = packed_b[4 * g:4 * g + 4].reshape(TILE, CODES).T.astype(BF16)

    for step in (1, 3, 2):
        s = r_slot(step)
        real = rem(u + step, 4) != 3
        arrive(rbuf.at[s], s_r + step, real)
        push(rbuf.at[s], rbuf.at[s], s_rs + step, sibling, real)
    arrive(pbuf.at[1 - xl], s_p + 1)
    fetch_p.wait()
    fetch_q.wait()

    qw[3]()

    p_all = pbuf[...].reshape(ROWS, D)
    scale = float(D) ** (-0.5)
    scale2 = scale * LOG2E
    for n in range(4):
        qc = qbuf[4 * n:4 * n + 4].reshape(256, D)
        t = dot(p_all, qc, NT)
        m_t = jnp.max(t, axis=0, keepdims=True)
        tbuf[n] = t
        e_t = jnp.exp2((t - m_t) * scale2)
        ebt[n] = e_t
        s_t = jnp.sum(e_t, axis=0, keepdims=True)
        m_t = m_t * scale
        lt = m_t + jnp.log(s_t)
        sumt[n] = s_t
        for k in range(2):
            mloc[2 * n + k:2 * n + k + 1, :] = m_t[:, 128 * k:128 * k + 128]
            stat_t[me, 2 * n + k:2 * n + k + 1, :] = lt[:, 128 * k:128 * k + 128]

    def plane_send(buf, base):
        for a, b in FAR_FIRST:
            push(buf.at[me], buf.at[me], base + (rem(4 - a, 4)) * 4 + rem(4 - b, 4), dev_yz(a, b))

    def plane_wait(buf, base):
        for a, b in FAR_FIRST:
            arrive(buf.at[(rem(y + a, 4)) * 4 + rem(z + b, 4)], base + a * 4 + b)

    s_ta = block(16)
    plane_send(stat_t, s_ta)
    for step in (0, 1, 3, 2):
        arrive(rbuf.at[r_sib(step)], s_rs + step, rem(u + 2 + step, 4) != 3)

    s_st = block(32)
    r_all = jnp.concatenate([rbuf[k] for k in (0, 1, 2, 4, 5, 6)], axis=1)
    for n in range(4):
        qc = qbuf[4 * n:4 * n + 4].reshape(256, D)
        s = dot(r_all, qc, NT)
        m_s = jnp.max(s, axis=0, keepdims=True)
        e_s = jnp.exp2((s - m_s) * scale2)
        ebs[n] = e_s
        m_s = m_s * scale
        ls = m_s + jnp.log(jnp.sum(e_s, axis=0, keepdims=True))
        cross = jnp.sum(ebt[n] * (tbuf[n] - s), axis=0, keepdims=True) * scale / sumt[n]
        for k in range(2):
            r = 2 * n + k
            mloc[8 + r:9 + r, :] = m_s[:, 128 * k:128 * k + 128]
            q = 2 * (n % 2) + k
            stat[n // 2, me, q:q + 1, :] = ls[:, 128 * k:128 * k + 128]
            stat[n // 2, me, 4 + q:5 + q, :] = cross[:, 128 * k:128 * k + 128]
        if n % 2:
            plane_send(stat.at[n // 2], s_st + 16 * (n // 2))

    plane_wait(stat_t, s_ta)
    lt = stat_t[...]
    plane_wait(stat.at[0], s_st)
    plane_wait(stat.at[1], s_st + 16)
    ls = jnp.concatenate([stat[0, :, 0:4], stat[1, :, 0:4]], axis=1)
    cx = jnp.concatenate([stat[0, :, 4:8], stat[1, :, 4:8]], axis=1)
    top_t = jnp.max(lt, axis=0)
    top_s = jnp.max(ls, axis=0)
    big_t = top_t + jnp.log(jnp.sum(jnp.exp(lt - top_t[None]), axis=0))
    big_s = top_s + jnp.log(jnp.sum(jnp.exp(ls - top_s[None]), axis=0))
    cross = jnp.sum(jnp.exp(lt - big_t[None]) * cx, axis=0)
    divb[xl] = cross - big_t + big_s
    s_d = block(1)
    push(divb.at[xl], divb.at[xl], s_d, dev(x + 1 - 2 * xl, y, z, core))
    weight = (PB * 32 / 64.0) * scale
    f_t = jnp.exp(mloc[0:8, :] - big_t) * weight
    f_s = jnp.exp(mloc[8:16, :] - big_s) * weight

    grads = []
    for n in range(4):
        for k in range(2):
            r = 2 * n + k
            cols = slice(128 * k, 128 * k + 128)
            diff = ebs[n, :, cols] * f_s[r:r + 1] - ebt[n, :, cols] * f_t[r:r + 1]
            grads.append(diff.astype(BF16))
    grad_scores = jnp.concatenate(grads, axis=1)

    def partial(group, first, tiles):
        at = pl.multiple_of(group * 384 + first * TILE, TILE)
        return dot(grad_scores, qbuf[:, :, pl.ds(at, TILE * tiles)].reshape(QN, TILE * tiles), NN)

    s_g = block(3)
    for group, dest in ((1 - core, gsrc), (core, gown)):
        two = partial(group, 0, 2)
        dest[0] = two[:, :TILE]
        dest[1] = two[:, TILE:]
        if dest is gsrc:
            push(gsrc.at[0], gsib.at[0], s_g, sibling)
            push(gsrc.at[1], gsib.at[1], s_g + 1, sibling)
        dest[2] = partial(group, 2, 1)
        if dest is gsrc:
            push(gsrc.at[2], gsib.at[2], s_g + 2, sibling)

    s_1 = block(2)
    s_2 = block(4)

    def half(n):
        return pl.ds(128 * n, 128)

    def near(step):
        return jnp.minimum(rem(u + step, 4), 2)

    for k in range(3):
        arrive(gsib.at[k], s_g + k)
        gown[k] = gown[k] + gsib[k]
    for part, to in ((0, right), (1, left)):
        push(gown.at[near(2), half(part), :], rs1.at[part], s_1 + part, to, rem(u + 2, 4) != 3)
    for part, to, step in ((0, right, 1), (1, left, 3)):
        push(
            gown.at[near(step), half(1 - part), :], rs2.at[part, half(1 - part), :],
            s_2 + 2 * part, to, rem(u + step, 4) != 3,
        )
    for part, to, step in ((0, right, 1), (1, left, 3)):
        ok = rem(u + step, 4) != 3
        arrive(rs1.at[part], s_1 + part, ok)
        rs2s[part] = gown[near(step), half(part), :] + rs1[part]
        push(rs2s.at[part], rs2.at[part, half(part), :], s_2 + 2 * part + 1, to, ok)
    for part in range(2):
        arrive(rs2.at[part, half(1 - part), :], s_2 + 2 * part, owner)
        arrive(rs2.at[part, half(part), :], s_2 + 2 * part + 1, owner)
    s_c = block(64)
    s_o = block(1)
    first_c = len(sends)
    sends.extend([None] * 64)

    def plane_order(n):
        y_n = rem(y + rem(n, 4), 4)
        return y_n * 4 + rem(y_n + quo(n, 4), 4)

    def piece_copy(n, step):
        other = plane_order(n)
        who, slot, sem = core, u, s_c + 16 * u + me
        if step == 0:
            own = 1 - jnp.minimum(jnp.abs(other - me), 1)
            who = core + own * (1 - 2 * core)
            slot = u + own * (3 - u)
            sem = sem + own * (s_o - sem)
        return pltpu.make_async_remote_copy(
            src_ref=dcs.at[other], dst_ref=dcr.at[slot, me],
            send_sem=send_sem.at[first_c + 4 * n + step], recv_sem=recv_sem.at[sem],
            device_id=dev(rem(x + step, 4), quo(other, 4), rem(other, 4), who), device_id_type=MESH,
        )

    def piece_send(n):
        for step in (2, 1, 3, 0):
            piece_copy(n, step).start()

    def piece_sent(n, carry):
        for step in (2, 1, 3, 0):
            piece_copy(n, step).wait_send()
        return carry

    def diff_of(n):
        i = plane_order(n)
        p, j = quo(i, 4), rem(i, 4)
        return dot(lhs_b[p], gpack[p] * pack_mask(j), NT)

    def differ(n, diff):
        i = plane_order(n)
        d1, d2 = split2((a1b[i].astype(F32) + a2b[i].astype(F32)) * diff)
        dbuf[0] = d1
        dbuf[1] = d2

    def contract(n):
        i = plane_order(n)
        ow = dot(gl[i], a1b[i], NT) + dot(gl[i], a2b[i], NT)
        od = dot(xlt[i], dbuf[0], NT) + dot(xlt[i], dbuf[1], NT)
        code = cb_ref[pl.ds(pl.multiple_of(SUB * i, SUB), SUB), :]
        dcs[i] = ow[0:8] + ow[8:16] + od[0:8] - code * od[8:16]

    def next_step(n, carry):
        diff = diff_of(n + 1)
        contract(n)
        differ(n + 1, diff)
        piece_send(n - 1)
        return carry

    @pl.when(owner)
    def _():
        g = gown[near(0)] + rs2[0] + rs2[1]
        gt = (g.T).reshape(GROUPS, SUB, ROWS) * inv[...]
        g1t, g2t = split2(gt)
        gl[...] = jnp.concatenate([g1t.astype(F32), g2t.astype(F32)], axis=1).astype(BF16)
        inner = -jnp.sum(gt * rt[...], axis=1, keepdims=True)
        t_parts = [jnp.broadcast_to(t.astype(F32), gt.shape) for t in split3(inner)]
        at_row = lax.broadcasted_iota(jnp.int32, gt.shape, 1)
        last = jnp.zeros_like(gt)
        for k in range(3):
            last = jnp.where(at_row == k, t_parts[k], last)
        g1f = g1t.astype(F32)
        stacked = jnp.concatenate([g1f, g1f, g2t.astype(F32), last], axis=1)
        for k in range(4):
            gpack[k] = stacked[4 * k:4 * k + 4].reshape(TILE, ROWS).T.astype(BF16)

        differ(0, diff_of(0))
        contract(0)
        differ(1, diff_of(1))
        lax.fori_loop(1, 15, next_step, 0)
        piece_send(14)
        contract(15)
        piece_send(15)
        dcr[u, me] = dcs[me]

    for entry in sends[:first_c]:
        guarded(entry[1], entry[0].wait_send)
    arrive(divb.at[1 - xl], s_d)
    for k in range(4):
        for h in range(2):
            div_ref[4 * k + 2 * h:4 * k + 2 * h + 2, :] = divb[h, 2 * k:2 * k + 2, :]

    for k in range(3):
        arrive(dcr.at[k, me], s_c + 16 * k + me, u != k)

    def piece_wait(n, carry):
        other = rem(me + n, 16)
        for k in range(3):
            arrive(dcr.at[k, other], s_c + 16 * k + other)
        return carry

    lax.fori_loop(1, 16, piece_wait, 0)
    arrive(dcr.at[3, me], s_o, rem(u + 2, 4) != 3)

    for k in range(3):
        out_ref[3 * core + k, me] = jnp.sum(dcr[k], axis=0)

    def trio(s, c):
        return out_ref.at[pl.ds(3 * c, 3), s]

    s_f = block(16)
    s_fs = block(16)
    for a, b in FAR_FIRST:
        push(trio(me, core), trio(me, core), s_f + me, dev_yz(a, b))
    push(trio(me, core), trio(me, core), s_fs + me, sibling)
    first_r = len(sends)
    sends.extend([None] * 16)

    def relay(n, carry):
        other = plane_order(n)

        @pl.when(other != me)
        def _():
            arrive(trio(other, core), s_f + other)
            pltpu.make_async_remote_copy(
                src_ref=trio(other, core), dst_ref=trio(other, core),
                send_sem=send_sem.at[first_r + n], recv_sem=recv_sem.at[s_fs + other],
                device_id=sibling, device_id_type=MESH,
            ).start()

        return carry

    def relay_wait(n, carry):
        other = plane_order(n)
        arrive(trio(other, 1 - core), s_fs + other)

        @pl.when(other != me)
        def _():
            pltpu.make_async_remote_copy(
                src_ref=trio(other, core), dst_ref=trio(other, core),
                send_sem=send_sem.at[first_r + n], recv_sem=recv_sem.at[s_fs + other],
                device_id=sibling, device_id_type=MESH,
            ).wait_send()

        return carry

    @pl.when(owner)
    def _():
        lax.fori_loop(0, 16, piece_sent, 0)

    lax.fori_loop(0, 16, relay, 0)
    lax.fori_loop(0, 16, relay_wait, 0)

    for entry in sends[first_c:]:
        if entry is not None:
            guarded(entry[1], entry[0].wait_send)


def local(passages, queries, codebook):
    vmem = pl.BlockSpec(memory_space=pltpu.VMEM)
    grad, divergence = pl.pallas_call(
        kernel,
        out_shape=(
            pltpu.VMEM((6, PLANE, SUB, CODES), F32),
            pltpu.VMEM((16, 128), F32),
        ),
        in_specs=[pl.BlockSpec(memory_space=pl.ANY)] * 3,
        out_specs=(vmem, vmem),
        scratch_shapes=[
            pltpu.VMEM((TILE, CODES), F32),
            pltpu.SemaphoreType.DMA((4,)),
            pltpu.VMEM((PLANE, QB, D), BF16),
            pltpu.VMEM((2, PB, D), BF16),
            pltpu.VMEM((8, ROWS, TILE), BF16),
            pltpu.VMEM((2, PB, TILE), BF16),
            pltpu.VMEM((CODES, ROWS), F32),
            pltpu.VMEM((4, PB, TILE), BF16),
            pltpu.VMEM((4, CODES, TILE), BF16),
            pltpu.VMEM((4, CODES, TILE), BF16),
            pltpu.VMEM((8, 64, CODES), BF16),
            pltpu.VMEM((GROUPS, SUB, ROWS), F32),
            pltpu.VMEM((GROUPS, 1, ROWS), F32),
            pltpu.VMEM((GROUPS, CODES, ROWS), BF16),
            pltpu.VMEM((GROUPS, CODES, ROWS), BF16),
            pltpu.VMEM((4, ROWS, 256), F32),
            pltpu.VMEM((4, ROWS, 256), F32),
            pltpu.VMEM((4, ROWS, 256), F32),
            pltpu.VMEM((4, 1, 256), F32),
            pltpu.VMEM((16, 128), F32),
            pltpu.VMEM((PLANE, 8, 128), F32),
            pltpu.VMEM((2, PLANE, 8, 128), F32),
            pltpu.VMEM((3, ROWS, TILE), F32),
            pltpu.VMEM((3, ROWS, TILE), F32),
            pltpu.VMEM((3, ROWS, TILE), F32),
            pltpu.VMEM((2, 128, TILE), F32),
            pltpu.VMEM((2, ROWS, TILE), F32),
            pltpu.VMEM((2, 128, TILE), F32),
            pltpu.VMEM((GROUPS, 16, ROWS), BF16),
            pltpu.VMEM((2, CODES, ROWS), BF16),
            pltpu.VMEM((GROUPS, 16, ROWS), BF16),
            pltpu.VMEM((4, ROWS, TILE), BF16),
            pltpu.VMEM((PLANE, SUB, CODES), F32),
            pltpu.VMEM((4, PLANE, SUB, CODES), F32),
            pltpu.VMEM((2, 8, 128), F32),
            pltpu.SemaphoreType.DMA((N_SEM,)),
            pltpu.SemaphoreType.DMA((240,)),
        ],
        compiler_params=pltpu.CompilerParams(
            collective_id=0, has_side_effects=True, vmem_limit_bytes=60 * 1024 * 1024
        ),
    )(passages, queries, codebook.reshape(D, CODES))
    return divergence.reshape(2048), grad.reshape(96, SUB, CODES)


def solution(mesh):
    placed = (P("corpus", None), P(("query", "corpus"), None), P())
    return jax.shard_map(
        local, mesh=mesh, in_specs=placed, out_specs=(P("query"), P()), check_vma=False
    )
```

```python
import functools

import jax
import jax.numpy as jnp
from jax import lax
from jax.experimental import pallas as pl
from jax.experimental.pallas import tpu as pltpu
from jax.sharding import PartitionSpec as P

MESH = pl.DeviceIdType.MESH
F32 = jnp.float32
BF16 = jnp.bfloat16
NT = (((1,), (1,)), ((), ()))
NN = (((1,), (0,)), ((), ()))

D = 768
SUB = 8
CODES = 256
QB = 64
PB = 128
PLANE = 16
TILE = 128
GROUPS = 16
ROWS = 256
QN = 1024
UNROLL = 1
N_SEM = 224
LOG2E = 1.4426950408889634
FAR_FIRST = [(2, 2), (2, 1), (2, 3), (1, 2), (3, 2), (1, 1), (1, 3), (3, 1), (3, 3), (2, 0), (0, 2), (1, 0), (3, 0), (0, 1), (0, 3)]


def rem(a, b):
    return a % b if isinstance(a, int) else lax.rem(a, b)


def quo(a, b):
    return a // b if isinstance(a, int) else lax.div(a, b)


def split3(value):
    high = value.astype(BF16)
    rest = value - high.astype(F32)
    mid = rest.astype(BF16)
    low = (rest - mid.astype(F32)).astype(BF16)
    return high, mid, low


def split2(value):
    high = value.astype(BF16)
    low = (value - high.astype(F32)).astype(BF16)
    return high, low


def dot(a, b, dims):
    return lax.dot_general(a, b, dims, preferred_element_type=F32)


def kernel(
    p_ref, q_ref, cb_hbm,
    out_ref, div_ref,
    cb_ref, cb_sem,
    qbuf, pbuf, rbuf,
    xtb, raw, xpack, lhs_f, lhs_b, cp3, rt, inv, a1b, a2b,
    tbuf, ebt, ebs, sumt, mloc, stat_t, stat,
    gown, gsib, gsrc, rs1, rs2, rs2s,
    gl, dbuf, xlt, gpack, dcs, dcr, divb,
    send_sem, recv_sem,
):
    qi = lax.axis_index("query")
    ci = lax.axis_index("corpus")
    xh, core = quo(qi, 2), rem(qi, 2)
    y, xl, z = quo(ci, 8), rem(quo(ci, 4), 2), rem(ci, 4)
    x = xh * 2 + xl
    u = rem(x + 4 - 2 * core, 4)

    def dev(x_, y_, z_, core_):
        return (quo(x_, 2) * 2 + core_, y_ * 8 + rem(x_, 2) * 4 + z_)

    def dev_x(step, core_=None):
        return dev(rem(x + step, 4), y, z, core if core_ is None else core_)

    def dev_yz(dy, dz):
        return dev(x, rem(y + dy, 4), rem(z + dz, 4), core)

    sibling = dev(x, y, z, 1 - core)
    left, right = dev_x(3), dev_x(1)

    sends = []
    count = [0]

    def guarded(cond, action):
        if cond is None:
            action()
        else:
            pl.when(cond)(action)

    def push(src, dst, index, device, cond=None):
        copy = pltpu.make_async_remote_copy(
            src_ref=src, dst_ref=dst, send_sem=send_sem.at[len(sends)],
            recv_sem=recv_sem.at[index], device_id=device, device_id_type=MESH,
        )
        guarded(cond, copy.start)
        sends.append((copy, cond))

    def arrive(dst, index, cond=None):
        guarded(cond, pltpu.make_async_remote_copy(
            src_ref=dst, dst_ref=dst, send_sem=send_sem.at[0],
            recv_sem=recv_sem.at[index], device_id=sibling, device_id_type=MESH,
        ).wait_recv)

    def block(n):
        first = count[0]
        count[0] += n
        return first

    def tile_col(u_):
        return pl.multiple_of((3 * core + jnp.minimum(u_, 2)) * TILE, TILE)

    col = tile_col(u)
    me = y * 4 + z
    fetch = pltpu.make_async_copy(cb_hbm.at[pl.ds(col, TILE), :], cb_ref, cb_sem.at[0])
    fetch_x = pltpu.make_async_copy(p_ref.at[:, pl.ds(col, TILE)], xtb.at[xl], cb_sem.at[1])
    fetch_p = pltpu.make_async_copy(p_ref, pbuf.at[xl], cb_sem.at[2])
    fetch_q = pltpu.make_async_copy(q_ref, qbuf.at[me], cb_sem.at[3])
    for copy in (fetch, fetch_x, fetch_p, fetch_q):
        copy.start()

    barrier = pltpu.get_barrier_semaphore()
    peers = [left, right, sibling]
    peers += [dev_yz(a, b) for a, b in ((0, 1), (0, 3), (0, 2), (1, 0), (3, 0), (2, 0))]
    for peer in peers:
        pl.semaphore_signal(barrier, inc=1, device_id=peer, device_id_type=MESH)


    pl.semaphore_wait(barrier, len(peers))

    def gather_plane(own, piece_of, base):
        def rel(h, a, b):
            return (a, b) if h == 0 else (b, a)

        def slot(dy, dz):
            return (rem(y + dy, 4)) * 4 + rem(z + dz, 4)

        def sem(dy, dz, h, part):
            return base + (((dy % 4) * 4 + dz % 4) * 2 + h) * 2 + (part or 0)

        def send(h, a, b, part, first_axis, step):
            dy, dz = rel(h, a, b)
            sy, sz = rel(h, step, 0) if first_axis else rel(h, 0, step)
            dst = piece_of(slot(dy, dz), h, part)
            src = own(h) if (a, b) == (0, 0) else dst
            push(src, dst, sem(dy - sy, dz - sz, h, part), dev_yz(sy % 4, sz % 4))

        def wait(h, a, b, part):
            dy, dz = rel(h, a, b)
            arrive(piece_of(slot(dy, dz), h, part), sem(dy, dz, h, part))

        def wave0():
            for h in range(2):
                for step in (2, 1, 3):
                    send(h, 0, 0, None, True, step)
            for h in range(2):
                for step in (2, 1, 3):
                    send(h, 0, 0, None, False, step)

        def onward(h, a):
            wait(h, a, 0, None)
            for step in (2, 1, 3):
                send(h, a, 0, None, False, step)

        def wave1():
            for h in range(2):
                onward(h, 1)
                onward(h, 3)

        def wave2():
            for h in range(2):
                onward(h, 2)

        def wave3():
            for h in range(2):
                for b in (1, 3, 2):
                    for a in (0, 1, 3, 2):
                        wait(h, a, b, None)

        return wave0, wave1, wave2, wave3

    def q_piece(s, h, part):
        if part is None:
            return qbuf.at[s, pl.ds(32 * h, 32), :]
        return qbuf.at[s, pl.ds(32 * h + 16 * part, 16), :]

    qw = gather_plane(lambda h: q_ref.at[pl.ds(32 * h, 32), :], q_piece, block(64))
    s_p = block(2)
    x_to = rem(x + 3 + 2 * core, 4)
    p_to = dev(x_to, y, z, core)
    col_to = tile_col(rem(x_to + 4 - 2 * core, 4))
    push(p_ref.at[:, pl.ds(col_to, TILE)], xtb.at[xl], s_p, p_to)
    qw[0]()
    push(p_ref, pbuf.at[xl], s_p + 1, p_to)

    fetch.wait()
    cb = cb_ref[...]
    grouped = cb.reshape(GROUPS, SUB, CODES)
    bias = -0.5 * jnp.sum(grouped * grouped, axis=1, keepdims=True)
    b_parts = [jnp.broadcast_to(b.astype(F32), grouped.shape) for b in split3(bias)]
    row = lax.broadcasted_iota(jnp.int32, grouped.shape, 1)
    extra = jnp.where(row == 3, 1.0, 0.0)
    for k in range(3):
        extra = jnp.where(row == k, b_parts[k], extra)
    c_parts = [c.astype(F32).reshape(GROUPS, SUB, CODES) for c in split3(cb)]
    packed = jnp.concatenate(c_parts + [extra], axis=1)
    cp3[...] = packed.reshape(8, 64, CODES).astype(BF16)
    for g in range(4):
        lhs_f[g] = packed[4 * g:4 * g + 4].reshape(TILE, CODES).T.astype(BF16)

    lane = lax.broadcasted_iota(jnp.int32, (TILE, 4 * TILE), 1)
    source = lax.broadcasted_iota(jnp.int32, (TILE, 4 * TILE), 0)
    inner_lane = lane % 32
    select = jnp.where(
        (source == (lane // 32) * SUB + lane % SUB) & (inner_lane < 24), 1.0, 0.0
    ).astype(BF16)
    tail_ones = jnp.where(
        (inner_lane[0:1] >= 24) & (inner_lane[0:1] < 27), 1.0, 0.0
    )
    pack_lane = lax.broadcasted_iota(jnp.int32, (1, TILE), 1) // 32

    def pack_mask(j):
        return jnp.where(pack_lane == j, 1.0, 0.0).astype(BF16)

    def pack_rows(h):
        packs = (dot(xtb[h], select, NN) + tail_ones).astype(BF16)
        for g in range(4):
            xpack[g] = packs[:, TILE * g:TILE * g + TILE]

    def half_lanes(h):
        return pl.ds(pl.multiple_of(h * 128, 128), 128)

    def logits_of(v):
        g, j = quo(v, 2), 2 * rem(v, 2)
        xp = xpack[g]
        rhs = jnp.concatenate([xp * pack_mask(j), xp * pack_mask(j + 1)], axis=0)
        raw[...] = dot(lhs_f[g], rhs, NT)

    def weigh(h, v):
        lanes = half_lanes(h)
        logits = raw[...]
        e1, e2 = split2(jnp.exp(logits - jnp.max(logits, axis=0, keepdims=True)))
        for k in range(2):
            a1b[2 * v + k, :, lanes] = e1[:, 128 * k:128 * k + 128]
            a2b[2 * v + k, :, lanes] = e2[:, 128 * k:128 * k + 128]

    def rebuild(h, v):
        lanes = half_lanes(h)
        got = sum(
            dot(cp3[v], jnp.concatenate([b[2 * v, :, lanes], b[2 * v + 1, :, lanes]], axis=1), NN)
            for b in (a1b, a2b)
        )
        for k in range(2):
            part = got[32 * k:32 * k + 32, 128 * k:128 * k + 128]
            scale_i = 1.0 / part[27:28]
            inv[2 * v + k, :, lanes] = scale_i
            rt[2 * v + k, :, lanes] = (part[0:8] + part[8:16] + part[16:24]) * scale_i

    def assign_steps(h, first, last):
        def step(v, carry):
            rebuild(h, v)
            weigh(h, v + 1)
            logits_of(v + 2)
            return carry

        lax.fori_loop(first, last, step, 0, unroll=UNROLL)

    fetch_x.wait()
    pack_rows(xl)
    def assign_open(h):
        logits_of(0)
        weigh(h, 0)
        logits_of(1)

    def assign_close(h):
        rebuild(h, 6)
        weigh(h, 7)
        rebuild(h, 7)

    assign_open(xl)
    assign_steps(xl, 0, 6)
    assign_close(xl)
    arrive(xtb.at[1 - xl], s_p)
    pack_rows(1 - xl)
    assign_open(1 - xl)
    qw[1]()
    assign_steps(1 - xl, 0, 3)
    qw[2]()
    assign_steps(1 - xl, 3, 6)
    assign_close(1 - xl)

    mine = core * 4 + u
    rbuf[mine] = rt[...].reshape(TILE, ROWS).T.astype(BF16)

    def r_slot(step):
        return core * 4 + rem(u + step, 4)

    def r_sib(step):
        return (1 - core) * 4 + rem(u + 2 + step, 4)

    s_r = block(4)
    s_rs = block(4)
    owner = u != 3
    for step in (2, 1, 3):
        push(rbuf.at[mine], rbuf.at[mine], s_r + 4 - step, dev_x(step), owner)
    push(rbuf.at[mine], rbuf.at[mine], s_rs, sibling, owner)

    xt = xtb[...].reshape(ROWS, TILE)
    xlt[...] = jnp.concatenate(
        [xt.astype(F32).T.reshape(GROUPS, SUB, ROWS), jnp.full((GROUPS, SUB, ROWS), 1.0, F32)], axis=1
    ).astype(BF16)
    code1, code2 = (c.astype(F32).reshape(GROUPS, SUB, CODES) for c in split2(cb_ref[...]))
    ones3 = jnp.where(lax.broadcasted_iota(jnp.int32, code1.shape, 1) < 3, 1.0, 0.0)
    packed_b = jnp.concatenate([code1, code2, code1, ones3], axis=1)
    for g in range(4):
        lhs_b[g] = packed_b[4 * g:4 * g + 4].reshape(TILE, CODES).T.astype(BF16)

    for step in (1, 3, 2):
        s = r_slot(step)
        real = rem(u + step, 4) != 3
        arrive(rbuf.at[s], s_r + step, real)
        push(rbuf.at[s], rbuf.at[s], s_rs + step, sibling, real)
    arrive(pbuf.at[1 - xl], s_p + 1)
    fetch_p.wait()
    fetch_q.wait()

    qw[3]()

    p_all = pbuf[...].reshape(ROWS, D)
    scale = float(D) ** (-0.5)
    scale2 = scale * LOG2E
    for n in range(4):
        qc = qbuf[4 * n:4 * n + 4].reshape(256, D)
        t = dot(p_all, qc, NT)
        m_t = jnp.max(t, axis=0, keepdims=True)
        tbuf[n] = t
        e_t = jnp.exp2((t - m_t) * scale2)
        ebt[n] = e_t
        s_t = jnp.sum(e_t, axis=0, keepdims=True)
        m_t = m_t * scale
        lt = m_t + jnp.log(s_t)
        sumt[n] = s_t
        for k in range(2):
            mloc[2 * n + k:2 * n + k + 1, :] = m_t[:, 128 * k:128 * k + 128]
            stat_t[me, 2 * n + k:2 * n + k + 1, :] = lt[:, 128 * k:128 * k + 128]

    def plane_send(buf, base):
        for a, b in FAR_FIRST:
            push(buf.at[me], buf.at[me], base + (rem(4 - a, 4)) * 4 + rem(4 - b, 4), dev_yz(a, b))

    def plane_wait(buf, base):
        for a, b in FAR_FIRST:
            arrive(buf.at[(rem(y + a, 4)) * 4 + rem(z + b, 4)], base + a * 4 + b)

    s_ta = block(16)
    plane_send(stat_t, s_ta)
    for step in (0, 1, 3, 2):
        arrive(rbuf.at[r_sib(step)], s_rs + step, rem(u + 2 + step, 4) != 3)

    s_st = block(32)
    r_all = jnp.concatenate([rbuf[k] for k in (0, 1, 2, 4, 5, 6)], axis=1)
    for n in range(4):
        qc = qbuf[4 * n:4 * n + 4].reshape(256, D)
        s = dot(r_all, qc, NT)
        m_s = jnp.max(s, axis=0, keepdims=True)
        e_s = jnp.exp2((s - m_s) * scale2)
        ebs[n] = e_s
        m_s = m_s * scale
        ls = m_s + jnp.log(jnp.sum(e_s, axis=0, keepdims=True))
        cross = jnp.sum(ebt[n] * (tbuf[n] - s), axis=0, keepdims=True) * scale / sumt[n]
        for k in range(2):
            r = 2 * n + k
            mloc[8 + r:9 + r, :] = m_s[:, 128 * k:128 * k + 128]
            q = 2 * (n % 2) + k
            stat[n // 2, me, q:q + 1, :] = ls[:, 128 * k:128 * k + 128]
            stat[n // 2, me, 4 + q:5 + q, :] = cross[:, 128 * k:128 * k + 128]
        if n % 2:
            plane_send(stat.at[n // 2], s_st + 16 * (n // 2))

    plane_wait(stat_t, s_ta)
    lt = stat_t[...]
    plane_wait(stat.at[0], s_st)
    plane_wait(stat.at[1], s_st + 16)
    ls = jnp.concatenate([stat[0, :, 0:4], stat[1, :, 0:4]], axis=1)
    cx = jnp.concatenate([stat[0, :, 4:8], stat[1, :, 4:8]], axis=1)
    top_t = jnp.max(lt, axis=0)
    top_s = jnp.max(ls, axis=0)
    big_t = top_t + jnp.log(jnp.sum(jnp.exp(lt - top_t[None]), axis=0))
    big_s = top_s + jnp.log(jnp.sum(jnp.exp(ls - top_s[None]), axis=0))
    cross = jnp.sum(jnp.exp(lt - big_t[None]) * cx, axis=0)
    divb[xl] = cross - big_t + big_s
    s_d = block(1)
    push(divb.at[xl], divb.at[xl], s_d, dev(x + 1 - 2 * xl, y, z, core))
    weight = (PB * 32 / 64.0) * scale
    f_t = jnp.exp(mloc[0:8, :] - big_t) * weight
    f_s = jnp.exp(mloc[8:16, :] - big_s) * weight

    grads = []
    for n in range(4):
        for k in range(2):
            r = 2 * n + k
            cols = slice(128 * k, 128 * k + 128)
            diff = ebs[n, :, cols] * f_s[r:r + 1] - ebt[n, :, cols] * f_t[r:r + 1]
            grads.append(diff.astype(BF16))
    grad_scores = jnp.concatenate(grads, axis=1)

    def partial(group, first, tiles):
        at = pl.multiple_of(group * 384 + first * TILE, TILE)
        return dot(grad_scores, qbuf[:, :, pl.ds(at, TILE * tiles)].reshape(QN, TILE * tiles), NN)

    s_g = block(3)
    for group, dest in ((1 - core, gsrc), (core, gown)):
        three = partial(group, 0, 3)
        for k in range(3):
            dest[k] = three[:, TILE * k:TILE * k + TILE]
            if dest is gsrc:
                push(gsrc.at[k], gsib.at[k], s_g + k, sibling)

    s_1 = block(2)
    s_2 = block(4)

    def half(n):
        return pl.ds(128 * n, 128)

    def near(step):
        return jnp.minimum(rem(u + step, 4), 2)

    for k in range(3):
        arrive(gsib.at[k], s_g + k)
        gown[k] = gown[k] + gsib[k]
    for part, to in ((0, right), (1, left)):
        push(gown.at[near(2), half(part), :], rs1.at[part], s_1 + part, to, rem(u + 2, 4) != 3)
    for part, to, step in ((0, right, 1), (1, left, 3)):
        push(
            gown.at[near(step), half(1 - part), :], rs2.at[part, half(1 - part), :],
            s_2 + 2 * part, to, rem(u + step, 4) != 3,
        )
    for part, to, step in ((0, right, 1), (1, left, 3)):
        ok = rem(u + step, 4) != 3
        arrive(rs1.at[part], s_1 + part, ok)
        rs2s[part] = gown[near(step), half(part), :] + rs1[part]
        push(rs2s.at[part], rs2.at[part, half(part), :], s_2 + 2 * part + 1, to, ok)
    for part in range(2):
        arrive(rs2.at[part, half(1 - part), :], s_2 + 2 * part, owner)
        arrive(rs2.at[part, half(part), :], s_2 + 2 * part + 1, owner)
    s_c = block(64)
    s_o = block(1)
    first_c = len(sends)
    sends.extend([None] * 64)

    def plane_order(n):
        y_n = rem(y + rem(n, 4), 4)
        return y_n * 4 + rem(y_n + quo(n, 4), 4)

    def piece_copy(n, step):
        other = plane_order(n)
        who, slot, sem = core, u, s_c + 16 * u + me
        if step == 0:
            own = 1 - jnp.minimum(jnp.abs(other - me), 1)
            who = core + own * (1 - 2 * core)
            slot = u + own * (3 - u)
            sem = sem + own * (s_o - sem)
        return pltpu.make_async_remote_copy(
            src_ref=dcs.at[other], dst_ref=dcr.at[slot, me],
            send_sem=send_sem.at[first_c + 4 * n + step], recv_sem=recv_sem.at[sem],
            device_id=dev(rem(x + step, 4), quo(other, 4), rem(other, 4), who), device_id_type=MESH,
        )

    def piece_send(n):
        for step in (2, 1, 3, 0):
            piece_copy(n, step).start()

    def piece_sent(n, carry):
        for step in (2, 1, 3, 0):
            piece_copy(n, step).wait_send()
        return carry

    def diff_of(n):
        i = plane_order(n)
        p, j = quo(i, 4), rem(i, 4)
        return dot(lhs_b[p], gpack[p] * pack_mask(j), NT)

    def differ(n, diff):
        i = plane_order(n)
        d1, d2 = split2((a1b[i].astype(F32) + a2b[i].astype(F32)) * diff)
        dbuf[0] = d1
        dbuf[1] = d2

    def contract(n):
        i = plane_order(n)
        ow = dot(gl[i], a1b[i], NT) + dot(gl[i], a2b[i], NT)
        od = dot(xlt[i], dbuf[0], NT) + dot(xlt[i], dbuf[1], NT)
        code = cb_ref[pl.ds(pl.multiple_of(SUB * i, SUB), SUB), :]
        dcs[i] = ow[0:8] + ow[8:16] + od[0:8] - code * od[8:16]

    def next_step(n, carry):
        diff = diff_of(n + 1)
        contract(n)
        differ(n + 1, diff)
        piece_send(n - 1)
        return carry

    @pl.when(owner)
    def _():
        g = gown[near(0)] + rs2[0] + rs2[1]
        gt = (g.T).reshape(GROUPS, SUB, ROWS) * inv[...]
        g1t, g2t = split2(gt)
        gl[...] = jnp.concatenate([g1t.astype(F32), g2t.astype(F32)], axis=1).astype(BF16)
        inner = -jnp.sum(gt * rt[...], axis=1, keepdims=True)
        t_parts = [jnp.broadcast_to(t.astype(F32), gt.shape) for t in split3(inner)]
        at_row = lax.broadcasted_iota(jnp.int32, gt.shape, 1)
        last = jnp.zeros_like(gt)
        for k in range(3):
            last = jnp.where(at_row == k, t_parts[k], last)
        g1f = g1t.astype(F32)
        stacked = jnp.concatenate([g1f, g1f, g2t.astype(F32), last], axis=1)
        for k in range(4):
            gpack[k] = stacked[4 * k:4 * k + 4].reshape(TILE, ROWS).T.astype(BF16)

        differ(0, diff_of(0))
        contract(0)
        differ(1, diff_of(1))
        lax.fori_loop(1, 15, next_step, 0)
        piece_send(14)
        contract(15)
        piece_send(15)
        dcr[u, me] = dcs[me]

    for entry in sends[:first_c]:
        guarded(entry[1], entry[0].wait_send)
    arrive(divb.at[1 - xl], s_d)
    for k in range(4):
        for h in range(2):
            div_ref[4 * k + 2 * h:4 * k + 2 * h + 2, :] = divb[h, 2 * k:2 * k + 2, :]

    for k in range(3):
        arrive(dcr.at[k, me], s_c + 16 * k + me, u != k)

    def piece_wait(n, carry):
        other = rem(me + n, 16)
        for k in range(3):
            arrive(dcr.at[k, other], s_c + 16 * k + other)
        return carry

    lax.fori_loop(1, 16, piece_wait, 0)
    arrive(dcr.at[3, me], s_o, rem(u + 2, 4) != 3)

    for k in range(3):
        out_ref[3 * core + k, me] = jnp.sum(dcr[k], axis=0)

    def trio(s, c):
        return out_ref.at[pl.ds(3 * c, 3), s]

    s_f = block(16)
    s_fs = block(16)
    for a, b in FAR_FIRST:
        push(trio(me, core), trio(me, core), s_f + me, dev_yz(a, b))
    push(trio(me, core), trio(me, core), s_fs + me, sibling)
    first_r = len(sends)
    sends.extend([None] * 16)

    def relay(n, carry):
        other = plane_order(n)

        @pl.when(other != me)
        def _():
            arrive(trio(other, core), s_f + other)
            pltpu.make_async_remote_copy(
                src_ref=trio(other, core), dst_ref=trio(other, core),
                send_sem=send_sem.at[first_r + n], recv_sem=recv_sem.at[s_fs + other],
                device_id=sibling, device_id_type=MESH,
            ).start()

        return carry

    def relay_wait(n, carry):
        other = plane_order(n)
        arrive(trio(other, 1 - core), s_fs + other)

        @pl.when(other != me)
        def _():
            pltpu.make_async_remote_copy(
                src_ref=trio(other, core), dst_ref=trio(other, core),
                send_sem=send_sem.at[first_r + n], recv_sem=recv_sem.at[s_fs + other],
                device_id=sibling, device_id_type=MESH,
            ).wait_send()

        return carry

    @pl.when(owner)
    def _():
        lax.fori_loop(0, 16, piece_sent, 0)

    lax.fori_loop(0, 16, relay, 0)
    lax.fori_loop(0, 16, relay_wait, 0)

    for entry in sends[first_c:]:
        if entry is not None:
            guarded(entry[1], entry[0].wait_send)


def local(passages, queries, codebook):
    vmem = pl.BlockSpec(memory_space=pltpu.VMEM)
    grad, divergence = pl.pallas_call(
        kernel,
        out_shape=(
            pltpu.VMEM((6, PLANE, SUB, CODES), F32),
            pltpu.VMEM((16, 128), F32),
        ),
        in_specs=[pl.BlockSpec(memory_space=pl.ANY)] * 3,
        out_specs=(vmem, vmem),
        scratch_shapes=[
            pltpu.VMEM((TILE, CODES), F32),
            pltpu.SemaphoreType.DMA((4,)),
            pltpu.VMEM((PLANE, QB, D), BF16),
            pltpu.VMEM((2, PB, D), BF16),
            pltpu.VMEM((8, ROWS, TILE), BF16),
            pltpu.VMEM((2, PB, TILE), BF16),
            pltpu.VMEM((CODES, ROWS), F32),
            pltpu.VMEM((4, PB, TILE), BF16),
            pltpu.VMEM((4, CODES, TILE), BF16),
            pltpu.VMEM((4, CODES, TILE), BF16),
            pltpu.VMEM((8, 64, CODES), BF16),
            pltpu.VMEM((GROUPS, SUB, ROWS), F32),
            pltpu.VMEM((GROUPS, 1, ROWS), F32),
            pltpu.VMEM((GROUPS, CODES, ROWS), BF16),
            pltpu.VMEM((GROUPS, CODES, ROWS), BF16),
            pltpu.VMEM((4, ROWS, 256), F32),
            pltpu.VMEM((4, ROWS, 256), F32),
            pltpu.VMEM((4, ROWS, 256), F32),
            pltpu.VMEM((4, 1, 256), F32),
            pltpu.VMEM((16, 128), F32),
            pltpu.VMEM((PLANE, 8, 128), F32),
            pltpu.VMEM((2, PLANE, 8, 128), F32),
            pltpu.VMEM((3, ROWS, TILE), F32),
            pltpu.VMEM((3, ROWS, TILE), F32),
            pltpu.VMEM((3, ROWS, TILE), F32),
            pltpu.VMEM((2, 128, TILE), F32),
            pltpu.VMEM((2, ROWS, TILE), F32),
            pltpu.VMEM((2, 128, TILE), F32),
            pltpu.VMEM((GROUPS, 16, ROWS), BF16),
            pltpu.VMEM((2, CODES, ROWS), BF16),
            pltpu.VMEM((GROUPS, 16, ROWS), BF16),
            pltpu.VMEM((4, ROWS, TILE), BF16),
            pltpu.VMEM((PLANE, SUB, CODES), F32),
            pltpu.VMEM((4, PLANE, SUB, CODES), F32),
            pltpu.VMEM((2, 8, 128), F32),
            pltpu.SemaphoreType.DMA((N_SEM,)),
            pltpu.SemaphoreType.DMA((240,)),
        ],
        compiler_params=pltpu.CompilerParams(
            collective_id=0, has_side_effects=True, vmem_limit_bytes=60 * 1024 * 1024
        ),
    )(passages, queries, codebook.reshape(D, CODES))
    return divergence.reshape(2048), grad.reshape(96, SUB, CODES)


def solution(mesh):
    placed = (P("corpus", None), P(("query", "corpus"), None), P())
    return jax.shard_map(
        local, mesh=mesh, in_specs=placed, out_specs=(P("query"), P()), check_vma=False
    )
```
